256 devices in a mesh: space: 32 (over z_hi, y, core), probe: 8 (over x, z_lo).
Axes of the slice: x: 4, y: 4, z: 8 (z_hi: 4, z_lo: 2; z = z_hi * 2 + z_lo), core: 2. Of those that a mesh axis runs over, the one named last changes fastest.
Arguments:
- positions: bfloat16 [256, 3, 32], P('space'), may hold values from -4.3125 to 4.3125
- probes: bfloat16 [256, 512, 128], P('space', 'probe'), may hold values from -4 to 4
- neighbours: int32 [256, 15], P('space'), may hold values from -1 to 255, as said below
Outputs:
- density: bfloat16 [128, 256, 15, 128], P('probe', 'space')
- forces: float32 [256, 3, 32], P('space')
The draws below stay inside these ranges and needn't reach their ends.
Inputs may be any that keep to these rules, and one draw needn't show every extreme that they name: `neighbours`: slot 0 of each cluster names the cluster itself. Clusters are held 8 to an index of space in order; every other entry is -1 or a cluster held by the same index of space or by the index one before or one after it, cyclically. The clusters named in one row are distinct.
All inputs are finite; a program needn't handle non-finite values.
Results may differ from the reference program's by a relative error of at most 0.0018.
The reference program's roundings to bfloat16 on the way (of `scaled`, `one_half` and `mixture`) count: a program that leaves them out, or rounds other values in their place, can miss the bound.
Values may be sent and summed in bfloat16 or wider, within the bound.
No kernel may reach another device: no remote copies, remote signals or barrier semaphores. Data moves between devices by JAX's collectives and lax.ppermute only.
A program may use at most 64 MiB of HBM per device.

```python
import jax
import jax.numpy as jnp
from jax import lax

ATOMS_C = 32
ORB = 128
NBLK = 15
PROBES = 512
CL_DEV = 8
CLUSTERS = 256
N_SPACE = 32


BOX_EDGE = 8.6


def draw_positions(key, part):
    coords = jax.random.uniform(key, (CLUSTERS, 3, ATOMS_C), jnp.float32, -0.5, 0.5) * BOX_EDGE
    return coords.astype(jnp.bfloat16)


def draw_neighbours(key, part):
    candidates = 3 * CL_DEV
    scores = jax.random.randint(key, (CLUSTERS, candidates), 0, 2 ** 20) * candidates
    scores = scores + jnp.arange(candidates, dtype=jnp.int32)[None, :]
    own_ids = jnp.arange(CLUSTERS, dtype=jnp.int32)
    device = own_ids // CL_DEV
    self_place = CL_DEV + own_ids % CL_DEV
    scores = jnp.where(jnp.arange(candidates, dtype=jnp.int32)[None, :] == self_place[:, None], 2 ** 30, scores)
    chosen = jnp.argsort(scores, axis=1)[:, :NBLK - 1].astype(jnp.int32)
    others = (device[:, None] + chosen // CL_DEV - 1) % N_SPACE * CL_DEV + chosen % CL_DEV
    surface = device[:, None] < max(1, N_SPACE // 4)
    coin = jax.random.randint(jax.random.fold_in(key, 7), (CLUSTERS, NBLK - 1), 0, 2)
    others = jnp.where(surface & (coin == 0), -1, others)
    return jnp.concatenate([own_ids[:, None], others], axis=1).astype(jnp.int32)


def shard_levels(key, extent, cuts, least, top_value):
    factor_of = 1.0
    for position, parts in cuts:
        steps = jax.random.uniform(jax.random.fold_in(jax.random.fold_in(key, 6), position), (parts,), jnp.float32, least / len(cuts), top_value / len(cuts))
        factor_of = factor_of * jnp.repeat(jnp.exp(steps), extent[position] // parts).reshape((-1,) + (1,) * (len(extent) - 1 - position))
    return factor_of


def gaussian(stream_key, extent, deviation, limit, split=(), held_as=jnp.bfloat16):
    factor_of = shard_levels(stream_key, extent, split, -0.22, 0.18) if split else 1.0
    values = jax.random.normal(stream_key, extent, jnp.float32) * deviation * factor_of
    return jnp.minimum(jnp.maximum(values, -limit), limit).astype(held_as)


def setup_inputs(seed: int = 0) -> dict:
    splits = jax.random.split(jax.random.key(seed), 4)
    positions = draw_positions(jax.random.fold_in(splits[3], 71), 0)
    probes = gaussian(splits[1], (CLUSTERS, PROBES, ORB), 1.0, 4.0, ((0, 32), (1, 8)))
    neighbours = draw_neighbours(jax.random.fold_in(splits[3], 71), 0)
    return {"positions": positions, "probes": probes, "neighbours": neighbours}


SS_SIGMA = -1.938
SP_SIGMA = 1.745
PP_SIGMA = 3.05
PP_PI = -1.075
BOND_LENGTH = 2.35
SOFT_SQUARE = 0.25
CELL_EDGE = 10.86
COEFF_ZERO = 0.6
COEFF_ONE = -0.7
COEFF_TWO = 0.45

def offsets():
    half = CELL_EDGE / 2.0
    table = [[0.0, 0.0, 0.0]]
    for sign_x in (-1.0, 1.0):
        for sign_y in (-1.0, 1.0):
            for sign_z in (-1.0, 1.0):
                table.append([sign_x * half, sign_y * half, sign_z * half])
    for axis_pick in range(3):
        for sign_a in (1.0, -1.0):
            entry = [0.0, 0.0, 0.0]
            entry[axis_pick] = sign_a * CELL_EDGE
            table.append(entry)
    return jnp.array(table, dtype=jnp.float32)

def build_rows(own_pos, col_pos, start_row, row_count):
    atom_count = own_pos.shape[-1]
    row_index = start_row + jnp.arange(row_count, dtype=jnp.int32)
    orbital = row_index // atom_count
    atom_index = row_index % atom_count
    atom_pick = (jnp.arange(atom_count, dtype=jnp.int32)[:, None] == atom_index[None, :]).astype(jnp.float32)
    weights = (jnp.arange(4, dtype=jnp.int32)[:, None] == orbital[None, :]).astype(jnp.float32)
    row_pos = jnp.dot(own_pos, atom_pick, precision=lax.Precision.HIGHEST)
    offset_vec = col_pos[:, None, :] - row_pos[:, :, None]
    dist_square = lax.optimization_barrier(jnp.sum(offset_vec * offset_vec, axis=0)) + SOFT_SQUARE
    cosine = offset_vec / jnp.sqrt(dist_square)
    radial = jnp.exp(1.0 - dist_square / (BOND_LENGTH * BOND_LENGTH))
    projected = lax.optimization_barrier(jnp.sum(weights[1:, :, None] * cosine, axis=0))
    s_orbital = weights[0][:, None]
    columns = [(s_orbital * SS_SIGMA - projected * SP_SIGMA) * radial]
    for direction in range(3):
        columns.append((s_orbital * cosine[direction] * SP_SIGMA + projected * cosine[direction] * (PP_SIGMA - PP_PI) + weights[1 + direction][:, None] * PP_PI) * radial)
    return jnp.stack(columns, axis=1).reshape(row_count, 4 * atom_count)

def cluster_blocks(own_pos, near_pos, present, start_row, row_count):
    made = jax.vmap(build_rows, in_axes=(None, 0, None, None))(own_pos, near_pos, start_row, row_count)
    return made * present.astype(jnp.float32)[:, None, None]

def reference(positions, probes, neighbours):
    coords = positions.astype(jnp.float32)
    cluster_count = coords.shape[0]
    orbitals = 4 * coords.shape[2]
    total_probes = probes.shape[1]
    slot_count = neighbours.shape[1]
    present = neighbours >= 0
    target = jnp.where(present, neighbours, 0).astype(jnp.int32)
    shifts = offsets()
    cluster_ids = jnp.arange(cluster_count, dtype=jnp.int32)

    def blocks_of(cluster):
        beside_all = coords[target[cluster]] + shifts[:, :, None]
        return cluster_blocks(coords[cluster], beside_all, present[cluster], 0, orbitals)
    row_peaks = lax.map(lambda cluster: jnp.max(lax.optimization_barrier(jnp.sum(jnp.abs(blocks_of(cluster)), axis=(0, 2)))), cluster_ids)
    spectral = jnp.max(row_peaks)

    def apply_all(vectors):

        def one_cluster(cluster):
            rounded = lax.optimization_barrier((blocks_of(cluster) / spectral).astype(jnp.bfloat16))
            scaled = rounded.astype(jnp.float32)
            nearby = vectors[target[cluster]].astype(jnp.float32)
            return jnp.einsum('kpj,kij->pi', nearby, scaled)
        return lax.map(one_cluster, cluster_ids)
    probe_wide = probes.astype(jnp.float32)
    term_one = apply_all(probes)
    one_half = term_one.astype(jnp.bfloat16)
    term_two = 2.0 * apply_all(one_half) - probe_wide
    mixture = (COEFF_ZERO * probe_wide + COEFF_ONE * term_one + COEFF_TWO * term_two).astype(jnp.bfloat16)

    def sample_of(cluster):
        nearby = probes[target[cluster]].astype(jnp.float32)
        alive = present[cluster].astype(jnp.float32)
        sample = jnp.einsum('pi,kpj->kij', mixture[cluster].astype(jnp.float32), nearby) * alive[:, None, None]

        def energy(own_pos, near_pos):
            made = cluster_blocks(own_pos, near_pos + shifts[:, :, None], present[cluster], 0, orbitals)
            return jnp.sum(made * sample) / total_probes
        own_grad, near_grad = jax.grad(energy, argnums=(0, 1))(coords[cluster], coords[target[cluster]])
        scaled_out = (sample / jnp.sqrt(jnp.float32(total_probes))).astype(jnp.bfloat16)
        return (scaled_out, own_grad, near_grad)
    density, own_grad, near_grad = lax.map(sample_of, cluster_ids)
    spread = jax.ops.segment_sum(near_grad.reshape(cluster_count * slot_count, 3, coords.shape[2]), target.reshape(-1), num_segments=cluster_count)
    forces = -(own_grad + spread)
    return (jnp.transpose(density, (2, 0, 1, 3)), forces)
```

```python
import functools
import math

import jax
import jax.numpy as jnp
import numpy as np
from jax import lax
from jax.experimental import pallas as pl
from jax.experimental.pallas import tpu as pltpu
from jax.sharding import PartitionSpec as P

SS_SIGMA = -1.938
SP_SIGMA = 1.745
PP_SIGMA = 3.05
PP_PI = -1.075
BOND_LENGTH = 2.35
SOFT_SQUARE = 0.25
CELL_EDGE = 10.86
COEFF_ZERO = 0.6
COEFF_ONE = -0.7
COEFF_TWO = 0.45

PP_SUM = PP_SIGMA - PP_PI
BOND_SQUARE = BOND_LENGTH * BOND_LENGTH
NEAR = 24
DEAD = 24
FAR = 1000.0
SLOTS = 16
F32 = jnp.float32
BF16 = jnp.bfloat16
VMEM = pl.BlockSpec(memory_space=pltpu.VMEM)
SMEM = pl.BlockSpec(memory_space=pltpu.SMEM)
PARAMS = pltpu.CompilerParams(vmem_limit_bytes=48 * 1024 * 1024)


def slot_offsets():
    half = CELL_EDGE / 2.0
    table = [[0.0, 0.0, 0.0]]
    for sign_x in (-1.0, 1.0):
        for sign_y in (-1.0, 1.0):
            for sign_z in (-1.0, 1.0):
                table.append([sign_x * half, sign_y * half, sign_z * half])
    for axis_pick in range(3):
        for sign_a in (1.0, -1.0):
            entry = [0.0, 0.0, 0.0]
            entry[axis_pick] = sign_a * CELL_EDGE
            table.append(entry)
    table.append([0.0, 0.0, 0.0])
    return np.array(table, dtype=np.float32)


def packed_shifts():
    table = slot_offsets().reshape(4, 4, 3).transpose(0, 2, 1)
    table = np.repeat(table, 32, axis=2)
    return np.pad(table, ((0, 0), (0, 5), (0, 0)))


def slot_shifts():
    table = np.broadcast_to(slot_offsets()[:, :, None], (SLOTS, 3, 128))
    return np.pad(table, ((0, 0), (0, 5), (0, 0)))


def lanes():
    return lax.broadcasted_iota(jnp.int32, (1, 128), 1)


def bond(columns, rows):
    d = [columns[x : x + 1, :] - rows[x] for x in range(3)]
    rho_square = d[0] * d[0] + d[1] * d[1] + d[2] * d[2] + SOFT_SQUARE
    inverse = lax.rsqrt(rho_square)
    radial = jnp.exp(1.0 - rho_square / BOND_SQUARE)
    return d, [v * inverse for v in d], radial, inverse


def four_slots(near_ref, slot_ref, shift_ref, c, g, lane):
    v = [near_ref[slot_ref[c, 4 * g + t]] for t in range(4)]
    joined = jnp.where(
        lane < 32, v[0], jnp.where(lane < 64, v[1], jnp.where(lane < 96, v[2], v[3]))
    )
    return joined + shift_ref[g]


def spectral_kernel(slot_ref, before_ref, own_ref, after_ref, shift_ref, row_ref, near_ref, peak_ref):
    near_ref[0:8] = before_ref[...]
    near_ref[8:16] = own_ref[...]
    near_ref[16:24] = after_ref[...]
    near_ref[DEAD] = jnp.full((8, 128), FAR, F32)
    lane = lanes()

    def one_cluster(c, peak):
        rows = [row_ref[c, x] for x in range(3)]
        sums = [jnp.zeros((32, 128), F32) for _ in range(4)]
        for g in range(4):
            columns = four_slots(near_ref, slot_ref, shift_ref, c, g, lane)
            _, cosine, radial, _ = bond(columns, rows)
            size = [jnp.abs(v) for v in cosine]
            sums[0] += (-SS_SIGMA + SP_SIGMA * (size[0] + size[1] + size[2])) * radial
            cross = {}
            for a in range(3):
                for b in range(a, 3):
                    product = cosine[a] * cosine[b] * PP_SUM
                    cross[a, b] = cross[b, a] = jnp.abs(product + PP_PI if a == b else product)
            for a in range(3):
                sums[1 + a] += (
                    SP_SIGMA * size[a] + cross[a, 0] + cross[a, 1] + cross[a, 2]
                ) * radial
        for v in sums:
            peak = jnp.maximum(peak, jnp.sum(v, axis=1, keepdims=True))
        return peak

    peak = lax.fori_loop(0, 8, one_cluster, jnp.zeros((32, 1), F32))
    peak_ref[...] = jnp.broadcast_to(jnp.max(peak), peak_ref.shape)


def build_kernel(
    slot_ref, near_ref, shift_ref, row_ref, before_ref, own_ref, after_ref,
    blocks_ref, operand_ref, turned_ref, probe_ref,
):
    lane = lanes()
    for part, ref in enumerate((before_ref, own_ref, after_ref)):
        for c in range(8):
            turned = ref[c].astype(F32).T
            if part == 1:
                turned_ref[c] = turned
            probe_ref[8 * part + c] = turned.astype(BF16)
    probe_ref[DEAD] = jnp.zeros((128, 64), BF16)

    def one_cluster(c, carry):
        rows = [row_ref[c, x] for x in range(3)]
        for g in range(4):
            columns = four_slots(near_ref, slot_ref, shift_ref, c, g, lane)
            _, cosine, radial, _ = bond(columns, rows)
            base = 512 * g
            blocks_ref[c, 0:32, base : base + 128] = SS_SIGMA * radial
            for a in range(3):
                wave = cosine[a] * SP_SIGMA * radial
                low, high = 32 * (a + 1), 128 * (a + 1)
                blocks_ref[c, 0:32, base + high : base + high + 128] = wave
                blocks_ref[c, low : low + 32, base : base + 128] = -wave
                for b in range(a, 3):
                    product = cosine[a] * cosine[b] * PP_SUM
                    value = (product + PP_PI if a == b else product) * radial
                    other = 128 * (b + 1)
                    blocks_ref[c, low : low + 32, base + other : base + other + 128] = value
                    if a != b:
                        blocks_ref[
                            c, 32 * (b + 1) : 32 * (b + 2), base + high : base + high + 128
                        ] = value
        gather_operand(slot_ref, probe_ref, operand_ref.at[c], c)
        return carry

    lax.fori_loop(0, 8, one_cluster, 0)


def gather_operand(slot_ref, source_ref, target_ref, c):
    for k in range(SLOTS):
        n = slot_ref[c, k]
        for b in range(4):
            low = 512 * (k // 4) + 128 * b + 32 * (k % 4)
            target_ref[low : low + 32, :] = source_ref[n, 32 * b : 32 * b + 32, :]


def first_kernel(peak_ref, blocks_ref, operand_ref, scaled_ref, one_ref, half_ref):
    inverse = 1.0 / jnp.max(peak_ref[...])

    def one_pair(pair, carry):
        for side in range(2):
            c = pair + 4 * side
            scaled = (blocks_ref[c] * inverse).astype(BF16)
            scaled_ref[c] = scaled
            one = jnp.dot(scaled, operand_ref[c], preferred_element_type=F32)
            one_ref[c] = one
            half_ref[pair, :, 64 * side : 64 * side + 64] = one.astype(BF16)
        return carry

    lax.fori_loop(0, 4, one_pair, 0)


def second_kernel(
    slot_ref, scaled_ref, before_ref, own_ref, after_ref, one_ref, turned_ref,
    mixture_ref, half_ref, operand_ref, joined_ref,
):
    for part, ref in enumerate((before_ref, own_ref, after_ref)):
        for pair in range(4):
            half_ref[8 * part + pair] = ref[pair, :, 0:64]
            half_ref[8 * part + pair + 4] = ref[pair, :, 64:128]
    half_ref[DEAD] = jnp.zeros((128, 64), BF16)

    def one_pair(pair, carry):
        for side in range(2):
            c = pair + 4 * side
            gather_operand(slot_ref, half_ref, operand_ref.at[side], c)
            two = jnp.dot(scaled_ref[c], operand_ref[side], preferred_element_type=F32)
            probe = turned_ref[c]
            term_two = 2.0 * two - probe
            mixture = COEFF_ZERO * probe + COEFF_ONE * one_ref[c] + COEFF_TWO * term_two
            joined_ref[:, 64 * side : 64 * side + 64] = mixture.astype(BF16)
        for q in range(8):
            mixture_ref[q, pl.ds(pl.multiple_of(16 * pair, 16), 16), :] = joined_ref[
                16 * q : 16 * q + 16, :
            ]
        return carry

    lax.fori_loop(0, 4, one_pair, 0)


def sample_kernel(
    slot_ref, rank_ref, mixture_ref, before_ref, own_ref, after_ref, near_ref, shift_ref, row_ref,
    density_ref, force_ref, left_ref, sample_ref, turn_ref, pull_ref,
):
    lane = lanes()
    rank = rank_ref[0]
    for q in range(8):
        block = mixture_ref[q]
        left_ref[0:64, 64 * q : 64 * q + 64] = block[:, 0:64]
        left_ref[64:128, 64 * q : 64 * q + 64] = block[:, 64:128]
    left = left_ref[...]
    for part, ref in enumerate((before_ref, own_ref, after_ref)):
        for pair in range(4):
            c = 2 * pair
            right = jnp.concatenate(
                [ref[:, c].reshape(512, 128), ref[:, c + 1].reshape(512, 128)], axis=1
            )
            product = jnp.dot(left, right, preferred_element_type=F32)
            sample_ref[8 * part + c] = product[:, 0:128]
            sample_ref[8 * part + c + 1] = product[:, 128:256]
    sample_ref[DEAD] = jnp.zeros((128, 128), F32)
    pull_ref[...] = jnp.zeros_like(pull_ref)

    orbital = rank // 2
    first_atom = 16 * (rank % 2)
    row_is = [(orbital == a).astype(F32) for a in range(4)]
    column_is = [(lane // 32 == b).astype(F32) for b in range(4)]
    constant = row_is[0] * SS_SIGMA * column_is[0] + PP_PI * (
        row_is[1] * column_is[1] + row_is[2] * column_is[2] + row_is[3] * column_is[3]
    )
    linear = [
        SP_SIGMA * (row_is[0] * column_is[1 + x] - column_is[0] * row_is[1 + x]) for x in range(3)
    ]
    row_sum = [PP_SUM * row_is[1 + x] for x in range(3)]
    column_sum = [PP_SUM * column_is[1 + x] for x in range(3)]
    row_lane = lax.broadcasted_iota(jnp.int32, (16, 128), 0) + first_atom
    on_row = lax.broadcasted_iota(jnp.int32, (16, 128), 1) == row_lane
    scale = 1.0 / math.sqrt(512.0)

    def one_cluster(c, carry):
        rows = [row_ref[c, x, pl.ds(pl.multiple_of(first_atom, 16), 16), :] for x in range(3)]
        own = [jnp.zeros((16, 128), F32) for _ in range(3)]
        for k in range(15):
            n = slot_ref[c, k]
            sample = sample_ref[n, pl.ds(pl.multiple_of(16 * c, 16), 16), :]
            turn_ref[pl.ds(k, 16, stride=SLOTS), :] = sample * scale
            columns = near_ref[n] + shift_ref[k]
            d, cosine, radial, inverse = bond(columns, rows)
            on_rows = row_is[1] * cosine[0] + row_is[2] * cosine[1] + row_is[3] * cosine[2]
            on_columns = (
                column_is[1] * cosine[0] + column_is[2] * cosine[1] + column_is[3] * cosine[2]
            )
            bent = PP_SUM * on_rows * on_columns
            slope = [
                linear[x] + row_sum[x] * on_columns + column_sum[x] * on_rows for x in range(3)
            ]
            straight = linear[0] * cosine[0] + linear[1] * cosine[1] + linear[2] * cosine[2]
            value = constant + straight + bent
            along = straight + 2.0 * bent
            weight = sample * radial
            across = weight * inverse
            inward = weight * (value * (-2.0 / BOND_SQUARE)) - across * (along * inverse)
            for x in range(3):
                pull = across * slope[x] + inward * d[x]
                own[x] = own[x] + pull
                pull_ref[n, x] = pull_ref[n, x] - (pull[0:8] + pull[8:16])
        for x in range(3):
            whole = jnp.broadcast_to(jnp.sum(own[x], axis=1, keepdims=True), (16, 128))
            placed = jnp.where(on_row, whole, 0.0)
            pull_ref[8 + c, x] = pull_ref[8 + c, x] + (placed[0:8] + placed[8:16])
        for r in range(16):
            density_ref[r, c] = turn_ref[SLOTS * r : SLOTS * r + 15, :].astype(BF16)
        return carry

    lax.fori_loop(0, 8, one_cluster, 0)

    total = jnp.sum(pull_ref[0:24], axis=2).reshape(72, 128)
    total = total + pltpu.roll(total, 64, 1)
    total = total + pltpu.roll(total, 32, 1)
    total = (total * (1.0 / 512.0)).reshape(24, 3, 128)
    joined = jnp.where(lane < 32, total[:, 0], jnp.where(lane < 64, total[:, 1], total[:, 2]))
    for q in range(8):
        force_ref[q] = joined


def around(block, size, distance):
    return lax.ppermute(block, "space", [((i - distance) % size, i) for i in range(size)])


def per_device(positions, probes, neighbours):
    space_count = lax.axis_size("space")
    space_rank = lax.axis_index("space")
    probe_rank = lax.axis_index("probe")
    both = lambda block: (around(block, space_count, 1), around(block, space_count, -1))

    coords = positions.astype(F32)
    packed = jnp.pad(jnp.tile(coords, (1, 1, 4)), ((0, 0), (0, 5), (0, 0)))
    pos_before, pos_after = both(packed)
    rows = jnp.broadcast_to(coords[..., None], (8, 3, 32, 128))
    present = neighbours >= 0
    slot = (neighbours // 8 - space_rank + 1) % space_count * 8 + neighbours % 8
    slot = jnp.pad(jnp.where(present, slot, DEAD), ((0, 0), (0, 1)), constant_values=DEAD)
    packed_shift = jnp.asarray(packed_shifts(), F32)
    slot_shift = jnp.asarray(slot_shifts(), F32)

    near, peak = pl.pallas_call(
        spectral_kernel,
        out_shape=(
            jax.ShapeDtypeStruct((NEAR + 1, 8, 128), F32),
            jax.ShapeDtypeStruct((space_count, 128), F32),
        ),
        in_specs=[SMEM] + [VMEM] * 5,
        out_specs=(VMEM, VMEM),
        compiler_params=PARAMS,
        name="spectral",
    )(slot, pos_before, packed, pos_after, packed_shift, rows)
    peaks = lax.all_to_all(peak, "space", 0, 0, tiled=True)

    probe_before, probe_after = both(probes)
    spread = jnp.broadcast_to(probes[None], (8,) + probes.shape)
    all_own = lax.all_to_all(spread, "probe", 0, 0, tiled=True).reshape(8, 8, 64, 128)
    all_before, all_after = both(all_own)

    blocks, operand, turned = pl.pallas_call(
        build_kernel,
        out_shape=(
            jax.ShapeDtypeStruct((8, 128, 2048), F32),
            jax.ShapeDtypeStruct((8, 2048, 64), BF16),
            jax.ShapeDtypeStruct((8, 128, 64), F32),
        ),
        in_specs=[SMEM] + [VMEM] * 6,
        out_specs=(VMEM, VMEM, VMEM),
        scratch_shapes=[pltpu.VMEM((NEAR + 1, 128, 64), BF16)],
        compiler_params=PARAMS,
        name="build",
    )(slot, near, packed_shift, rows, probe_before, probes, probe_after)

    scaled, one, half = pl.pallas_call(
        first_kernel,
        out_shape=(
            jax.ShapeDtypeStruct((8, 128, 2048), BF16),
            jax.ShapeDtypeStruct((8, 128, 64), F32),
            jax.ShapeDtypeStruct((4, 128, 128), BF16),
        ),
        in_specs=[VMEM] * 3,
        out_specs=(VMEM, VMEM, VMEM),
        compiler_params=PARAMS,
        name="first",
    )(peaks, blocks, operand)
    half_before, half_after = both(half)

    mixture = pl.pallas_call(
        second_kernel,
        out_shape=jax.ShapeDtypeStruct((8, 64, 128), BF16),
        in_specs=[SMEM] + [VMEM] * 6,
        out_specs=VMEM,
        scratch_shapes=[
            pltpu.VMEM((NEAR + 1, 128, 64), BF16),
            pltpu.VMEM((2, 2048, 64), BF16),
            pltpu.VMEM((128, 128), BF16),
        ],
        compiler_params=PARAMS,
        name="second",
    )(slot, scaled, half_before, half, half_after, one, turned)
    row_mixture = lax.all_to_all(mixture, "probe", 0, 0, tiled=True)

    density, force = pl.pallas_call(
        sample_kernel,
        out_shape=(
            jax.ShapeDtypeStruct((16, 8, 15, 128), BF16),
            jax.ShapeDtypeStruct((8, NEAR, 128), F32),
        ),
        in_specs=[SMEM, SMEM] + [VMEM] * 7,
        out_specs=(VMEM, VMEM),
        scratch_shapes=[
            pltpu.VMEM((128, 512), BF16),
            pltpu.VMEM((NEAR + 1, 128, 128), F32),
            pltpu.VMEM((16 * SLOTS, 128), F32),
            pltpu.VMEM((NEAR + 1, 3, 8, 128), F32),
        ],
        compiler_params=PARAMS,
        name="sample",
    )(
        slot, probe_rank.reshape(1), row_mixture, all_before, all_own, all_after,
        near, slot_shift, rows,
    )
    force = jnp.sum(lax.all_to_all(force, "probe", 0, 0, tiled=True), axis=0)
    from_after = around(force[0:8], space_count, -1)
    from_before = around(force[16:24], space_count, 1)
    forces = force[8:16] + from_after + from_before
    return density, forces[:, :96].reshape(8, 3, 32)


def solution(mesh):
    in_specs = (P("space", None, None), P("space", "probe", None), P("space", None))
    out_specs = (P("probe", "space", None, None), P("space", None, None))
    return jax.shard_map(
        per_device, mesh=mesh, in_specs=in_specs, out_specs=out_specs, check_vma=False
    )
```

```python
import functools
import math

import jax
import jax.numpy as jnp
import numpy as np
from jax import lax
from jax.experimental import pallas as pl
from jax.experimental.pallas import tpu as pltpu
from jax.sharding import PartitionSpec as P

SS_SIGMA = -1.938
SP_SIGMA = 1.745
PP_SIGMA = 3.05
PP_PI = -1.075
BOND_LENGTH = 2.35
SOFT_SQUARE = 0.25
CELL_EDGE = 10.86
COEFF_ZERO = 0.6
COEFF_ONE = -0.7
COEFF_TWO = 0.45

PP_SUM = PP_SIGMA - PP_PI
BOND_SQUARE = BOND_LENGTH * BOND_LENGTH
NEAR = 24
DEAD = 24
FAR = 1000.0
SLOTS = 16
F32 = jnp.float32
BF16 = jnp.bfloat16
WHOLE = pl.BlockSpec()
SMEM = pl.BlockSpec(memory_space=pltpu.SMEM)


def params(mebibytes):
    return pltpu.CompilerParams(vmem_limit_bytes=mebibytes * 1024 * 1024)


def slot_offsets():
    half = CELL_EDGE / 2.0
    table = [[0.0, 0.0, 0.0]]
    for sign_x in (-1.0, 1.0):
        for sign_y in (-1.0, 1.0):
            for sign_z in (-1.0, 1.0):
                table.append([sign_x * half, sign_y * half, sign_z * half])
    for axis_pick in range(3):
        for sign_a in (1.0, -1.0):
            entry = [0.0, 0.0, 0.0]
            entry[axis_pick] = sign_a * CELL_EDGE
            table.append(entry)
    table.append([0.0, 0.0, 0.0])
    return np.array(table, dtype=np.float32)


def fill_shifts(shift_ref):
    lane = lanes()
    table = slot_offsets()
    for g in range(4):
        for x in range(3):
            v = [float(table[4 * g + t, x]) for t in range(4)]
            shift_ref[g, x : x + 1, :] = jnp.where(
                lane < 32, v[0], jnp.where(lane < 64, v[1], jnp.where(lane < 96, v[2], v[3]))
            )


def lanes():
    return lax.broadcasted_iota(jnp.int32, (1, 128), 1)


def bond(columns, rows):
    d = [columns[x : x + 1, :] - rows[x] for x in range(3)]
    rho_square = d[0] * d[0] + d[1] * d[1] + d[2] * d[2] + SOFT_SQUARE
    inverse = lax.rsqrt(rho_square)
    radial = jnp.exp(1.0 - rho_square / BOND_SQUARE)
    return d, [v * inverse for v in d], radial, inverse


def four_slots(near_ref, slot_ref, shift_ref, c, g, lane):
    v = [near_ref[slot_ref[c, 4 * g + t]] for t in range(4)]
    joined = jnp.where(
        lane < 32, v[0], jnp.where(lane < 64, v[1], jnp.where(lane < 96, v[2], v[3]))
    )
    return joined + shift_ref[g]


def spectral_kernel(
    slot_ref, before_ref, own_ref, after_ref, near_ref, row_ref, peak_ref, shift_ref
):
    fill_shifts(shift_ref)
    for part, ref in enumerate((before_ref, own_ref, after_ref)):
        for x in range(3):
            coords = ref[x].astype(F32)
            wide = jnp.concatenate([coords] * 4, axis=1)
            for n in range(8):
                near_ref[8 * part + n, x : x + 1, :] = wide[n : n + 1, :]
            if part == 1:
                upright = wide.T
                for c in range(8):
                    row_ref[c, x] = jnp.broadcast_to(upright[0:32, c : c + 1], (32, 128))
    near_ref[DEAD] = jnp.full((8, 128), FAR, F32)
    lane = lanes()

    def one_cluster(c, peak):
        rows = [row_ref[c, x] for x in range(3)]
        sums = [jnp.zeros((32, 128), F32) for _ in range(4)]
        for g in range(4):
            columns = four_slots(near_ref, slot_ref, shift_ref, c, g, lane)
            _, cosine, radial, _ = bond(columns, rows)
            size = [jnp.abs(v) for v in cosine]
            sums[0] += (-SS_SIGMA + SP_SIGMA * (size[0] + size[1] + size[2])) * radial
            cross = {}
            for a in range(3):
                for b in range(a, 3):
                    product = cosine[a] * cosine[b] * PP_SUM
                    cross[a, b] = cross[b, a] = jnp.abs(product + PP_PI if a == b else product)
            for a in range(3):
                sums[1 + a] += (
                    SP_SIGMA * size[a] + cross[a, 0] + cross[a, 1] + cross[a, 2]
                ) * radial
        for v in sums:
            peak = jnp.maximum(peak, jnp.sum(v, axis=1, keepdims=True))
        return peak

    peak = lax.fori_loop(0, 8, one_cluster, jnp.zeros((32, 1), F32))
    peak_ref[...] = jnp.broadcast_to(jnp.max(peak), peak_ref.shape)


def gather_operand(slot_ref, source_ref, target_ref, c):
    for k in range(SLOTS):
        n = slot_ref[c, k]
        for b in range(4):
            low = 512 * (k // 4) + 128 * b + 32 * (k % 4)
            target_ref[low : low + 32, :] = source_ref[n, 32 * b : 32 * b + 32, :]


def first_kernel(
    slot_ref, peak_ref, near_ref, row_ref, before_ref, own_ref, after_ref,
    scaled_ref, operand_ref, turned_ref, one_ref, half_ref, probe_ref, shift_ref,
):
    fill_shifts(shift_ref)
    lane = lanes()
    inverse_peak = 1.0 / jnp.max(peak_ref[...])
    for part, ref in enumerate((before_ref, own_ref, after_ref)):
        for c in range(8):
            turned = ref[c].astype(F32).T
            if part == 1:
                turned_ref[c] = turned
            probe_ref[8 * part + c] = turned.astype(BF16)
    probe_ref[DEAD] = jnp.zeros((128, 64), BF16)

    def one_pair(pair, carry):
        for side in range(2):
            c = pair + 4 * side
            rows = [row_ref[c, x] for x in range(3)]
            gather_operand(slot_ref, probe_ref, operand_ref.at[c], c)
            for g in range(4):
                columns = four_slots(near_ref, slot_ref, shift_ref, c, g, lane)
                _, cosine, radial, _ = bond(columns, rows)
                radial = radial * inverse_peak
                place = functools.partial(block_at, scaled_ref, c, g)
                place(0, 0, SS_SIGMA * radial)
                sp = SP_SIGMA * radial
                pp = PP_SUM * radial
                pi = PP_PI * radial
                for a in range(3):
                    wave = cosine[a] * sp
                    place(0, a + 1, wave)
                    place(a + 1, 0, -wave)
                    leaning = cosine[a] * pp
                    for b in range(a, 3):
                        value = leaning * cosine[b]
                        if a == b:
                            place(a + 1, a + 1, value + pi)
                        else:
                            place(a + 1, b + 1, value)
                            place(b + 1, a + 1, value)
            one = jnp.dot(scaled_ref[c], operand_ref[c], preferred_element_type=F32)
            one_ref[c] = one
            half_ref[pair, :, 64 * side : 64 * side + 64] = one.astype(BF16)
        return carry

    lax.fori_loop(0, 4, one_pair, 0)


def block_at(scaled_ref, c, g, a, b, value):
    low = 512 * g + 128 * b
    scaled_ref[c, 32 * a : 32 * a + 32, low : low + 128] = value.astype(BF16)


def second_kernel(
    slot_ref, near_ref, row_ref, scaled_ref, operand_ref, turned_ref, one_ref,
    before_ref, own_ref, after_ref, send_ref, half_ref, gathered_ref, pull_ref, shift_ref,
):
    fill_shifts(shift_ref)
    lane = lanes()
    for part, ref in enumerate((before_ref, own_ref, after_ref)):
        for pair in range(4):
            half_ref[8 * part + pair] = ref[pair, :, 0:64]
            half_ref[8 * part + pair + 4] = ref[pair, :, 64:128]
    half_ref[DEAD] = jnp.zeros((128, 64), BF16)
    pull_ref[...] = jnp.zeros_like(pull_ref)
    on_row = lax.broadcasted_iota(jnp.int32, (32, 128), 0) == lax.broadcasted_iota(
        jnp.int32, (32, 128), 1
    )

    def one_pair(pair, carry):
        for side in range(2):
            c = pair + 4 * side
            gather_operand(slot_ref, half_ref, gathered_ref.at[side], c)
            two = jnp.dot(scaled_ref[c], gathered_ref[side], preferred_element_type=F32)
            probe = turned_ref[c]
            term_two = 2.0 * two - probe
            mixture = COEFF_ZERO * probe + COEFF_ONE * one_ref[c] + COEFF_TWO * term_two
            mixture = mixture.astype(BF16)
            wide = mixture.astype(F32)
            for q in range(8):
                send_ref[
                    q, pl.ds(pl.multiple_of(16 * pair, 16), 16), 64 * side : 64 * side + 64
                ] = wide[16 * q : 16 * q + 16, :]
            rows = [row_ref[c, x] for x in range(3)]
            own = [jnp.zeros((32, 128), F32) for _ in range(3)]
            for g in range(4):
                sample = lax.dot_general(
                    mixture,
                    operand_ref[c, 512 * g : 512 * g + 512, :],
                    (((1,), (1,)), ((), ())),
                    preferred_element_type=F32,
                )
                columns = four_slots(near_ref, slot_ref, shift_ref, c, g, lane)
                pulls = pair_pulls(sample, columns, rows)
                for x in range(3):
                    own[x] = own[x] + pulls[x]
                    folded = jnp.sum(pulls[x].reshape(4, 8, 128), axis=0)
                    for t in range(4):
                        n = slot_ref[c, 4 * g + t]
                        pull_ref[n, x] = pull_ref[n, x] - jnp.where(lane // 32 == t, folded, 0.0)
            for x in range(3):
                whole = jnp.broadcast_to(jnp.sum(own[x], axis=1, keepdims=True), (32, 128))
                placed = jnp.where(on_row, whole, 0.0)
                pull_ref[8 + c, x] = pull_ref[8 + c, x] + jnp.sum(
                    placed.reshape(4, 8, 128), axis=0
                )
        return carry

    lax.fori_loop(0, 4, one_pair, 0)

    total = jnp.sum(pull_ref[0:24], axis=2).reshape(72, 128)
    total = total + pltpu.roll(total, 64, 1)
    total = total + pltpu.roll(total, 32, 1)
    total = (total * (1.0 / 512.0)).reshape(24, 3, 128)
    joined = jnp.where(lane < 32, total[:, 0], jnp.where(lane < 64, total[:, 1], total[:, 2]))
    for q in range(8):
        send_ref[q, 64:88, :] = joined


def pair_pulls(sample, columns, rows):
    part = lambda a, b: sample[32 * a : 32 * a + 32, 128 * b : 128 * b + 128]
    d, cosine, radial, inverse = bond(columns, rows)
    mixed = [SP_SIGMA * (part(0, 1 + x) - part(1 + x, 0)) for x in range(3)]
    double = [2.0 * PP_SUM * part(1 + x, 1 + x) for x in range(3)]
    cross = {}
    for a, b in ((0, 1), (0, 2), (1, 2)):
        cross[a, b] = cross[b, a] = PP_SUM * (part(1 + a, 1 + b) + part(1 + b, 1 + a))
    bent = []
    for a in range(3):
        b, c = [x for x in range(3) if x != a]
        bent.append(double[a] * cosine[a] + cross[a, b] * cosine[b] + cross[a, c] * cosine[c])
    still = SS_SIGMA * part(0, 0) + PP_PI * (part(1, 1) + part(2, 2) + part(3, 3))
    straight = mixed[0] * cosine[0] + mixed[1] * cosine[1] + mixed[2] * cosine[2]
    curved = bent[0] * cosine[0] + bent[1] * cosine[1] + bent[2] * cosine[2]
    value = still + straight + 0.5 * curved
    across = radial * inverse
    inward = radial * value * (-2.0 / BOND_SQUARE) - across * inverse * (straight + curved)
    return [across * (mixed[x] + bent[x]) + inward * d[x] for x in range(3)]


def sample_kernel(
    slot_ref, received_ref, before_ref, own_ref, after_ref, density_ref, left_ref, sample_ref, turn_ref
):
    for q in range(8):
        block = received_ref[q, 0:64, :].astype(BF16)
        left_ref[0:64, 64 * q : 64 * q + 64] = block[:, 0:64]
        left_ref[64:128, 64 * q : 64 * q + 64] = block[:, 64:128]
    left = left_ref[...]
    scale = 1.0 / math.sqrt(512.0)
    for part, ref in enumerate((before_ref, own_ref, after_ref)):
        for pair in range(4):
            c = 2 * pair
            right = jnp.concatenate(
                [ref[:, c].reshape(512, 128), ref[:, c + 1].reshape(512, 128)], axis=1
            )
            product = jnp.dot(left, right, preferred_element_type=F32) * scale
            sample_ref[8 * part + c] = product[:, 0:128]
            sample_ref[8 * part + c + 1] = product[:, 128:256]
    sample_ref[DEAD] = jnp.zeros((128, 128), F32)
    for c in range(8):
        for k in range(15):
            turn_ref[pl.ds(8 * k + c, 16, stride=120), :] = sample_ref[
                slot_ref[c, k], 16 * c : 16 * c + 16, :
            ]
    for r in range(16):
        density_ref[r] = turn_ref[120 * r : 120 * r + 120].astype(BF16).reshape(15, 8, 128)


def around(block, size, distance):
    return lax.ppermute(block, "space", [((i - distance) % size, i) for i in range(size)])


def per_device(positions, probes, neighbours):
    space_count = lax.axis_size("space")
    space_rank = lax.axis_index("space")
    both = lambda block: (around(block, space_count, 1), around(block, space_count, -1))

    pos_own = positions.transpose(1, 0, 2)
    pos_before, pos_after = both(pos_own)
    probe_before, probe_after = both(probes)
    spread = jnp.broadcast_to(probes[None], (8,) + probes.shape)
    all_own = lax.all_to_all(spread, "probe", 0, 0, tiled=True).reshape(8, 8, 64, 128)

    pos_before, pos_after, all_own = lax.optimization_barrier((pos_before, pos_after, all_own))
    all_before, all_after = both(all_own)

    present = neighbours >= 0
    slot = (neighbours // 8 - space_rank + 1) % space_count * 8 + neighbours % 8
    slot = jnp.pad(jnp.where(present, slot, DEAD), ((0, 0), (0, 1)), constant_values=DEAD)

    near, rows, peak = pl.pallas_call(
        spectral_kernel,
        out_shape=(
            jax.ShapeDtypeStruct((NEAR + 1, 8, 128), F32),
            jax.ShapeDtypeStruct((8, 3, 32, 128), F32),
            jax.ShapeDtypeStruct((space_count, 128), F32),
        ),
        in_specs=[SMEM] + [WHOLE] * 3,
        out_specs=(WHOLE,) * 3,
        scratch_shapes=[pltpu.VMEM((4, 8, 128), F32)],
        compiler_params=params(4),
        name="spectral",
    )(slot, pos_before, pos_own, pos_after)
    peaks = lax.all_to_all(peak, "space", 0, 0, tiled=True)

    scaled, operand, turned, one, half = pl.pallas_call(
        first_kernel,
        out_shape=(
            jax.ShapeDtypeStruct((8, 128, 2048), BF16),
            jax.ShapeDtypeStruct((8, 2048, 64), BF16),
            jax.ShapeDtypeStruct((8, 128, 64), F32),
            jax.ShapeDtypeStruct((8, 128, 64), F32),
            jax.ShapeDtypeStruct((4, 128, 128), BF16),
        ),
        in_specs=[SMEM] + [WHOLE] * 6,
        out_specs=(WHOLE,) * 5,
        scratch_shapes=[pltpu.VMEM((NEAR + 1, 128, 64), BF16), pltpu.VMEM((4, 8, 128), F32)],
        compiler_params=params(16),
        name="first",
    )(slot, peaks, near, rows, probe_before, probes, probe_after)
    half_before, half_after = both(half)
    half_before, half_after, all_before, all_after = lax.optimization_barrier(
        (half_before, half_after, all_before, all_after)
    )

    send = pl.pallas_call(
        second_kernel,
        out_shape=jax.ShapeDtypeStruct((8, 88, 128), F32),
        in_specs=[SMEM] + [WHOLE] * 9,
        out_specs=WHOLE,
        scratch_shapes=[
            pltpu.VMEM((NEAR + 1, 128, 64), BF16),
            pltpu.VMEM((2, 2048, 64), BF16),
            pltpu.VMEM((NEAR + 1, 3, 8, 128), F32),
            pltpu.VMEM((4, 8, 128), F32),
        ],
        compiler_params=params(16),
        name="second",
    )(slot, near, rows, scaled, operand, turned, one, half_before, half, half_after)
    received = lax.all_to_all(send, "probe", 0, 0, tiled=True)
    force = jnp.sum(received[:, 64:88], axis=0)
    from_after = around(force[0:8], space_count, -1)
    from_before = around(force[16:24], space_count, 1)

    density = pl.pallas_call(
        sample_kernel,
        out_shape=jax.ShapeDtypeStruct((16, 15, 8, 128), BF16),
        in_specs=[SMEM] + [WHOLE] * 4,
        out_specs=WHOLE,
        scratch_shapes=[
            pltpu.VMEM((128, 512), BF16),
            pltpu.VMEM((NEAR + 1, 128, 128), F32),
            pltpu.VMEM((16 * 120, 128), F32),
        ],
        compiler_params=params(16),
        name="sample",
    )(slot, received, all_before, all_own, all_after)
    forces = force[8:16] + from_after + from_before
    forces = jnp.stack([forces[:, 32 * x : 32 * x + 32] for x in range(3)])
    return density.transpose(0, 2, 1, 3), forces.transpose(1, 0, 2)


def solution(mesh):
    in_specs = (P("space", None, None), P("space", "probe", None), P("space", None))
    out_specs = (P("probe", "space", None, None), P("space", None, None))
    return jax.shard_map(
        per_device, mesh=mesh, in_specs=in_specs, out_specs=out_specs, check_vma=False
    )
```

```python
import functools
import math

import jax
import jax.numpy as jnp
import numpy as np
from jax import lax
from jax.experimental import pallas as pl
from jax.experimental.pallas import tpu as pltpu
from jax.sharding import PartitionSpec as P

SS_SIGMA = -1.938
SP_SIGMA = 1.745
PP_SIGMA = 3.05
PP_PI = -1.075
BOND_LENGTH = 2.35
SOFT_SQUARE = 0.25
CELL_EDGE = 10.86
COEFF_ZERO = 0.6
COEFF_ONE = -0.7
COEFF_TWO = 0.45

PP_SUM = PP_SIGMA - PP_PI
BOND_SQUARE = BOND_LENGTH * BOND_LENGTH
NEAR = 24
DEAD = 24
FAR = 1000.0
SLOTS = 16
F32 = jnp.float32
BF16 = jnp.bfloat16
WHOLE = pl.BlockSpec()
SMEM = pl.BlockSpec(memory_space=pltpu.SMEM)
HBM = pl.BlockSpec(memory_space=pltpu.MemorySpace.HBM)
HEAVY = pl.CostEstimate(flops=0, transcendentals=0, bytes_accessed=60_000_000)
LIGHT = pl.CostEstimate(flops=0, transcendentals=0, bytes_accessed=0)


def params(mebibytes):
    return pltpu.CompilerParams(vmem_limit_bytes=mebibytes * 1024 * 1024)


def slot_offsets():
    half = CELL_EDGE / 2.0
    table = [[0.0, 0.0, 0.0]]
    for sign_x in (-1.0, 1.0):
        for sign_y in (-1.0, 1.0):
            for sign_z in (-1.0, 1.0):
                table.append([sign_x * half, sign_y * half, sign_z * half])
    for axis_pick in range(3):
        for sign_a in (1.0, -1.0):
            entry = [0.0, 0.0, 0.0]
            entry[axis_pick] = sign_a * CELL_EDGE
            table.append(entry)
    table.append([0.0, 0.0, 0.0])
    return np.array(table, dtype=np.float32)


def fill_shifts(shift_ref):
    lane = lanes()
    table = slot_offsets()
    for g in range(4):
        for x in range(3):
            v = [float(table[4 * g + t, x]) for t in range(4)]
            shift_ref[g, x : x + 1, :] = jnp.where(
                lane < 32, v[0], jnp.where(lane < 64, v[1], jnp.where(lane < 96, v[2], v[3]))
            )


def lanes():
    return lax.broadcasted_iota(jnp.int32, (1, 128), 1)


def bond(columns, rows):
    d = [columns[x : x + 1, :] - rows[x] for x in range(3)]
    rho_square = d[0] * d[0] + d[1] * d[1] + d[2] * d[2] + SOFT_SQUARE
    inverse = lax.rsqrt(rho_square)
    radial = jnp.exp(1.0 - rho_square / BOND_SQUARE)
    return d, [v * inverse for v in d], radial, inverse


def four_slots(near_ref, slot_ref, shift_ref, c, g, lane):
    v = [near_ref[slot_ref[c, 4 * g + t]] for t in range(4)]
    joined = jnp.where(
        lane < 32, v[0], jnp.where(lane < 64, v[1], jnp.where(lane < 96, v[2], v[3]))
    )
    return joined + shift_ref[g]


def spectral_kernel(
    slot_ref, before_ref, own_ref, after_ref, near_out, row_out, peak_out,
    coord_ref, near_ref, row_ref, peak_ref, shift_ref, in_sem, out_sem,
):
    copies = [
        pltpu.make_async_copy(ref, coord_ref.at[part], in_sem.at[part])
        for part, ref in enumerate((before_ref, own_ref, after_ref))
    ]
    for copy in copies:
        copy.start()
    fill_shifts(shift_ref)
    for part in range(3):
        copies[part].wait()
        for x in range(3):
            coords = coord_ref[part, x].astype(F32)
            wide = jnp.concatenate([coords] * 4, axis=1)
            for n in range(8):
                near_ref[8 * part + n, x : x + 1, :] = wide[n : n + 1, :]
            if part == 1:
                upright = wide.T
                for c in range(8):
                    row_ref[c, x] = jnp.broadcast_to(upright[0:32, c : c + 1], (32, 128))
    near_ref[DEAD] = jnp.full((8, 128), FAR, F32)
    kept = [
        pltpu.make_async_copy(near_ref, near_out, out_sem.at[0]),
        pltpu.make_async_copy(row_ref, row_out, out_sem.at[1]),
    ]
    for copy in kept:
        copy.start()
    lane = lanes()

    def one_cluster(c, peak):
        rows = [row_ref[c, x] for x in range(3)]
        sums = [jnp.zeros((32, 128), F32) for _ in range(4)]
        for g in range(4):
            columns = four_slots(near_ref, slot_ref, shift_ref, c, g, lane)
            _, cosine, radial, _ = bond(columns, rows)
            size = [jnp.abs(v) for v in cosine]
            sums[0] += (-SS_SIGMA + SP_SIGMA * (size[0] + size[1] + size[2])) * radial
            cross = {}
            for a in range(3):
                for b in range(a, 3):
                    product = cosine[a] * cosine[b] * PP_SUM
                    cross[a, b] = cross[b, a] = jnp.abs(product + PP_PI if a == b else product)
            for a in range(3):
                sums[1 + a] += (
                    SP_SIGMA * size[a] + cross[a, 0] + cross[a, 1] + cross[a, 2]
                ) * radial
        for v in sums:
            peak = jnp.maximum(peak, jnp.sum(v, axis=1, keepdims=True))
        return peak

    peak = lax.fori_loop(0, 8, one_cluster, jnp.zeros((32, 1), F32))
    peak_ref[...] = jnp.broadcast_to(jnp.max(peak), peak_ref.shape)
    copy = pltpu.make_async_copy(peak_ref, peak_out, out_sem.at[2])
    copy.start()
    copy.wait()
    for copy in kept:
        copy.wait()


def gather_operand(slot_ref, source_ref, target_ref, c):
    for k in range(SLOTS):
        n = slot_ref[c, k]
        for b in range(4):
            low = 512 * (k // 4) + 128 * b + 32 * (k % 4)
            target_ref[low : low + 32, :] = source_ref[n, 32 * b : 32 * b + 32, :]


def first_kernel(
    slot_ref, peak_in, near_in, row_in, before_ref, own_ref, after_ref,
    scaled_ref, operand_ref, turned_ref, one_ref, half_ref,
    peak_ref, near_ref, row_ref, flat_ref, probe_ref, shift_ref, sem,
):
    pieces = [
        pltpu.make_async_copy(ref, flat_ref.at[part], sem.at[part])
        for part, ref in enumerate((before_ref, own_ref, after_ref))
    ]
    copies = [
        pltpu.make_async_copy(peak_in, peak_ref, sem.at[3]),
        pltpu.make_async_copy(near_in, near_ref, sem.at[4]),
        pltpu.make_async_copy(row_in, row_ref, sem.at[5]),
    ]
    for copy in pieces + copies:
        copy.start()
    fill_shifts(shift_ref)
    lane = lanes()
    for part in range(3):
        pieces[part].wait()
        for c in range(8):
            turned = flat_ref[part, c].astype(F32).T
            if part == 1:
                turned_ref[c] = turned
            probe_ref[8 * part + c] = turned.astype(BF16)
    probe_ref[DEAD] = jnp.zeros((128, 64), BF16)
    for copy in copies:
        copy.wait()
    inverse_peak = 1.0 / jnp.max(peak_ref[...])

    def one_pair(pair, carry):
        for side in range(2):
            c = pair + 4 * side
            rows = [row_ref[c, x] for x in range(3)]
            gather_operand(slot_ref, probe_ref, operand_ref.at[c], c)
            for g in range(4):
                columns = four_slots(near_ref, slot_ref, shift_ref, c, g, lane)
                _, cosine, radial, _ = bond(columns, rows)
                radial = radial * inverse_peak
                place = functools.partial(block_at, scaled_ref, c, g)
                place(0, 0, SS_SIGMA * radial)
                sp = SP_SIGMA * radial
                pp = PP_SUM * radial
                pi = PP_PI * radial
                for a in range(3):
                    wave = cosine[a] * sp
                    place(0, a + 1, wave)
                    place(a + 1, 0, -wave)
                    leaning = cosine[a] * pp
                    for b in range(a, 3):
                        value = leaning * cosine[b]
                        if a == b:
                            place(a + 1, a + 1, value + pi)
                        else:
                            place(a + 1, b + 1, value)
                            place(b + 1, a + 1, value)
            one = jnp.dot(scaled_ref[c], operand_ref[c], preferred_element_type=F32)
            one_ref[c] = one
            half_ref[pair, :, 64 * side : 64 * side + 64] = one.astype(BF16)
        return carry

    lax.fori_loop(0, 4, one_pair, 0)


def block_at(scaled_ref, c, g, a, b, value):
    low = 512 * g + 128 * b
    scaled_ref[c, 32 * a : 32 * a + 32, low : low + 128] = value.astype(BF16)


def second_kernel(
    slot_ref, near_in, row_in, scaled_ref, operand_ref, turned_ref, one_ref,
    before_ref, own_ref, after_ref, send_ref,
    near_ref, row_ref, half_ref, gathered_ref, pull_ref, shift_ref, sem,
):
    copies = [
        pltpu.make_async_copy(near_in, near_ref, sem.at[0]),
        pltpu.make_async_copy(row_in, row_ref, sem.at[1]),
    ]
    for copy in copies:
        copy.start()
    fill_shifts(shift_ref)
    lane = lanes()
    for part, ref in enumerate((before_ref, own_ref, after_ref)):
        for pair in range(4):
            half_ref[8 * part + pair] = ref[pair, :, 0:64]
            half_ref[8 * part + pair + 4] = ref[pair, :, 64:128]
    half_ref[DEAD] = jnp.zeros((128, 64), BF16)
    pull_ref[...] = jnp.zeros_like(pull_ref)
    for copy in copies:
        copy.wait()
    on_row = lax.broadcasted_iota(jnp.int32, (32, 128), 0) == lax.broadcasted_iota(
        jnp.int32, (32, 128), 1
    )

    def one_pair(pair, carry):
        for side in range(2):
            c = pair + 4 * side
            gather_operand(slot_ref, half_ref, gathered_ref.at[side], c)
            two = jnp.dot(scaled_ref[c], gathered_ref[side], preferred_element_type=F32)
            probe = turned_ref[c]
            term_two = 2.0 * two - probe
            mixture = COEFF_ZERO * probe + COEFF_ONE * one_ref[c] + COEFF_TWO * term_two
            mixture = mixture.astype(BF16)
            wide = mixture.astype(F32)
            for q in range(8):
                send_ref[
                    q, pl.ds(pl.multiple_of(16 * pair, 16), 16), 64 * side : 64 * side + 64
                ] = wide[16 * q : 16 * q + 16, :]
            rows = [row_ref[c, x] for x in range(3)]
            own = [jnp.zeros((32, 128), F32) for _ in range(3)]
            for g in range(4):
                sample = lax.dot_general(
                    mixture,
                    operand_ref[c, 512 * g : 512 * g + 512, :],
                    (((1,), (1,)), ((), ())),
                    preferred_element_type=F32,
                )
                columns = four_slots(near_ref, slot_ref, shift_ref, c, g, lane)
                pulls = pair_pulls(sample, columns, rows)
                for x in range(3):
                    own[x] = own[x] + pulls[x]
                    folded = jnp.sum(pulls[x].reshape(4, 8, 128), axis=0)
                    for t in range(4):
                        n = slot_ref[c, 4 * g + t]
                        pull_ref[n, x] = pull_ref[n, x] - jnp.where(lane // 32 == t, folded, 0.0)
            for x in range(3):
                whole = jnp.broadcast_to(jnp.sum(own[x], axis=1, keepdims=True), (32, 128))
                placed = jnp.where(on_row, whole, 0.0)
                pull_ref[8 + c, x] = pull_ref[8 + c, x] + jnp.sum(
                    placed.reshape(4, 8, 128), axis=0
                )
        return carry

    lax.fori_loop(0, 4, one_pair, 0)

    total = jnp.sum(pull_ref[0:24], axis=2).reshape(72, 128)
    total = total + pltpu.roll(total, 64, 1)
    total = total + pltpu.roll(total, 32, 1)
    total = (total * (1.0 / 512.0)).reshape(24, 3, 128)
    joined = jnp.where(lane < 32, total[:, 0], jnp.where(lane < 64, total[:, 1], total[:, 2]))
    for q in range(8):
        send_ref[q, 64:88, :] = joined


def pair_pulls(sample, columns, rows):
    part = lambda a, b: sample[32 * a : 32 * a + 32, 128 * b : 128 * b + 128]
    d, cosine, radial, inverse = bond(columns, rows)
    mixed = [SP_SIGMA * (part(0, 1 + x) - part(1 + x, 0)) for x in range(3)]
    double = [2.0 * PP_SUM * part(1 + x, 1 + x) for x in range(3)]
    cross = {}
    for a, b in ((0, 1), (0, 2), (1, 2)):
        cross[a, b] = cross[b, a] = PP_SUM * (part(1 + a, 1 + b) + part(1 + b, 1 + a))
    bent = []
    for a in range(3):
        b, c = [x for x in range(3) if x != a]
        bent.append(double[a] * cosine[a] + cross[a, b] * cosine[b] + cross[a, c] * cosine[c])
    still = SS_SIGMA * part(0, 0) + PP_PI * (part(1, 1) + part(2, 2) + part(3, 3))
    straight = mixed[0] * cosine[0] + mixed[1] * cosine[1] + mixed[2] * cosine[2]
    curved = bent[0] * cosine[0] + bent[1] * cosine[1] + bent[2] * cosine[2]
    value = still + straight + 0.5 * curved
    across = radial * inverse
    inward = radial * value * (-2.0 / BOND_SQUARE) - across * inverse * (straight + curved)
    return [across * (mixed[x] + bent[x]) + inward * d[x] for x in range(3)]


def sample_kernel(
    slot_ref, received_ref, before_ref, own_ref, after_ref, density_ref, left_ref, sample_ref, turn_ref
):
    for q in range(8):
        block = received_ref[q, 0:64, :].astype(BF16)
        left_ref[0:64, 64 * q : 64 * q + 64] = block[:, 0:64]
        left_ref[64:128, 64 * q : 64 * q + 64] = block[:, 64:128]
    left = left_ref[...]
    scale = 1.0 / math.sqrt(512.0)
    for part, ref in enumerate((before_ref, own_ref, after_ref)):
        for pair in range(4):
            c = 2 * pair
            right = jnp.concatenate(
                [ref[:, c].reshape(512, 128), ref[:, c + 1].reshape(512, 128)], axis=1
            )
            product = jnp.dot(left, right, preferred_element_type=F32) * scale
            sample_ref[8 * part + c] = product[:, 0:128]
            sample_ref[8 * part + c + 1] = product[:, 128:256]
    sample_ref[DEAD] = jnp.zeros((128, 128), F32)
    for c in range(8):
        for k in range(15):
            turn_ref[pl.ds(8 * k + c, 16, stride=120), :] = sample_ref[
                slot_ref[c, k], 16 * c : 16 * c + 16, :
            ]
    for r in range(16):
        density_ref[r] = turn_ref[120 * r : 120 * r + 120].astype(BF16).reshape(15, 8, 128)


def around(block, size, distance):
    return lax.ppermute(block, "space", [((i - distance) % size, i) for i in range(size)])


def per_device(positions, probes, neighbours):
    space_count = lax.axis_size("space")
    space_rank = lax.axis_index("space")
    both = lambda block: (around(block, space_count, 1), around(block, space_count, -1))

    pos_own = positions.transpose(1, 0, 2)
    pos_before, pos_after = both(pos_own)
    probe_before, probe_after = both(probes)
    spread = jnp.broadcast_to(probes[None], (8,) + probes.shape)
    all_own = lax.all_to_all(spread, "probe", 0, 0, tiled=True).reshape(8, 8, 64, 128)

    present = neighbours >= 0
    slot = (neighbours // 8 - space_rank + 1) % space_count * 8 + neighbours % 8
    slot = jnp.pad(jnp.where(present, slot, DEAD), ((0, 0), (0, 1)), constant_values=DEAD)

    near, rows, peak = pl.pallas_call(
        spectral_kernel,
        out_shape=(
            jax.ShapeDtypeStruct((NEAR + 1, 8, 128), F32),
            jax.ShapeDtypeStruct((8, 3, 32, 128), F32),
            jax.ShapeDtypeStruct((space_count, 128), F32),
        ),
        in_specs=[SMEM] + [HBM] * 3,
        out_specs=(HBM,) * 3,
        scratch_shapes=[
            pltpu.VMEM((3, 3, 8, 32), BF16),
            pltpu.VMEM((NEAR + 1, 8, 128), F32),
            pltpu.VMEM((8, 3, 32, 128), F32),
            pltpu.VMEM((space_count, 128), F32),
            pltpu.VMEM((4, 8, 128), F32),
            pltpu.SemaphoreType.DMA((3,)),
            pltpu.SemaphoreType.DMA((3,)),
        ],
        cost_estimate=HEAVY,
        compiler_params=params(4),
        name="spectral",
    )(slot, pos_before, pos_own, pos_after)
    peak, all_own, probe_before, probe_after = lax.optimization_barrier(
        (peak, all_own, probe_before, probe_after)
    )
    peaks = lax.all_to_all(peak, "space", 0, 0, tiled=True)
    peaks, all_own = lax.optimization_barrier((peaks, all_own))
    all_before, all_after = both(all_own)

    scaled, operand, turned, one, half = pl.pallas_call(
        first_kernel,
        out_shape=(
            jax.ShapeDtypeStruct((8, 128, 2048), BF16),
            jax.ShapeDtypeStruct((8, 2048, 64), BF16),
            jax.ShapeDtypeStruct((8, 128, 64), F32),
            jax.ShapeDtypeStruct((8, 128, 64), F32),
            jax.ShapeDtypeStruct((4, 128, 128), BF16),
        ),
        in_specs=[SMEM] + [HBM] * 6,
        out_specs=(WHOLE,) * 5,
        scratch_shapes=[
            pltpu.VMEM((space_count, 128), F32),
            pltpu.VMEM((NEAR + 1, 8, 128), F32),
            pltpu.VMEM((8, 3, 32, 128), F32),
            pltpu.VMEM((3, 8, 64, 128), BF16),
            pltpu.VMEM((NEAR + 1, 128, 64), BF16),
            pltpu.VMEM((4, 8, 128), F32),
            pltpu.SemaphoreType.DMA((6,)),
        ],
        cost_estimate=LIGHT,
        compiler_params=params(16),
        name="first",
    )(slot, peaks, near, rows, probe_before, probes, probe_after)
    half_before, half_after = both(half)

    send = pl.pallas_call(
        second_kernel,
        out_shape=jax.ShapeDtypeStruct((8, 88, 128), F32),
        in_specs=[SMEM, HBM, HBM] + [WHOLE] * 7,
        out_specs=WHOLE,
        cost_estimate=LIGHT,
        scratch_shapes=[
            pltpu.VMEM((NEAR + 1, 8, 128), F32),
            pltpu.VMEM((8, 3, 32, 128), F32),
            pltpu.VMEM((NEAR + 1, 128, 64), BF16),
            pltpu.VMEM((2, 2048, 64), BF16),
            pltpu.VMEM((NEAR + 1, 3, 8, 128), F32),
            pltpu.VMEM((4, 8, 128), F32),
            pltpu.SemaphoreType.DMA((2,)),
        ],
        compiler_params=params(16),
        name="second",
    )(slot, near, rows, scaled, operand, turned, one, half_before, half, half_after)
    send, all_before, all_after = lax.optimization_barrier((send, all_before, all_after))
    received = lax.all_to_all(send, "probe", 0, 0, tiled=True)
    force = jnp.sum(received[:, 64:88], axis=0)
    from_after = around(force[0:8], space_count, -1)
    from_before = around(force[16:24], space_count, 1)

    density = pl.pallas_call(
        sample_kernel,
        out_shape=jax.ShapeDtypeStruct((16, 15, 8, 128), BF16),
        in_specs=[SMEM] + [WHOLE] * 4,
        out_specs=WHOLE,
        scratch_shapes=[
            pltpu.VMEM((128, 512), BF16),
            pltpu.VMEM((NEAR + 1, 128, 128), F32),
            pltpu.VMEM((16 * 120, 128), F32),
        ],
        compiler_params=params(16),
        name="sample",
    )(slot, received, all_before, all_own, all_after)
    forces = force[8:16] + from_after + from_before
    forces = jnp.stack([forces[:, 32 * x : 32 * x + 32] for x in range(3)])
    return density.transpose(0, 2, 1, 3), forces.transpose(1, 0, 2)


def solution(mesh):
    in_specs = (P("space", None, None), P("space", "probe", None), P("space", None))
    out_specs = (P("probe", "space", None, None), P("space", None, None))
    return jax.shard_map(
        per_device, mesh=mesh, in_specs=in_specs, out_specs=out_specs, check_vma=False
    )
```

```python
import functools
import math

import jax
import jax.numpy as jnp
import numpy as np
from jax import lax
from jax.experimental import pallas as pl
from jax.experimental.pallas import tpu as pltpu
from jax.sharding import PartitionSpec as P

SS_SIGMA = -1.938
SP_SIGMA = 1.745
PP_SIGMA = 3.05
PP_PI = -1.075
BOND_LENGTH = 2.35
SOFT_SQUARE = 0.25
CELL_EDGE = 10.86
COEFF_ZERO = 0.6
COEFF_ONE = -0.7
COEFF_TWO = 0.45

PP_SUM = PP_SIGMA - PP_PI
BOND_SQUARE = BOND_LENGTH * BOND_LENGTH
NEAR = 24
DEAD = 24
FAR = 1000.0
SLOTS = 16
F32 = jnp.float32
BF16 = jnp.bfloat16
WHOLE = pl.BlockSpec()
SMEM = pl.BlockSpec(memory_space=pltpu.SMEM)
HBM = pl.BlockSpec(memory_space=pltpu.MemorySpace.HBM)
HEAVY = pl.CostEstimate(flops=0, transcendentals=0, bytes_accessed=60_000_000)
LIGHT = pl.CostEstimate(flops=0, transcendentals=0, bytes_accessed=0)


def params(mebibytes):
    return pltpu.CompilerParams(vmem_limit_bytes=mebibytes * 1024 * 1024)


def slot_offsets():
    half = CELL_EDGE / 2.0
    table = [[0.0, 0.0, 0.0]]
    for sign_x in (-1.0, 1.0):
        for sign_y in (-1.0, 1.0):
            for sign_z in (-1.0, 1.0):
                table.append([sign_x * half, sign_y * half, sign_z * half])
    for axis_pick in range(3):
        for sign_a in (1.0, -1.0):
            entry = [0.0, 0.0, 0.0]
            entry[axis_pick] = sign_a * CELL_EDGE
            table.append(entry)
    table.append([0.0, 0.0, 0.0])
    return np.array(table, dtype=np.float32)


def fill_shifts(shift_ref):
    lane = lanes()
    table = slot_offsets()
    for g in range(4):
        for x in range(3):
            v = [float(table[4 * g + t, x]) for t in range(4)]
            shift_ref[g, x : x + 1, :] = jnp.where(
                lane < 32, v[0], jnp.where(lane < 64, v[1], jnp.where(lane < 96, v[2], v[3]))
            )


def lanes():
    return lax.broadcasted_iota(jnp.int32, (1, 128), 1)


def bond(columns, rows):
    d = [columns[x : x + 1, :] - rows[x] for x in range(3)]
    rho_square = d[0] * d[0] + d[1] * d[1] + d[2] * d[2] + SOFT_SQUARE
    inverse = lax.rsqrt(rho_square)
    radial = jnp.exp(1.0 - rho_square / BOND_SQUARE)
    return d, [v * inverse for v in d], radial, inverse


def four_slots(near_ref, slot_ref, shift_ref, c, g, lane):
    v = [near_ref[slot_ref[c, 4 * g + t]] for t in range(4)]
    joined = jnp.where(
        lane < 32, v[0], jnp.where(lane < 64, v[1], jnp.where(lane < 96, v[2], v[3]))
    )
    return joined + shift_ref[g]


def spectral_kernel(
    slot_ref, before_ref, own_ref, after_ref, near_out, row_out, peak_out,
    coord_ref, near_ref, row_ref, peak_ref, shift_ref, in_sem, out_sem,
):
    copies = [
        pltpu.make_async_copy(ref.at[512:536], coord_ref.at[part], in_sem.at[part])
        for part, ref in enumerate((before_ref, own_ref, after_ref))
    ]
    for copy in copies:
        copy.start()
    fill_shifts(shift_ref)
    for part in range(3):
        copies[part].wait()
        for x in range(3):
            coords = coord_ref[part, 8 * x : 8 * x + 8, 0:32].astype(F32)
            wide = jnp.concatenate([coords] * 4, axis=1)
            for n in range(8):
                near_ref[8 * part + n, x : x + 1, :] = wide[n : n + 1, :]
            if part == 1:
                upright = wide.T
                for c in range(8):
                    row_ref[c, x] = jnp.broadcast_to(upright[0:32, c : c + 1], (32, 128))
    near_ref[DEAD] = jnp.full((8, 128), FAR, F32)
    kept = [
        pltpu.make_async_copy(near_ref, near_out, out_sem.at[0]),
        pltpu.make_async_copy(row_ref, row_out, out_sem.at[1]),
    ]
    for copy in kept:
        copy.start()
    lane = lanes()

    def one_cluster(c, peak):
        rows = [row_ref[c, x] for x in range(3)]
        sums = [jnp.zeros((32, 128), F32) for _ in range(4)]
        for g in range(4):
            columns = four_slots(near_ref, slot_ref, shift_ref, c, g, lane)
            _, cosine, radial, _ = bond(columns, rows)
            size = [jnp.abs(v) for v in cosine]
            sums[0] += (-SS_SIGMA + SP_SIGMA * (size[0] + size[1] + size[2])) * radial
            cross = {}
            for a in range(3):
                for b in range(a, 3):
                    product = cosine[a] * cosine[b] * PP_SUM
                    cross[a, b] = cross[b, a] = jnp.abs(product + PP_PI if a == b else product)
            for a in range(3):
                sums[1 + a] += (
                    SP_SIGMA * size[a] + cross[a, 0] + cross[a, 1] + cross[a, 2]
                ) * radial
        for v in sums:
            peak = jnp.maximum(peak, jnp.sum(v, axis=1, keepdims=True))
        return peak

    peak = lax.fori_loop(0, 8, one_cluster, jnp.zeros((32, 1), F32))
    peak_ref[...] = jnp.broadcast_to(jnp.max(peak), peak_ref.shape)
    copy = pltpu.make_async_copy(peak_ref, peak_out, out_sem.at[2])
    copy.start()
    copy.wait()
    for copy in kept:
        copy.wait()


def gather_operand(slot_ref, source_ref, target_ref, c):
    for k in range(SLOTS):
        n = slot_ref[c, k]
        for b in range(4):
            low = 512 * (k // 4) + 128 * b + 32 * (k % 4)
            target_ref[low : low + 32, :] = source_ref[n, 32 * b : 32 * b + 32, :]


def first_kernel(
    slot_ref, peak_in, near_in, row_in, before_ref, own_ref, after_ref,
    scaled_ref, operand_ref, turned_ref, one_ref, half_ref,
    peak_ref, near_ref, row_ref, flat_ref, probe_ref, shift_ref, sem,
):
    pieces = [
        pltpu.make_async_copy(ref.at[0:512], flat_ref.at[part], sem.at[part])
        for part, ref in enumerate((before_ref, own_ref, after_ref))
    ]
    copies = [
        pltpu.make_async_copy(peak_in, peak_ref, sem.at[3]),
        pltpu.make_async_copy(near_in, near_ref, sem.at[4]),
        pltpu.make_async_copy(row_in, row_ref, sem.at[5]),
    ]
    for copy in pieces + copies:
        copy.start()
    fill_shifts(shift_ref)
    lane = lanes()
    for part in range(3):
        pieces[part].wait()
        for c in range(8):
            turned = flat_ref[part, 64 * c : 64 * c + 64].astype(F32).T
            if part == 1:
                turned_ref[c] = turned
            probe_ref[8 * part + c] = turned.astype(BF16)
    probe_ref[DEAD] = jnp.zeros((128, 64), BF16)
    for copy in copies:
        copy.wait()
    inverse_peak = 1.0 / jnp.max(peak_ref[...])

    def one_pair(pair, carry):
        for side in range(2):
            c = pair + 4 * side
            rows = [row_ref[c, x] for x in range(3)]
            gather_operand(slot_ref, probe_ref, operand_ref.at[c], c)
            for g in range(4):
                columns = four_slots(near_ref, slot_ref, shift_ref, c, g, lane)
                _, cosine, radial, _ = bond(columns, rows)
                radial = radial * inverse_peak
                place = functools.partial(block_at, scaled_ref, c, g)
                place(0, 0, SS_SIGMA * radial)
                sp = SP_SIGMA * radial
                pp = PP_SUM * radial
                pi = PP_PI * radial
                for a in range(3):
                    wave = cosine[a] * sp
                    place(0, a + 1, wave)
                    place(a + 1, 0, -wave)
                    leaning = cosine[a] * pp
                    for b in range(a, 3):
                        value = leaning * cosine[b]
                        if a == b:
                            place(a + 1, a + 1, value + pi)
                        else:
                            place(a + 1, b + 1, value)
                            place(b + 1, a + 1, value)
            one = jnp.dot(scaled_ref[c], operand_ref[c], preferred_element_type=F32)
            one_ref[c] = one
            half_ref[pair, :, 64 * side : 64 * side + 64] = one.astype(BF16)
        return carry

    lax.fori_loop(0, 4, one_pair, 0)


def block_at(scaled_ref, c, g, a, b, value):
    low = 512 * g + 128 * b
    scaled_ref[c, 32 * a : 32 * a + 32, low : low + 128] = value.astype(BF16)


def second_kernel(
    slot_ref, near_in, row_in, scaled_ref, operand_ref, turned_ref, one_ref,
    before_ref, own_ref, after_ref, send_ref,
    near_ref, row_ref, half_ref, gathered_ref, pull_ref, shift_ref, sem,
):
    copies = [
        pltpu.make_async_copy(near_in, near_ref, sem.at[0]),
        pltpu.make_async_copy(row_in, row_ref, sem.at[1]),
    ]
    for copy in copies:
        copy.start()
    fill_shifts(shift_ref)
    lane = lanes()
    for part, ref in enumerate((before_ref, own_ref, after_ref)):
        for pair in range(4):
            half_ref[8 * part + pair] = ref[pair, :, 0:64]
            half_ref[8 * part + pair + 4] = ref[pair, :, 64:128]
    half_ref[DEAD] = jnp.zeros((128, 64), BF16)
    pull_ref[...] = jnp.zeros_like(pull_ref)
    for copy in copies:
        copy.wait()
    on_row = lax.broadcasted_iota(jnp.int32, (32, 128), 0) == lax.broadcasted_iota(
        jnp.int32, (32, 128), 1
    )

    def one_pair(pair, carry):
        for side in range(2):
            c = pair + 4 * side
            gather_operand(slot_ref, half_ref, gathered_ref.at[side], c)
            two = jnp.dot(scaled_ref[c], gathered_ref[side], preferred_element_type=F32)
            probe = turned_ref[c]
            term_two = 2.0 * two - probe
            mixture = COEFF_ZERO * probe + COEFF_ONE * one_ref[c] + COEFF_TWO * term_two
            mixture = mixture.astype(BF16)
            wide = mixture.astype(F32)
            for q in range(8):
                send_ref[
                    q, pl.ds(pl.multiple_of(16 * pair, 16), 16), 64 * side : 64 * side + 64
                ] = wide[16 * q : 16 * q + 16, :]
            rows = [row_ref[c, x] for x in range(3)]
            own = [jnp.zeros((32, 128), F32) for _ in range(3)]
            for g in range(4):
                sample = lax.dot_general(
                    mixture,
                    operand_ref[c, 512 * g : 512 * g + 512, :],
                    (((1,), (1,)), ((), ())),
                    preferred_element_type=F32,
                )
                columns = four_slots(near_ref, slot_ref, shift_ref, c, g, lane)
                pulls = pair_pulls(sample, columns, rows)
                for x in range(3):
                    own[x] = own[x] + pulls[x]
                    folded = jnp.sum(pulls[x].reshape(4, 8, 128), axis=0)
                    for t in range(4):
                        n = slot_ref[c, 4 * g + t]
                        pull_ref[n, x] = pull_ref[n, x] - jnp.where(lane // 32 == t, folded, 0.0)
            for x in range(3):
                whole = jnp.broadcast_to(jnp.sum(own[x], axis=1, keepdims=True), (32, 128))
                placed = jnp.where(on_row, whole, 0.0)
                pull_ref[8 + c, x] = pull_ref[8 + c, x] + jnp.sum(
                    placed.reshape(4, 8, 128), axis=0
                )
        return carry

    lax.fori_loop(0, 4, one_pair, 0)

    total = jnp.sum(pull_ref[0:24], axis=2).reshape(72, 128)
    total = total + pltpu.roll(total, 64, 1)
    total = total + pltpu.roll(total, 32, 1)
    total = (total * (1.0 / 512.0)).reshape(24, 3, 128)
    joined = jnp.where(lane < 32, total[:, 0], jnp.where(lane < 64, total[:, 1], total[:, 2]))
    for q in range(8):
        send_ref[q, 64:88, :] = joined


def pair_pulls(sample, columns, rows):
    part = lambda a, b: sample[32 * a : 32 * a + 32, 128 * b : 128 * b + 128]
    d, cosine, radial, inverse = bond(columns, rows)
    mixed = [SP_SIGMA * (part(0, 1 + x) - part(1 + x, 0)) for x in range(3)]
    double = [2.0 * PP_SUM * part(1 + x, 1 + x) for x in range(3)]
    cross = {}
    for a, b in ((0, 1), (0, 2), (1, 2)):
        cross[a, b] = cross[b, a] = PP_SUM * (part(1 + a, 1 + b) + part(1 + b, 1 + a))
    bent = []
    for a in range(3):
        b, c = [x for x in range(3) if x != a]
        bent.append(double[a] * cosine[a] + cross[a, b] * cosine[b] + cross[a, c] * cosine[c])
    still = SS_SIGMA * part(0, 0) + PP_PI * (part(1, 1) + part(2, 2) + part(3, 3))
    straight = mixed[0] * cosine[0] + mixed[1] * cosine[1] + mixed[2] * cosine[2]
    curved = bent[0] * cosine[0] + bent[1] * cosine[1] + bent[2] * cosine[2]
    value = still + straight + 0.5 * curved
    across = radial * inverse
    inward = radial * value * (-2.0 / BOND_SQUARE) - across * inverse * (straight + curved)
    return [across * (mixed[x] + bent[x]) + inward * d[x] for x in range(3)]


def sample_kernel(slot_ref, received_ref, near_ref, density_ref, left_ref, sample_ref, turn_ref):
    for q in range(8):
        block = received_ref[q, 0:64, :].astype(BF16)
        left_ref[0:64, 64 * q : 64 * q + 64] = block[:, 0:64]
        left_ref[64:128, 64 * q : 64 * q + 64] = block[:, 64:128]
    left = left_ref[...]
    scale = 1.0 / math.sqrt(512.0)
    for part in range(3):
        for pair in range(4):
            c = 2 * pair
            right = jnp.concatenate(
                [
                    near_ref[:, part, 64 * n : 64 * n + 64, :].reshape(512, 128)
                    for n in (c, c + 1)
                ],
                axis=1,
            )
            product = jnp.dot(left, right, preferred_element_type=F32) * scale
            sample_ref[8 * part + c] = product[:, 0:128]
            sample_ref[8 * part + c + 1] = product[:, 128:256]
    sample_ref[DEAD] = jnp.zeros((128, 128), F32)
    for c in range(8):
        for k in range(15):
            turn_ref[pl.ds(8 * k + c, 16, stride=120), :] = sample_ref[
                slot_ref[c, k], 16 * c : 16 * c + 16, :
            ]
    for r in range(16):
        density_ref[r] = turn_ref[120 * r : 120 * r + 120].astype(BF16).reshape(15, 8, 128)


def around(block, size, distance):
    return lax.ppermute(block, "space", [((i - distance) % size, i) for i in range(size)])


def per_device(positions, probes, neighbours):
    space_count = lax.axis_size("space")
    space_rank = lax.axis_index("space")
    both = lambda block: (around(block, space_count, 1), around(block, space_count, -1))

    coords = jnp.pad(positions.transpose(1, 0, 2), ((0, 0), (0, 0), (0, 96)))
    own = jnp.concatenate([probes.reshape(512, 128), coords.reshape(24, 128)])
    before, after = both(own)
    near_all = lax.all_gather(jnp.stack([before, own, after]), "probe")

    present = neighbours >= 0
    slot = (neighbours // 8 - space_rank + 1) % space_count * 8 + neighbours % 8
    slot = jnp.pad(jnp.where(present, slot, DEAD), ((0, 0), (0, 1)), constant_values=DEAD)

    near, rows, peak = pl.pallas_call(
        spectral_kernel,
        out_shape=(
            jax.ShapeDtypeStruct((NEAR + 1, 8, 128), F32),
            jax.ShapeDtypeStruct((8, 3, 32, 128), F32),
            jax.ShapeDtypeStruct((space_count, 128), F32),
        ),
        in_specs=[SMEM] + [HBM] * 3,
        out_specs=(HBM,) * 3,
        scratch_shapes=[
            pltpu.VMEM((3, 24, 128), BF16),
            pltpu.VMEM((NEAR + 1, 8, 128), F32),
            pltpu.VMEM((8, 3, 32, 128), F32),
            pltpu.VMEM((space_count, 128), F32),
            pltpu.VMEM((4, 8, 128), F32),
            pltpu.SemaphoreType.DMA((3,)),
            pltpu.SemaphoreType.DMA((3,)),
        ],
        cost_estimate=HEAVY,
        compiler_params=params(4),
        name="spectral",
    )(slot, before, own, after)
    peaks = lax.all_to_all(peak, "space", 0, 0, tiled=True)

    scaled, operand, turned, one, half = pl.pallas_call(
        first_kernel,
        out_shape=(
            jax.ShapeDtypeStruct((8, 128, 2048), BF16),
            jax.ShapeDtypeStruct((8, 2048, 64), BF16),
            jax.ShapeDtypeStruct((8, 128, 64), F32),
            jax.ShapeDtypeStruct((8, 128, 64), F32),
            jax.ShapeDtypeStruct((4, 128, 128), BF16),
        ),
        in_specs=[SMEM] + [HBM] * 6,
        out_specs=(WHOLE,) * 5,
        scratch_shapes=[
            pltpu.VMEM((space_count, 128), F32),
            pltpu.VMEM((NEAR + 1, 8, 128), F32),
            pltpu.VMEM((8, 3, 32, 128), F32),
            pltpu.VMEM((3, 512, 128), BF16),
            pltpu.VMEM((NEAR + 1, 128, 64), BF16),
            pltpu.VMEM((4, 8, 128), F32),
            pltpu.SemaphoreType.DMA((6,)),
        ],
        cost_estimate=LIGHT,
        compiler_params=params(16),
        name="first",
    )(slot, peaks, near, rows, before, own, after)
    half_before, half_after = both(half)

    send = pl.pallas_call(
        second_kernel,
        out_shape=jax.ShapeDtypeStruct((8, 88, 128), F32),
        in_specs=[SMEM, HBM, HBM] + [WHOLE] * 7,
        out_specs=WHOLE,
        cost_estimate=LIGHT,
        scratch_shapes=[
            pltpu.VMEM((NEAR + 1, 8, 128), F32),
            pltpu.VMEM((8, 3, 32, 128), F32),
            pltpu.VMEM((NEAR + 1, 128, 64), BF16),
            pltpu.VMEM((2, 2048, 64), BF16),
            pltpu.VMEM((NEAR + 1, 3, 8, 128), F32),
            pltpu.VMEM((4, 8, 128), F32),
            pltpu.SemaphoreType.DMA((2,)),
        ],
        compiler_params=params(16),
        name="second",
    )(slot, near, rows, scaled, operand, turned, one, half_before, half, half_after)
    received = lax.all_to_all(send, "probe", 0, 0, tiled=True)
    force = jnp.sum(received[:, 64:88], axis=0)
    from_after = around(force[0:8], space_count, -1)
    from_before = around(force[16:24], space_count, 1)

    density = pl.pallas_call(
        sample_kernel,
        out_shape=jax.ShapeDtypeStruct((16, 15, 8, 128), BF16),
        in_specs=[SMEM, WHOLE, WHOLE],
        out_specs=WHOLE,
        scratch_shapes=[
            pltpu.VMEM((128, 512), BF16),
            pltpu.VMEM((NEAR + 1, 128, 128), F32),
            pltpu.VMEM((16 * 120, 128), F32),
        ],
        compiler_params=params(16),
        name="sample",
    )(slot, received, near_all)
    forces = force[8:16] + from_after + from_before
    forces = jnp.stack([forces[:, 32 * x : 32 * x + 32] for x in range(3)])
    return density.transpose(0, 2, 1, 3), forces.transpose(1, 0, 2)


def solution(mesh):
    in_specs = (P("space", None, None), P("space", "probe", None), P("space", None))
    out_specs = (P("probe", "space", None, None), P("space", None, None))
    return jax.shard_map(
        per_device, mesh=mesh, in_specs=in_specs, out_specs=out_specs, check_vma=False
    )
```

```python
import functools
import math

import jax
import jax.numpy as jnp
import numpy as np
from jax import lax
from jax.experimental import pallas as pl
from jax.experimental.pallas import tpu as pltpu
from jax.sharding import PartitionSpec as P

SS_SIGMA = -1.938
SP_SIGMA = 1.745
PP_SIGMA = 3.05
PP_PI = -1.075
BOND_LENGTH = 2.35
SOFT_SQUARE = 0.25
CELL_EDGE = 10.86
COEFF_ZERO = 0.6
COEFF_ONE = -0.7
COEFF_TWO = 0.45

PP_SUM = PP_SIGMA - PP_PI
BOND_SQUARE = BOND_LENGTH * BOND_LENGTH
NEAR = 24
DEAD = 24
FAR = 1000.0
SLOTS = 16
F32 = jnp.float32
BF16 = jnp.bfloat16
WHOLE = pl.BlockSpec()
SMEM = pl.BlockSpec(memory_space=pltpu.SMEM)
HBM = pl.BlockSpec(memory_space=pltpu.MemorySpace.HBM)
HEAVY = pl.CostEstimate(flops=0, transcendentals=0, bytes_accessed=60_000_000)
LIGHT = pl.CostEstimate(flops=0, transcendentals=0, bytes_accessed=0)


def params(mebibytes):
    return pltpu.CompilerParams(vmem_limit_bytes=mebibytes * 1024 * 1024)


def slot_offsets():
    half = CELL_EDGE / 2.0
    table = [[0.0, 0.0, 0.0]]
    for sign_x in (-1.0, 1.0):
        for sign_y in (-1.0, 1.0):
            for sign_z in (-1.0, 1.0):
                table.append([sign_x * half, sign_y * half, sign_z * half])
    for axis_pick in range(3):
        for sign_a in (1.0, -1.0):
            entry = [0.0, 0.0, 0.0]
            entry[axis_pick] = sign_a * CELL_EDGE
            table.append(entry)
    table.append([0.0, 0.0, 0.0])
    return np.array(table, dtype=np.float32)


def fill_shifts(shift_ref):
    lane = lanes()
    table = slot_offsets()
    for g in range(4):
        for x in range(3):
            v = [float(table[4 * g + t, x]) for t in range(4)]
            shift_ref[g, x : x + 1, :] = jnp.where(
                lane < 32, v[0], jnp.where(lane < 64, v[1], jnp.where(lane < 96, v[2], v[3]))
            )


def lanes():
    return lax.broadcasted_iota(jnp.int32, (1, 128), 1)


def bond(columns, rows):
    d = [columns[x : x + 1, :] - rows[x] for x in range(3)]
    rho_square = d[0] * d[0] + d[1] * d[1] + d[2] * d[2] + SOFT_SQUARE
    inverse = lax.rsqrt(rho_square)
    radial = jnp.exp(1.0 - rho_square / BOND_SQUARE)
    return d, [v * inverse for v in d], radial, inverse


def four_slots(near_ref, slot_ref, shift_ref, c, g, lane):
    v = [near_ref[slot_ref[c, 4 * g + t]] for t in range(4)]
    joined = jnp.where(
        lane < 32, v[0], jnp.where(lane < 64, v[1], jnp.where(lane < 96, v[2], v[3]))
    )
    return joined + shift_ref[g]


def spectral_kernel(
    slot_ref, before_ref, own_ref, after_ref, near_out, row_out, peak_out,
    coord_ref, near_ref, row_ref, peak_ref, shift_ref, in_sem, out_sem,
):
    copies = [
        pltpu.make_async_copy(ref.at[512:536], coord_ref.at[part], in_sem.at[part])
        for part, ref in enumerate((before_ref, own_ref, after_ref))
    ]
    for copy in copies:
        copy.start()
    fill_shifts(shift_ref)
    for part in range(3):
        copies[part].wait()
        for x in range(3):
            coords = coord_ref[part, 8 * x : 8 * x + 8, 0:32].astype(F32)
            wide = jnp.concatenate([coords] * 4, axis=1)
            for n in range(8):
                near_ref[8 * part + n, x : x + 1, :] = wide[n : n + 1, :]
            if part == 1:
                upright = wide.T
                for c in range(8):
                    row_ref[c, x] = jnp.broadcast_to(upright[0:32, c : c + 1], (32, 128))
    near_ref[DEAD] = jnp.full((8, 128), FAR, F32)
    kept = [
        pltpu.make_async_copy(near_ref, near_out, out_sem.at[0]),
        pltpu.make_async_copy(row_ref, row_out, out_sem.at[1]),
    ]
    for copy in kept:
        copy.start()
    lane = lanes()

    def one_cluster(c, peak):
        rows = [row_ref[c, x] for x in range(3)]
        sums = [jnp.zeros((32, 128), F32) for _ in range(4)]
        for g in range(4):
            columns = four_slots(near_ref, slot_ref, shift_ref, c, g, lane)
            _, cosine, radial, _ = bond(columns, rows)
            size = [jnp.abs(v) for v in cosine]
            sums[0] += (-SS_SIGMA + SP_SIGMA * (size[0] + size[1] + size[2])) * radial
            cross = {}
            for a in range(3):
                for b in range(a, 3):
                    product = cosine[a] * cosine[b] * PP_SUM
                    cross[a, b] = cross[b, a] = jnp.abs(product + PP_PI if a == b else product)
            for a in range(3):
                sums[1 + a] += (
                    SP_SIGMA * size[a] + cross[a, 0] + cross[a, 1] + cross[a, 2]
                ) * radial
        for v in sums:
            peak = jnp.maximum(peak, jnp.sum(v, axis=1, keepdims=True))
        return peak

    peak = lax.fori_loop(0, 8, one_cluster, jnp.zeros((32, 1), F32))
    peak_ref[...] = jnp.broadcast_to(jnp.max(peak), peak_ref.shape)
    copy = pltpu.make_async_copy(peak_ref, peak_out, out_sem.at[2])
    copy.start()
    copy.wait()
    for copy in kept:
        copy.wait()


def gather_operand(slot_ref, source_ref, target_ref, c):
    for k in range(SLOTS):
        n = slot_ref[c, k]
        for b in range(4):
            low = 512 * (k // 4) + 128 * b + 32 * (k % 4)
            target_ref[low : low + 32, :] = source_ref[n, 32 * b : 32 * b + 32, :]


def first_kernel(
    slot_ref, peak_in, near_in, row_in, before_ref, own_ref, after_ref,
    scaled_ref, operand_ref, turned_ref, one_ref, half_ref,
    peak_ref, near_ref, row_ref, flat_ref, probe_ref, shift_ref, sem,
):
    pieces = [
        pltpu.make_async_copy(ref.at[0:512], flat_ref.at[part], sem.at[part])
        for part, ref in enumerate((before_ref, own_ref, after_ref))
    ]
    copies = [
        pltpu.make_async_copy(peak_in, peak_ref, sem.at[3]),
        pltpu.make_async_copy(near_in, near_ref, sem.at[4]),
        pltpu.make_async_copy(row_in, row_ref, sem.at[5]),
    ]
    for copy in pieces + copies:
        copy.start()
    fill_shifts(shift_ref)
    lane = lanes()
    for part in range(3):
        pieces[part].wait()
        for c in range(8):
            turned = flat_ref[part, 64 * c : 64 * c + 64].astype(F32).T
            if part == 1:
                turned_ref[c] = turned
            probe_ref[8 * part + c] = turned.astype(BF16)
    probe_ref[DEAD] = jnp.zeros((128, 64), BF16)
    for copy in copies:
        copy.wait()
    inverse_peak = 1.0 / jnp.max(peak_ref[...])

    def one_pair(pair, carry):
        for side in range(2):
            c = pair + 4 * side
            rows = [row_ref[c, x] for x in range(3)]
            gather_operand(slot_ref, probe_ref, operand_ref.at[c], c)
            for g in range(4):
                columns = four_slots(near_ref, slot_ref, shift_ref, c, g, lane)
                _, cosine, radial, _ = bond(columns, rows)
                radial = radial * inverse_peak
                place = functools.partial(block_at, scaled_ref, c, g)
                place(0, 0, SS_SIGMA * radial)
                sp = SP_SIGMA * radial
                pp = PP_SUM * radial
                pi = PP_PI * radial
                for a in range(3):
                    wave = cosine[a] * sp
                    place(0, a + 1, wave)
                    place(a + 1, 0, -wave)
                    leaning = cosine[a] * pp
                    for b in range(a, 3):
                        value = leaning * cosine[b]
                        if a == b:
                            place(a + 1, a + 1, value + pi)
                        else:
                            place(a + 1, b + 1, value)
                            place(b + 1, a + 1, value)
            one = jnp.dot(scaled_ref[c], operand_ref[c], preferred_element_type=F32)
            one_ref[c] = one
            half_ref[pair, :, 64 * side : 64 * side + 64] = one.astype(BF16)
        return carry

    lax.fori_loop(0, 4, one_pair, 0)


def block_at(scaled_ref, c, g, a, b, value):
    low = 512 * g + 128 * b
    scaled_ref[c, 32 * a : 32 * a + 32, low : low + 128] = value.astype(BF16)


def second_kernel(
    slot_ref, near_in, row_in, scaled_ref, operand_ref, turned_ref, one_ref,
    before_ref, own_ref, after_ref, send_ref,
    near_ref, row_ref, half_ref, gathered_ref, pull_ref, shift_ref, sem,
):
    copies = [
        pltpu.make_async_copy(near_in, near_ref, sem.at[0]),
        pltpu.make_async_copy(row_in, row_ref, sem.at[1]),
    ]
    for copy in copies:
        copy.start()
    fill_shifts(shift_ref)
    lane = lanes()
    for part, ref in enumerate((before_ref, own_ref, after_ref)):
        for pair in range(4):
            half_ref[8 * part + pair] = ref[pair, :, 0:64]
            half_ref[8 * part + pair + 4] = ref[pair, :, 64:128]
    half_ref[DEAD] = jnp.zeros((128, 64), BF16)
    pull_ref[...] = jnp.zeros_like(pull_ref)
    for copy in copies:
        copy.wait()
    on_row = lax.broadcasted_iota(jnp.int32, (32, 128), 0) == lax.broadcasted_iota(
        jnp.int32, (32, 128), 1
    )

    def one_pair(pair, carry):
        for side in range(2):
            c = pair + 4 * side
            gather_operand(slot_ref, half_ref, gathered_ref.at[side], c)
            two = jnp.dot(scaled_ref[c], gathered_ref[side], preferred_element_type=F32)
            probe = turned_ref[c]
            term_two = 2.0 * two - probe
            mixture = COEFF_ZERO * probe + COEFF_ONE * one_ref[c] + COEFF_TWO * term_two
            mixture = mixture.astype(BF16)
            wide = mixture.astype(F32)
            for q in range(8):
                send_ref[
                    q, pl.ds(pl.multiple_of(16 * pair, 16), 16), 64 * side : 64 * side + 64
                ] = wide[16 * q : 16 * q + 16, :]
            rows = [row_ref[c, x] for x in range(3)]
            own = [jnp.zeros((32, 128), F32) for _ in range(3)]
            for g in range(4):
                sample = lax.dot_general(
                    mixture,
                    operand_ref[c, 512 * g : 512 * g + 512, :],
                    (((1,), (1,)), ((), ())),
                    preferred_element_type=F32,
                )
                columns = four_slots(near_ref, slot_ref, shift_ref, c, g, lane)
                pulls = pair_pulls(sample, columns, rows)
                for x in range(3):
                    own[x] = own[x] + pulls[x]
                    folded = jnp.sum(pulls[x].reshape(4, 8, 128), axis=0)
                    for t in range(4):
                        n = slot_ref[c, 4 * g + t]
                        pull_ref[n, x] = pull_ref[n, x] - jnp.where(lane // 32 == t, folded, 0.0)
            for x in range(3):
                whole = jnp.broadcast_to(jnp.sum(own[x], axis=1, keepdims=True), (32, 128))
                placed = jnp.where(on_row, whole, 0.0)
                pull_ref[8 + c, x] = pull_ref[8 + c, x] + jnp.sum(
                    placed.reshape(4, 8, 128), axis=0
                )
        return carry

    lax.fori_loop(0, 4, one_pair, 0)

    total = jnp.sum(pull_ref[0:24], axis=2).reshape(72, 128)
    total = total + pltpu.roll(total, 64, 1)
    total = total + pltpu.roll(total, 32, 1)
    total = (total * (1.0 / 512.0)).reshape(24, 3, 128)
    joined = jnp.where(lane < 32, total[:, 0], jnp.where(lane < 64, total[:, 1], total[:, 2]))
    for q in range(8):
        send_ref[q, 64:88, :] = joined


def pair_pulls(sample, columns, rows):
    part = lambda a, b: sample[32 * a : 32 * a + 32, 128 * b : 128 * b + 128]
    d, cosine, radial, inverse = bond(columns, rows)
    mixed = [SP_SIGMA * (part(0, 1 + x) - part(1 + x, 0)) for x in range(3)]
    double = [2.0 * PP_SUM * part(1 + x, 1 + x) for x in range(3)]
    cross = {}
    for a, b in ((0, 1), (0, 2), (1, 2)):
        cross[a, b] = cross[b, a] = PP_SUM * (part(1 + a, 1 + b) + part(1 + b, 1 + a))
    bent = []
    for a in range(3):
        b, c = [x for x in range(3) if x != a]
        bent.append(double[a] * cosine[a] + cross[a, b] * cosine[b] + cross[a, c] * cosine[c])
    still = SS_SIGMA * part(0, 0) + PP_PI * (part(1, 1) + part(2, 2) + part(3, 3))
    straight = mixed[0] * cosine[0] + mixed[1] * cosine[1] + mixed[2] * cosine[2]
    curved = bent[0] * cosine[0] + bent[1] * cosine[1] + bent[2] * cosine[2]
    value = still + straight + 0.5 * curved
    across = radial * inverse
    inward = radial * value * (-2.0 / BOND_SQUARE) - across * inverse * (straight + curved)
    return [across * (mixed[x] + bent[x]) + inward * d[x] for x in range(3)]


def sample_kernel(
    slot_ref, place_ref, received_ref, *refs
):
    pieces, swapped = refs[0:4], refs[4:8]
    density_ref, left_ref, sample_ref, turn_ref = refs[8:]
    rank, core = place_ref[0], place_ref[1]
    for distance in range(4):
        source = (rank - 2 * distance + 8) % 8
        for e in range(2):
            q = source if e == 0 else source + 1 - 2 * (source % 2)
            low = 64 * (2 * distance + e)
            block = received_ref[q, 0:64, :].astype(BF16)
            left_ref[0:64, low : low + 64] = block[:, 0:64]
            left_ref[64:128, low : low + 64] = block[:, 64:128]
    left = left_ref[...]
    scale = 1.0 / math.sqrt(512.0)
    sides = ((pieces, 0, 16 * core), (pieces, 1, 8), (swapped, 1, 16 - 16 * core))
    for source_refs, index, base in sides:
        for pair in range(4):
            c = 2 * pair
            right = jnp.concatenate(
                [
                    jnp.concatenate(
                        [
                            ref[e, index, 64 * n : 64 * n + 64, :]
                            for ref in source_refs
                            for e in range(2)
                        ],
                        axis=0,
                    )
                    for n in (c, c + 1)
                ],
                axis=1,
            )
            product = jnp.dot(left, right, preferred_element_type=F32) * scale
            sample_ref[base + c] = product[:, 0:128]
            sample_ref[base + c + 1] = product[:, 128:256]
    sample_ref[DEAD] = jnp.zeros((128, 128), F32)
    for c in range(8):
        for k in range(15):
            turn_ref[pl.ds(8 * k + c, 16, stride=120), :] = sample_ref[
                slot_ref[c, k], 16 * c : 16 * c + 16, :
            ]
    for r in range(16):
        density_ref[r] = turn_ref[120 * r : 120 * r + 120].astype(BF16).reshape(15, 8, 128)


def around(block, size, distance):
    return lax.ppermute(block, "space", [((i - distance) % size, i) for i in range(size)])


def along_probe(block, target):
    return lax.ppermute(block, "probe", [(i, target(i)) for i in range(8)])


def per_device(positions, probes, neighbours):
    space_count = lax.axis_size("space")
    space_rank = lax.axis_index("space")
    both = lambda block: (around(block, space_count, 1), around(block, space_count, -1))

    coords = jnp.pad(positions.transpose(1, 0, 2), ((0, 0), (0, 0), (0, 96)))
    own = jnp.concatenate([probes.reshape(512, 128), coords.reshape(24, 128)])
    before, after = both(own)
    core = space_rank % 2
    pair = jnp.stack([jnp.where(core == 0, before, after)[:512], own[:512]])
    across = along_probe(pair, lambda i: i ^ 1)

    present = neighbours >= 0
    slot = (neighbours // 8 - space_rank + 1) % space_count * 8 + neighbours % 8
    slot = jnp.pad(jnp.where(present, slot, DEAD), ((0, 0), (0, 1)), constant_values=DEAD)

    near, rows, peak = pl.pallas_call(
        spectral_kernel,
        out_shape=(
            jax.ShapeDtypeStruct((NEAR + 1, 8, 128), F32),
            jax.ShapeDtypeStruct((8, 3, 32, 128), F32),
            jax.ShapeDtypeStruct((space_count, 128), F32),
        ),
        in_specs=[SMEM] + [HBM] * 3,
        out_specs=(HBM,) * 3,
        scratch_shapes=[
            pltpu.VMEM((3, 24, 128), BF16),
            pltpu.VMEM((NEAR + 1, 8, 128), F32),
            pltpu.VMEM((8, 3, 32, 128), F32),
            pltpu.VMEM((space_count, 128), F32),
            pltpu.VMEM((4, 8, 128), F32),
            pltpu.SemaphoreType.DMA((3,)),
            pltpu.SemaphoreType.DMA((3,)),
        ],
        cost_estimate=HEAVY,
        compiler_params=params(4),
        name="spectral",
    )(slot, before, own, after)
    peaks = lax.all_to_all(peak, "space", 0, 0, tiled=True)
    peaks, pair, across = lax.optimization_barrier((peaks, pair, across))
    quad = jnp.stack([pair, across])
    pieces = [quad] + [
        along_probe(quad, lambda i, distance=distance: (i + 2 * distance) % 8)
        for distance in range(1, 4)
    ]

    scaled, operand, turned, one, half = pl.pallas_call(
        first_kernel,
        out_shape=(
            jax.ShapeDtypeStruct((8, 128, 2048), BF16),
            jax.ShapeDtypeStruct((8, 2048, 64), BF16),
            jax.ShapeDtypeStruct((8, 128, 64), F32),
            jax.ShapeDtypeStruct((8, 128, 64), F32),
            jax.ShapeDtypeStruct((4, 128, 128), BF16),
        ),
        in_specs=[SMEM] + [HBM] * 6,
        out_specs=(WHOLE,) * 5,
        scratch_shapes=[
            pltpu.VMEM((space_count, 128), F32),
            pltpu.VMEM((NEAR + 1, 8, 128), F32),
            pltpu.VMEM((8, 3, 32, 128), F32),
            pltpu.VMEM((3, 512, 128), BF16),
            pltpu.VMEM((NEAR + 1, 128, 64), BF16),
            pltpu.VMEM((4, 8, 128), F32),
            pltpu.SemaphoreType.DMA((6,)),
        ],
        cost_estimate=LIGHT,
        compiler_params=params(16),
        name="first",
    )(slot, peaks, near, rows, before, own, after)
    half_before, half_after = both(half)

    send = pl.pallas_call(
        second_kernel,
        out_shape=jax.ShapeDtypeStruct((8, 88, 128), F32),
        in_specs=[SMEM, HBM, HBM] + [WHOLE] * 7,
        out_specs=WHOLE,
        cost_estimate=LIGHT,
        scratch_shapes=[
            pltpu.VMEM((NEAR + 1, 8, 128), F32),
            pltpu.VMEM((8, 3, 32, 128), F32),
            pltpu.VMEM((NEAR + 1, 128, 64), BF16),
            pltpu.VMEM((2, 2048, 64), BF16),
            pltpu.VMEM((NEAR + 1, 3, 8, 128), F32),
            pltpu.VMEM((4, 8, 128), F32),
            pltpu.SemaphoreType.DMA((2,)),
        ],
        compiler_params=params(16),
        name="second",
    )(slot, near, rows, scaled, operand, turned, one, half_before, half, half_after)
    send, pieces = lax.optimization_barrier((send, pieces))
    swapped = [
        lax.ppermute(piece, "space", [(i, i ^ 1) for i in range(space_count)]) for piece in pieces
    ]
    received = lax.all_to_all(send, "probe", 0, 0, tiled=True)
    force = jnp.sum(received[:, 64:88], axis=0)
    from_after = around(force[0:8], space_count, -1)
    from_before = around(force[16:24], space_count, 1)

    density = pl.pallas_call(
        sample_kernel,
        out_shape=jax.ShapeDtypeStruct((16, 15, 8, 128), BF16),
        in_specs=[SMEM, SMEM] + [WHOLE] * 9,
        out_specs=WHOLE,
        scratch_shapes=[
            pltpu.VMEM((128, 512), BF16),
            pltpu.VMEM((NEAR + 1, 128, 128), F32),
            pltpu.VMEM((16 * 120, 128), F32),
        ],
        compiler_params=params(16),
        name="sample",
    )(
        slot, jnp.stack([lax.axis_index("probe"), core]), received, *pieces, *swapped
    )
    forces = force[8:16] + from_after + from_before
    forces = jnp.stack([forces[:, 32 * x : 32 * x + 32] for x in range(3)])
    return density.transpose(0, 2, 1, 3), forces.transpose(1, 0, 2)


def solution(mesh):
    in_specs = (P("space", None, None), P("space", "probe", None), P("space", None))
    out_specs = (P("probe", "space", None, None), P("space", None, None))
    return jax.shard_map(
        per_device, mesh=mesh, in_specs=in_specs, out_specs=out_specs, check_vma=False
    )
```

```python
import functools
import math

import jax
import jax.numpy as jnp
import numpy as np
from jax import lax
from jax.experimental import pallas as pl
from jax.experimental.pallas import tpu as pltpu
from jax.sharding import PartitionSpec as P

SS_SIGMA = -1.938
SP_SIGMA = 1.745
PP_SIGMA = 3.05
PP_PI = -1.075
BOND_LENGTH = 2.35
SOFT_SQUARE = 0.25
CELL_EDGE = 10.86
COEFF_ZERO = 0.6
COEFF_ONE = -0.7
COEFF_TWO = 0.45

PP_SUM = PP_SIGMA - PP_PI
BOND_SQUARE = BOND_LENGTH * BOND_LENGTH
NEAR = 24
DEAD = 24
FAR = 1000.0
SLOTS = 16
F32 = jnp.float32
BF16 = jnp.bfloat16
WHOLE = pl.BlockSpec()
SMEM = pl.BlockSpec(memory_space=pltpu.SMEM)
HBM = pl.BlockSpec(memory_space=pltpu.MemorySpace.HBM)
HEAVY = pl.CostEstimate(flops=0, transcendentals=0, bytes_accessed=60_000_000)
LIGHT = pl.CostEstimate(flops=0, transcendentals=0, bytes_accessed=0)


def params(mebibytes):
    return pltpu.CompilerParams(vmem_limit_bytes=mebibytes * 1024 * 1024)


def slot_offsets():
    half = CELL_EDGE / 2.0
    table = [[0.0, 0.0, 0.0]]
    for sign_x in (-1.0, 1.0):
        for sign_y in (-1.0, 1.0):
            for sign_z in (-1.0, 1.0):
                table.append([sign_x * half, sign_y * half, sign_z * half])
    for axis_pick in range(3):
        for sign_a in (1.0, -1.0):
            entry = [0.0, 0.0, 0.0]
            entry[axis_pick] = sign_a * CELL_EDGE
            table.append(entry)
    table.append([0.0, 0.0, 0.0])
    return np.array(table, dtype=np.float32)


def fill_shifts(shift_ref):
    lane = lanes()
    table = slot_offsets()
    for g in range(4):
        for x in range(3):
            v = [float(table[4 * g + t, x]) for t in range(4)]
            shift_ref[g, x : x + 1, :] = jnp.where(
                lane < 32, v[0], jnp.where(lane < 64, v[1], jnp.where(lane < 96, v[2], v[3]))
            )


def lanes():
    return lax.broadcasted_iota(jnp.int32, (1, 128), 1)


def bond(columns, rows):
    d = [columns[x : x + 1, :] - rows[x] for x in range(3)]
    rho_square = d[0] * d[0] + d[1] * d[1] + d[2] * d[2] + SOFT_SQUARE
    inverse = lax.rsqrt(rho_square)
    radial = jnp.exp(1.0 - rho_square / BOND_SQUARE)
    return d, [v * inverse for v in d], radial, inverse


def four_slots(near_ref, slot_ref, shift_ref, c, g, lane):
    v = [near_ref[slot_ref[c, 4 * g + t]] for t in range(4)]
    joined = jnp.where(
        lane < 32, v[0], jnp.where(lane < 64, v[1], jnp.where(lane < 96, v[2], v[3]))
    )
    return joined + shift_ref[g]


def spectral_kernel(
    slot_ref, before_ref, own_ref, after_ref, near_out, row_out, peak_out,
    coord_ref, near_ref, row_ref, peak_ref, shift_ref, in_sem, out_sem,
):
    copies = [
        pltpu.make_async_copy(ref.at[512:536], coord_ref.at[part], in_sem.at[part])
        for part, ref in enumerate((before_ref, own_ref, after_ref))
    ]
    for copy in copies:
        copy.start()
    fill_shifts(shift_ref)
    for part in range(3):
        copies[part].wait()
        for x in range(3):
            coords = coord_ref[part, 8 * x : 8 * x + 8, 0:32].astype(F32)
            wide = jnp.concatenate([coords] * 4, axis=1)
            for n in range(8):
                near_ref[8 * part + n, x : x + 1, :] = wide[n : n + 1, :]
            if part == 1:
                upright = wide.T
                for c in range(8):
                    row_ref[c, x] = jnp.broadcast_to(upright[0:32, c : c + 1], (32, 128))
    near_ref[DEAD] = jnp.full((8, 128), FAR, F32)
    kept = [
        pltpu.make_async_copy(near_ref, near_out, out_sem.at[0]),
        pltpu.make_async_copy(row_ref, row_out, out_sem.at[1]),
    ]
    for copy in kept:
        copy.start()
    lane = lanes()

    def one_cluster(c, peak):
        rows = [row_ref[c, x] for x in range(3)]
        sums = [jnp.zeros((32, 128), F32) for _ in range(4)]
        for g in range(4):
            columns = four_slots(near_ref, slot_ref, shift_ref, c, g, lane)
            _, cosine, radial, _ = bond(columns, rows)
            size = [jnp.abs(v) for v in cosine]
            sums[0] += (-SS_SIGMA + SP_SIGMA * (size[0] + size[1] + size[2])) * radial
            cross = {}
            for a in range(3):
                for b in range(a, 3):
                    product = cosine[a] * cosine[b] * PP_SUM
                    cross[a, b] = cross[b, a] = jnp.abs(product + PP_PI if a == b else product)
            for a in range(3):
                sums[1 + a] += (
                    SP_SIGMA * size[a] + cross[a, 0] + cross[a, 1] + cross[a, 2]
                ) * radial
        for v in sums:
            peak = jnp.maximum(peak, jnp.sum(v, axis=1, keepdims=True))
        return peak

    peak = lax.fori_loop(0, 8, one_cluster, jnp.zeros((32, 1), F32))
    peak_ref[...] = jnp.broadcast_to(jnp.max(peak), peak_ref.shape)
    copy = pltpu.make_async_copy(peak_ref, peak_out, out_sem.at[2])
    copy.start()
    copy.wait()
    for copy in kept:
        copy.wait()


def gather_operand(slot_ref, source_ref, target_ref, c):
    for k in range(SLOTS):
        n = slot_ref[c, k]
        for b in range(4):
            low = 512 * (k // 4) + 128 * b + 32 * (k % 4)
            target_ref[low : low + 32, :] = source_ref[n, 32 * b : 32 * b + 32, :]


def prepare_kernel(
    slot_ref, before_ref, own_ref, after_ref, probe_ref, turned_ref, table_ref,
    flat_ref, hot_ref, sem,
):
    pieces = [
        pltpu.make_async_copy(ref.at[0:512], flat_ref.at[part], sem.at[part])
        for part, ref in enumerate((before_ref, own_ref, after_ref))
    ]
    for copy in pieces:
        copy.start()
    lane = lanes()
    for t in range(4):
        for c in range(8):
            for g in range(4):
                row = 32 * t + 4 * c + g
                hot_ref[row : row + 1, :] = (lane == slot_ref[c, 4 * g + t]).astype(F32)
    table_ref[...] = hot_ref[...].T[0:NEAR, :]
    probe_ref[DEAD] = jnp.zeros((128, 64), BF16)
    for part in range(3):
        pieces[part].wait()
        for c in range(8):
            turned = flat_ref[part, 64 * c : 64 * c + 64].astype(F32).T
            if part == 1:
                turned_ref[c] = turned
            probe_ref[8 * part + c] = turned.astype(BF16)


def first_kernel(
    slot_ref, peak_in, near_in, row_in, probe_ref,
    scaled_ref, operand_ref, one_ref, half_ref, peak_ref, near_ref, row_ref, shift_ref, sem,
):
    copies = [
        pltpu.make_async_copy(peak_in, peak_ref, sem.at[0]),
        pltpu.make_async_copy(near_in, near_ref, sem.at[1]),
        pltpu.make_async_copy(row_in, row_ref, sem.at[2]),
    ]
    for copy in copies:
        copy.start()
    fill_shifts(shift_ref)
    lane = lanes()
    for copy in copies:
        copy.wait()
    inverse_peak = 1.0 / jnp.max(peak_ref[...])

    def one_pair(pair, carry):
        for side in range(2):
            c = pair + 4 * side
            rows = [row_ref[c, x] for x in range(3)]
            gather_operand(slot_ref, probe_ref, operand_ref.at[c], c)
            for g in range(4):
                columns = four_slots(near_ref, slot_ref, shift_ref, c, g, lane)
                _, cosine, radial, _ = bond(columns, rows)
                radial = radial * inverse_peak
                place = functools.partial(block_at, scaled_ref, c, g)
                place(0, 0, SS_SIGMA * radial)
                sp = SP_SIGMA * radial
                pp = PP_SUM * radial
                pi = PP_PI * radial
                for a in range(3):
                    wave = cosine[a] * sp
                    place(0, a + 1, wave)
                    place(a + 1, 0, -wave)
                    leaning = cosine[a] * pp
                    for b in range(a, 3):
                        value = leaning * cosine[b]
                        if a == b:
                            place(a + 1, a + 1, value + pi)
                        else:
                            place(a + 1, b + 1, value)
                            place(b + 1, a + 1, value)
            one = jnp.dot(scaled_ref[c], operand_ref[c], preferred_element_type=F32)
            one_ref[c] = one
            half_ref[pair, :, 64 * side : 64 * side + 64] = one.astype(BF16)
        return carry

    lax.fori_loop(0, 4, one_pair, 0)


def block_at(scaled_ref, c, g, a, b, value):
    low = 512 * g + 128 * b
    scaled_ref[c, 32 * a : 32 * a + 32, low : low + 128] = value.astype(BF16)


def second_kernel(
    slot_ref, near_in, row_in, scaled_ref, operand_ref, turned_ref, one_ref,
    before_ref, own_ref, after_ref, table_ref, send_ref,
    near_ref, row_ref, half_ref, gathered_ref, near_pull_ref, own_pull_ref, shift_ref, sem,
):
    copies = [
        pltpu.make_async_copy(near_in, near_ref, sem.at[0]),
        pltpu.make_async_copy(row_in, row_ref, sem.at[1]),
    ]
    for copy in copies:
        copy.start()
    fill_shifts(shift_ref)
    lane = lanes()
    for part, ref in enumerate((before_ref, own_ref, after_ref)):
        for pair in range(4):
            half_ref[8 * part + pair] = ref[pair, :, 0:64]
            half_ref[8 * part + pair + 4] = ref[pair, :, 64:128]
    half_ref[DEAD] = jnp.zeros((128, 64), BF16)
    for copy in copies:
        copy.wait()
    on_row = lax.broadcasted_iota(jnp.int32, (32, 128), 0) == lax.broadcasted_iota(
        jnp.int32, (32, 128), 1
    )

    def one_pair(pair, carry):
        for side in range(2):
            c = pair + 4 * side
            gather_operand(slot_ref, half_ref, gathered_ref.at[side], c)
            two = jnp.dot(scaled_ref[c], gathered_ref[side], preferred_element_type=F32)
            probe = turned_ref[c]
            term_two = 2.0 * two - probe
            mixture = COEFF_ZERO * probe + COEFF_ONE * one_ref[c] + COEFF_TWO * term_two
            mixture = mixture.astype(BF16)
            wide = mixture.astype(F32)
            for q in range(8):
                send_ref[
                    q, pl.ds(pl.multiple_of(16 * pair, 16), 16), 64 * side : 64 * side + 64
                ] = wide[16 * q : 16 * q + 16, :]
            rows = [row_ref[c, x] for x in range(3)]
            own = [jnp.zeros((32, 128), F32) for _ in range(3)]
            for g in range(4):
                sample = lax.dot_general(
                    mixture,
                    operand_ref[c, 512 * g : 512 * g + 512, :],
                    (((1,), (1,)), ((), ())),
                    preferred_element_type=F32,
                )
                columns = four_slots(near_ref, slot_ref, shift_ref, c, g, lane)
                pulls = pair_pulls(sample, columns, rows)
                for x in range(3):
                    own[x] = own[x] + pulls[x]
                    near_pull_ref[x, pl.ds(4 * c + g, 1), :] = jnp.sum(
                        pulls[x], axis=0, keepdims=True
                    )
            for x in range(3):
                whole = jnp.broadcast_to(jnp.sum(own[x], axis=1, keepdims=True), (32, 128))
                own_pull_ref[x, pl.ds(c, 1), :] = jnp.sum(
                    jnp.where(on_row, whole, 0.0), axis=0, keepdims=True
                )
        return carry

    lax.fori_loop(0, 4, one_pair, 0)

    stacked = jnp.concatenate(
        [
            jnp.concatenate(
                [jnp.where(lane // 32 == t, near_pull_ref[x], 0.0) for x in range(3)], axis=1
            )
            for t in range(4)
        ],
        axis=0,
    )
    gathered = jnp.dot(
        table_ref[...], stacked, precision=lax.Precision.HIGHEST, preferred_element_type=F32
    )
    total = [-gathered[:, 128 * x : 128 * x + 128] for x in range(3)]
    nothing = jnp.zeros((8, 128), F32)
    for x in range(3):
        v = total[x] + jnp.concatenate([nothing, own_pull_ref[x], nothing], axis=0)
        v = v + pltpu.roll(v, 64, 1)
        v = v + pltpu.roll(v, 32, 1)
        total[x] = v * (1.0 / 512.0)
    joined = jnp.where(lane < 32, total[0], jnp.where(lane < 64, total[1], total[2]))
    for q in range(8):
        send_ref[q, 64:88, :] = joined


def pair_pulls(sample, columns, rows):
    part = lambda a, b: sample[32 * a : 32 * a + 32, 128 * b : 128 * b + 128]
    d, cosine, radial, inverse = bond(columns, rows)
    mixed = [SP_SIGMA * (part(0, 1 + x) - part(1 + x, 0)) for x in range(3)]
    double = [2.0 * PP_SUM * part(1 + x, 1 + x) for x in range(3)]
    cross = {}
    for a, b in ((0, 1), (0, 2), (1, 2)):
        cross[a, b] = cross[b, a] = PP_SUM * (part(1 + a, 1 + b) + part(1 + b, 1 + a))
    bent = []
    for a in range(3):
        b, c = [x for x in range(3) if x != a]
        bent.append(double[a] * cosine[a] + cross[a, b] * cosine[b] + cross[a, c] * cosine[c])
    still = SS_SIGMA * part(0, 0) + PP_PI * (part(1, 1) + part(2, 2) + part(3, 3))
    straight = mixed[0] * cosine[0] + mixed[1] * cosine[1] + mixed[2] * cosine[2]
    curved = bent[0] * cosine[0] + bent[1] * cosine[1] + bent[2] * cosine[2]
    value = still + straight + 0.5 * curved
    across = radial * inverse
    inward = radial * value * (-2.0 / BOND_SQUARE) - across * inverse * (straight + curved)
    return [across * (mixed[x] + bent[x]) + inward * d[x] for x in range(3)]


def sample_kernel(
    slot_ref, place_ref, received_ref, *refs
):
    pieces, swapped = refs[0:4], refs[4:8]
    density_ref, left_ref, sample_ref, turn_ref = refs[8:]
    rank, core = place_ref[0], place_ref[1]
    for distance in range(4):
        source = (rank - 2 * distance + 8) % 8
        for e in range(2):
            q = source if e == 0 else source + 1 - 2 * (source % 2)
            low = 64 * (2 * distance + e)
            block = received_ref[q, 0:64, :].astype(BF16)
            left_ref[0:64, low : low + 64] = block[:, 0:64]
            left_ref[64:128, low : low + 64] = block[:, 64:128]
    left = left_ref[...]
    scale = 1.0 / math.sqrt(512.0)
    sides = ((pieces, 0, 16 * core), (pieces, 1, 8), (swapped, 1, 16 - 16 * core))
    for source_refs, index, base in sides:
        for pair in range(4):
            c = 2 * pair
            right = jnp.concatenate(
                [
                    jnp.concatenate(
                        [
                            ref[e, index, 64 * n : 64 * n + 64, :]
                            for ref in source_refs
                            for e in range(2)
                        ],
                        axis=0,
                    )
                    for n in (c, c + 1)
                ],
                axis=1,
            )
            product = jnp.dot(left, right, preferred_element_type=F32) * scale
            sample_ref[base + c] = product[:, 0:128]
            sample_ref[base + c + 1] = product[:, 128:256]
    sample_ref[DEAD] = jnp.zeros((128, 128), F32)
    for c in range(8):
        for k in range(15):
            turn_ref[pl.ds(8 * k + c, 16, stride=120), :] = sample_ref[
                slot_ref[c, k], 16 * c : 16 * c + 16, :
            ]
    for r in range(16):
        density_ref[r] = turn_ref[120 * r : 120 * r + 120].astype(BF16).reshape(15, 8, 128)


def around(block, size, distance):
    return lax.ppermute(block, "space", [((i - distance) % size, i) for i in range(size)])


def along_probe(block, target):
    return lax.ppermute(block, "probe", [(i, target(i)) for i in range(8)])


def per_device(positions, probes, neighbours):
    space_count = lax.axis_size("space")
    space_rank = lax.axis_index("space")
    both = lambda block: (around(block, space_count, 1), around(block, space_count, -1))

    coords = jnp.pad(positions.transpose(1, 0, 2), ((0, 0), (0, 0), (0, 96)))
    own = jnp.concatenate([probes.reshape(512, 128), coords.reshape(24, 128)])
    before, after = both(own)
    core = space_rank % 2
    present = neighbours >= 0
    slot = (neighbours // 8 - space_rank + 1) % space_count * 8 + neighbours % 8
    slot = jnp.pad(jnp.where(present, slot, DEAD), ((0, 0), (0, 1)), constant_values=DEAD)

    near, rows, peak = pl.pallas_call(
        spectral_kernel,
        out_shape=(
            jax.ShapeDtypeStruct((NEAR + 1, 8, 128), F32),
            jax.ShapeDtypeStruct((8, 3, 32, 128), F32),
            jax.ShapeDtypeStruct((space_count, 128), F32),
        ),
        in_specs=[SMEM] + [HBM] * 3,
        out_specs=(HBM,) * 3,
        scratch_shapes=[
            pltpu.VMEM((3, 24, 128), BF16),
            pltpu.VMEM((NEAR + 1, 8, 128), F32),
            pltpu.VMEM((8, 3, 32, 128), F32),
            pltpu.VMEM((space_count, 128), F32),
            pltpu.VMEM((4, 8, 128), F32),
            pltpu.SemaphoreType.DMA((3,)),
            pltpu.SemaphoreType.DMA((3,)),
        ],
        cost_estimate=HEAVY,
        compiler_params=params(4),
        name="spectral",
    )(slot, before, own, after)
    peak, held = lax.optimization_barrier((peak, (before, own, after)))
    peaks = lax.all_to_all(peak, "space", 0, 0, tiled=True)
    probe_turned, turned, table = pl.pallas_call(
        prepare_kernel,
        out_shape=(
            jax.ShapeDtypeStruct((NEAR + 1, 128, 64), BF16),
            jax.ShapeDtypeStruct((8, 128, 64), F32),
            jax.ShapeDtypeStruct((NEAR, 128), F32),
        ),
        in_specs=[SMEM] + [HBM] * 3,
        out_specs=(WHOLE,) * 3,
        scratch_shapes=[
            pltpu.VMEM((3, 512, 128), BF16),
            pltpu.VMEM((128, 128), F32),
            pltpu.SemaphoreType.DMA((3,)),
        ],
        compiler_params=params(4),
        name="prepare",
    )(slot, *held)
    pair = jnp.stack([jnp.where(core == 0, held[0], held[2])[:512], held[1][:512]])
    peaks, pair, probe_turned = lax.optimization_barrier((peaks, pair, probe_turned))
    across = along_probe(pair, lambda i: i ^ 1)
    scaled, operand, one, half = pl.pallas_call(
        first_kernel,
        out_shape=(
            jax.ShapeDtypeStruct((8, 128, 2048), BF16),
            jax.ShapeDtypeStruct((8, 2048, 64), BF16),
            jax.ShapeDtypeStruct((8, 128, 64), F32),
            jax.ShapeDtypeStruct((4, 128, 128), BF16),
        ),
        in_specs=[SMEM] + [HBM] * 3 + [WHOLE],
        out_specs=(WHOLE,) * 4,
        scratch_shapes=[
            pltpu.VMEM((space_count, 128), F32),
            pltpu.VMEM((NEAR + 1, 8, 128), F32),
            pltpu.VMEM((8, 3, 32, 128), F32),
            pltpu.VMEM((4, 8, 128), F32),
            pltpu.SemaphoreType.DMA((3,)),
        ],
        cost_estimate=LIGHT,
        compiler_params=params(16),
        name="first",
    )(slot, peaks, near, rows, probe_turned)
    half_before, half_after = both(half)
    half, pair, across = lax.optimization_barrier((half, pair, across))
    quad = jnp.stack([pair, across])
    pieces = [quad] + [
        along_probe(quad, lambda i, distance=distance: (i + 2 * distance) % 8)
        for distance in range(1, 4)
    ]
    send = pl.pallas_call(
        second_kernel,
        out_shape=jax.ShapeDtypeStruct((8, 88, 128), F32),
        in_specs=[SMEM, HBM, HBM] + [WHOLE] * 8,
        out_specs=WHOLE,
        cost_estimate=LIGHT,
        scratch_shapes=[
            pltpu.VMEM((NEAR + 1, 8, 128), F32),
            pltpu.VMEM((8, 3, 32, 128), F32),
            pltpu.VMEM((NEAR + 1, 128, 64), BF16),
            pltpu.VMEM((2, 2048, 64), BF16),
            pltpu.VMEM((3, 32, 128), F32),
            pltpu.VMEM((3, 8, 128), F32),
            pltpu.VMEM((4, 8, 128), F32),
            pltpu.SemaphoreType.DMA((2,)),
        ],
        compiler_params=params(16),
        name="second",
    )(slot, near, rows, scaled, operand, turned, one, half_before, half, half_after, table)
    send, pieces = lax.optimization_barrier((send, pieces))
    swapped = [
        lax.ppermute(piece, "space", [(i, i ^ 1) for i in range(space_count)]) for piece in pieces
    ]
    received = lax.all_to_all(send, "probe", 0, 0, tiled=True)
    force = jnp.sum(received[:, 64:88], axis=0)
    from_after = around(force[0:8], space_count, -1)
    from_before = around(force[16:24], space_count, 1)

    density = pl.pallas_call(
        sample_kernel,
        out_shape=jax.ShapeDtypeStruct((16, 15, 8, 128), BF16),
        in_specs=[SMEM, SMEM] + [WHOLE] * 9,
        out_specs=WHOLE,
        scratch_shapes=[
            pltpu.VMEM((128, 512), BF16),
            pltpu.VMEM((NEAR + 1, 128, 128), F32),
            pltpu.VMEM((16 * 120, 128), F32),
        ],
        compiler_params=params(16),
        name="sample",
    )(
        slot, jnp.stack([lax.axis_index("probe"), core]), received, *pieces, *swapped
    )
    forces = force[8:16] + from_after + from_before
    forces = jnp.stack([forces[:, 32 * x : 32 * x + 32] for x in range(3)])
    return density.transpose(0, 2, 1, 3), forces.transpose(1, 0, 2)


def solution(mesh):
    in_specs = (P("space", None, None), P("space", "probe", None), P("space", None))
    out_specs = (P("probe", "space", None, None), P("space", None, None))
    return jax.shard_map(
        per_device, mesh=mesh, in_specs=in_specs, out_specs=out_specs, check_vma=False
    )
```

```python
import functools
import math

import jax
import jax.numpy as jnp
import numpy as np
from jax import lax
from jax.experimental import pallas as pl
from jax.experimental.pallas import tpu as pltpu
from jax.sharding import PartitionSpec as P

SS_SIGMA = -1.938
SP_SIGMA = 1.745
PP_SIGMA = 3.05
PP_PI = -1.075
BOND_LENGTH = 2.35
SOFT_SQUARE = 0.25
CELL_EDGE = 10.86
COEFF_ZERO = 0.6
COEFF_ONE = -0.7
COEFF_TWO = 0.45

PP_SUM = PP_SIGMA - PP_PI
BOND_SQUARE = BOND_LENGTH * BOND_LENGTH
NEAR = 24
DEAD = 24
FAR = 1000.0
SLOTS = 16
F32 = jnp.float32
BF16 = jnp.bfloat16
WHOLE = pl.BlockSpec()
SMEM = pl.BlockSpec(memory_space=pltpu.SMEM)
HEAVY = pl.CostEstimate(flops=0, transcendentals=0, bytes_accessed=60_000_000)
LIGHT = pl.CostEstimate(flops=0, transcendentals=0, bytes_accessed=0)


def params(mebibytes):
    return pltpu.CompilerParams(vmem_limit_bytes=mebibytes * 1024 * 1024)


def slot_offsets():
    half = CELL_EDGE / 2.0
    table = [[0.0, 0.0, 0.0]]
    for sign_x in (-1.0, 1.0):
        for sign_y in (-1.0, 1.0):
            for sign_z in (-1.0, 1.0):
                table.append([sign_x * half, sign_y * half, sign_z * half])
    for axis_pick in range(3):
        for sign_a in (1.0, -1.0):
            entry = [0.0, 0.0, 0.0]
            entry[axis_pick] = sign_a * CELL_EDGE
            table.append(entry)
    table.append([0.0, 0.0, 0.0])
    return np.array(table, dtype=np.float32)


def fill_shifts(shift_ref):
    lane = lanes()
    table = slot_offsets()
    for g in range(4):
        for x in range(3):
            v = [float(table[4 * g + t, x]) for t in range(4)]
            shift_ref[g, x : x + 1, :] = jnp.where(
                lane < 32, v[0], jnp.where(lane < 64, v[1], jnp.where(lane < 96, v[2], v[3]))
            )


def lanes():
    return lax.broadcasted_iota(jnp.int32, (1, 128), 1)


def bond(columns, rows):
    d = [columns[x : x + 1, :] - rows[x] for x in range(3)]
    rho_square = d[0] * d[0] + d[1] * d[1] + d[2] * d[2] + SOFT_SQUARE
    inverse = lax.rsqrt(rho_square)
    radial = jnp.exp(1.0 - rho_square / BOND_SQUARE)
    return d, [v * inverse for v in d], radial, inverse


def four_slots(near_ref, slot_ref, shift_ref, c, g, lane):
    v = [near_ref[slot_ref[c, 4 * g + t]] for t in range(4)]
    joined = jnp.where(
        lane < 32, v[0], jnp.where(lane < 64, v[1], jnp.where(lane < 96, v[2], v[3]))
    )
    return joined + shift_ref[g]


def spectral_kernel(
    slot_ref, before_ref, own_ref, after_ref, near_ref, row_ref, peak_ref, shift_ref
):
    fill_shifts(shift_ref)
    for part, ref in enumerate((before_ref, own_ref, after_ref)):
        for x in range(3):
            coords = ref[512 + 8 * x : 520 + 8 * x, 0:32].astype(F32)
            wide = jnp.concatenate([coords] * 4, axis=1)
            for n in range(8):
                near_ref[8 * part + n, x : x + 1, :] = wide[n : n + 1, :]
            if part == 1:
                upright = wide.T
                for c in range(8):
                    row_ref[c, x] = jnp.broadcast_to(upright[0:32, c : c + 1], (32, 128))
    near_ref[DEAD] = jnp.full((8, 128), FAR, F32)
    lane = lanes()

    def one_cluster(c, peak):
        rows = [row_ref[c, x] for x in range(3)]
        sums = [jnp.zeros((32, 128), F32) for _ in range(4)]
        for g in range(4):
            columns = four_slots(near_ref, slot_ref, shift_ref, c, g, lane)
            _, cosine, radial, _ = bond(columns, rows)
            size = [jnp.abs(v) for v in cosine]
            sums[0] += (-SS_SIGMA + SP_SIGMA * (size[0] + size[1] + size[2])) * radial
            cross = {}
            for a in range(3):
                for b in range(a, 3):
                    product = cosine[a] * cosine[b] * PP_SUM
                    cross[a, b] = cross[b, a] = jnp.abs(product + PP_PI if a == b else product)
            for a in range(3):
                sums[1 + a] += (
                    SP_SIGMA * size[a] + cross[a, 0] + cross[a, 1] + cross[a, 2]
                ) * radial
        for v in sums:
            peak = jnp.maximum(peak, jnp.sum(v, axis=1, keepdims=True))
        return peak

    peak = jnp.zeros((32, 1), F32)
    for c in range(8):
        peak = one_cluster(c, peak)
    peak_ref[...] = jnp.broadcast_to(jnp.max(peak), peak_ref.shape)


def gather_operand(slot_ref, source_ref, target_ref, c):
    for k in range(SLOTS):
        n = slot_ref[c, k]
        for b in range(4):
            low = 512 * (k // 4) + 128 * b + 32 * (k % 4)
            target_ref[low : low + 32, :] = source_ref[n, 32 * b : 32 * b + 32, :]


def prepare_kernel(
    slot_ref, before_ref, own_ref, after_ref, probe_ref, table_ref,
    hot_ref,
):
    lane = lanes()
    for t in range(4):
        for c in range(8):
            for g in range(4):
                row = 32 * t + 4 * c + g
                hot_ref[row : row + 1, :] = (lane == slot_ref[c, 4 * g + t]).astype(F32)
    table_ref[...] = hot_ref[...].T[0:NEAR, :]
    probe_ref[DEAD] = jnp.zeros((128, 64), BF16)
    for part, ref in enumerate((before_ref, own_ref, after_ref)):
        for c in range(8):
            turned = ref[64 * c : 64 * c + 64].astype(F32).T
            probe_ref[8 * part + c] = turned.astype(BF16)


def first_kernel(
    slot_ref, peak_ref, near_ref, row_ref, probe_ref,
    scaled_ref, operand_ref, one_ref, half_ref, shift_ref,
):
    fill_shifts(shift_ref)
    lane = lanes()
    inverse_peak = 1.0 / jnp.max(peak_ref[...])

    def one_pair(pair):
        for side in range(2):
            c = pair + 4 * side
            rows = [row_ref[c, x] for x in range(3)]
            gather_operand(slot_ref, probe_ref, operand_ref.at[c], c)
            for g in range(4):
                columns = four_slots(near_ref, slot_ref, shift_ref, c, g, lane)
                _, cosine, radial, _ = bond(columns, rows)
                radial = radial * inverse_peak
                place = functools.partial(block_at, scaled_ref, c, g)
                place(0, 0, SS_SIGMA * radial)
                sp = SP_SIGMA * radial
                pp = PP_SUM * radial
                pi = PP_PI * radial
                for a in range(3):
                    wave = cosine[a] * sp
                    place(0, a + 1, wave)
                    place(a + 1, 0, -wave)
                    leaning = cosine[a] * pp
                    for b in range(a, 3):
                        value = leaning * cosine[b]
                        if a == b:
                            place(a + 1, a + 1, value + pi)
                        else:
                            place(a + 1, b + 1, value)
                            place(b + 1, a + 1, value)
            one = jnp.dot(scaled_ref[c], operand_ref[c], preferred_element_type=F32)
            one_ref[c] = one
            half_ref[pair, :, 64 * side : 64 * side + 64] = one.astype(BF16)

    for pair in range(4):
        one_pair(pair)


def block_at(scaled_ref, c, g, a, b, value):
    low = 512 * g + 128 * b
    scaled_ref[c, 32 * a : 32 * a + 32, low : low + 128] = value.astype(BF16)


def second_kernel(
    slot_ref, near_ref, row_ref, scaled_ref, operand_ref, probe_ref, one_ref,
    before_ref, own_ref, after_ref, table_ref, send_ref,
    half_ref, gathered_ref, near_pull_ref, own_pull_ref, shift_ref,
):
    fill_shifts(shift_ref)
    lane = lanes()
    for part, ref in enumerate((before_ref, own_ref, after_ref)):
        for pair in range(4):
            half_ref[8 * part + pair] = ref[pair, :, 0:64]
            half_ref[8 * part + pair + 4] = ref[pair, :, 64:128]
    half_ref[DEAD] = jnp.zeros((128, 64), BF16)
    on_row = lax.broadcasted_iota(jnp.int32, (32, 128), 0) == lax.broadcasted_iota(
        jnp.int32, (32, 128), 1
    )

    def one_pair(pair):
        for side in range(2):
            c = pair + 4 * side
            gather_operand(slot_ref, half_ref, gathered_ref.at[side], c)
            two = jnp.dot(scaled_ref[c], gathered_ref[side], preferred_element_type=F32)
            probe = probe_ref[8 + c].astype(F32)
            term_two = 2.0 * two - probe
            mixture = COEFF_ZERO * probe + COEFF_ONE * one_ref[c] + COEFF_TWO * term_two
            mixture = mixture.astype(BF16)
            wide = mixture.astype(F32)
            for q in range(8):
                send_ref[
                    q, 16 * pair : 16 * pair + 16, 64 * side : 64 * side + 64
                ] = wide[16 * q : 16 * q + 16, :]
            rows = [row_ref[c, x] for x in range(3)]
            own = [jnp.zeros((32, 128), F32) for _ in range(3)]
            for g in range(4):
                sample = lax.dot_general(
                    mixture,
                    operand_ref[c, 512 * g : 512 * g + 512, :],
                    (((1,), (1,)), ((), ())),
                    preferred_element_type=F32,
                )
                columns = four_slots(near_ref, slot_ref, shift_ref, c, g, lane)
                pulls = pair_pulls(sample, columns, rows)
                for x in range(3):
                    own[x] = own[x] + pulls[x]
                    near_pull_ref[x, 4 * c + g : 4 * c + g + 1, :] = jnp.sum(
                        pulls[x], axis=0, keepdims=True
                    )
            for x in range(3):
                whole = jnp.broadcast_to(jnp.sum(own[x], axis=1, keepdims=True), (32, 128))
                own_pull_ref[x, c : c + 1, :] = jnp.sum(
                    jnp.where(on_row, whole, 0.0), axis=0, keepdims=True
                )

    for pair in range(4):
        one_pair(pair)

    stacked = jnp.concatenate(
        [
            jnp.concatenate(
                [jnp.where(lane // 32 == t, near_pull_ref[x], 0.0) for x in range(3)], axis=1
            )
            for t in range(4)
        ],
        axis=0,
    )
    gathered = jnp.dot(
        table_ref[...], stacked, precision=lax.Precision.HIGHEST, preferred_element_type=F32
    )
    total = [-gathered[:, 128 * x : 128 * x + 128] for x in range(3)]
    nothing = jnp.zeros((8, 128), F32)
    for x in range(3):
        v = total[x] + jnp.concatenate([nothing, own_pull_ref[x], nothing], axis=0)
        v = v + pltpu.roll(v, 64, 1)
        v = v + pltpu.roll(v, 32, 1)
        total[x] = v * (1.0 / 512.0)
    joined = jnp.where(lane < 32, total[0], jnp.where(lane < 64, total[1], total[2]))
    for q in range(8):
        send_ref[q, 64:88, :] = joined


def pair_pulls(sample, columns, rows):
    part = lambda a, b: sample[32 * a : 32 * a + 32, 128 * b : 128 * b + 128]
    d, cosine, radial, inverse = bond(columns, rows)
    mixed = [SP_SIGMA * (part(0, 1 + x) - part(1 + x, 0)) for x in range(3)]
    double = [2.0 * PP_SUM * part(1 + x, 1 + x) for x in range(3)]
    cross = {}
    for a, b in ((0, 1), (0, 2), (1, 2)):
        cross[a, b] = cross[b, a] = PP_SUM * (part(1 + a, 1 + b) + part(1 + b, 1 + a))
    bent = []
    for a in range(3):
        b, c = [x for x in range(3) if x != a]
        bent.append(double[a] * cosine[a] + cross[a, b] * cosine[b] + cross[a, c] * cosine[c])
    still = SS_SIGMA * part(0, 0) + PP_PI * (part(1, 1) + part(2, 2) + part(3, 3))
    straight = mixed[0] * cosine[0] + mixed[1] * cosine[1] + mixed[2] * cosine[2]
    curved = bent[0] * cosine[0] + bent[1] * cosine[1] + bent[2] * cosine[2]
    value = still + straight + 0.5 * curved
    across = radial * inverse
    inward = radial * value * (-2.0 / BOND_SQUARE) - across * inverse * (straight + curved)
    return [across * (mixed[x] + bent[x]) + inward * d[x] for x in range(3)]


def sample_kernel(
    slot_ref, place_ref, received_ref, *refs
):
    pieces, swapped = refs[0:4], refs[4:8]
    density_ref, left_ref, sample_ref, turn_ref = refs[8:]
    rank, core = place_ref[0], place_ref[1]
    for distance in range(4):
        source = (rank - 2 * distance + 8) % 8
        for e in range(2):
            q = source if e == 0 else source + 1 - 2 * (source % 2)
            low = 64 * (2 * distance + e)
            block = received_ref[q, 0:64, :].astype(BF16)
            left_ref[0:64, low : low + 64] = block[:, 0:64]
            left_ref[64:128, low : low + 64] = block[:, 64:128]
    left = left_ref[...]
    scale = 1.0 / math.sqrt(512.0)
    sides = ((pieces, 0, 16 * core), (pieces, 1, 8), (swapped, 1, 16 - 16 * core))
    for source_refs, index, base in sides:
        for pair in range(4):
            c = 2 * pair
            right = jnp.concatenate(
                [
                    jnp.concatenate(
                        [
                            ref[e, index, 64 * n : 64 * n + 64, :]
                            for ref in source_refs
                            for e in range(2)
                        ],
                        axis=0,
                    )
                    for n in (c, c + 1)
                ],
                axis=1,
            )
            product = jnp.dot(left, right, preferred_element_type=F32) * scale
            sample_ref[base + c] = product[:, 0:128]
            sample_ref[base + c + 1] = product[:, 128:256]
    sample_ref[DEAD] = jnp.zeros((128, 128), F32)
    for c in range(8):
        for k in range(15):
            turn_ref[pl.ds(8 * k + c, 16, stride=120), :] = sample_ref[
                slot_ref[c, k], 16 * c : 16 * c + 16, :
            ]
    for r in range(16):
        density_ref[r] = turn_ref[120 * r : 120 * r + 120].astype(BF16).reshape(15, 8, 128)


def around(block, size, distance):
    return lax.ppermute(block, "space", [((i - distance) % size, i) for i in range(size)])


def along_probe(block, target):
    return lax.ppermute(block, "probe", [(i, target(i)) for i in range(8)])


def per_device(positions, probes, neighbours):
    space_count = lax.axis_size("space")
    space_rank = lax.axis_index("space")
    both = lambda block: (around(block, space_count, 1), around(block, space_count, -1))

    coords = jnp.pad(positions.transpose(1, 0, 2), ((0, 0), (0, 0), (0, 96)))
    own = jnp.concatenate([probes.reshape(512, 128), coords.reshape(24, 128)])
    before, after = both(own)
    core = space_rank % 2
    pair = jnp.stack([jnp.where(core == 0, before, after)[:512], own[:512]])
    across = along_probe(pair, lambda i: i ^ 1)
    present = neighbours >= 0
    slot = (neighbours // 8 - space_rank + 1) % space_count * 8 + neighbours % 8
    slot = jnp.pad(jnp.where(present, slot, DEAD), ((0, 0), (0, 1)), constant_values=DEAD)

    near, rows, peak = pl.pallas_call(
        spectral_kernel,
        out_shape=(
            jax.ShapeDtypeStruct((NEAR + 1, 8, 128), F32),
            jax.ShapeDtypeStruct((8, 3, 32, 128), F32),
            jax.ShapeDtypeStruct((space_count, 128), F32),
        ),
        in_specs=[SMEM] + [WHOLE] * 3,
        out_specs=(WHOLE,) * 3,
        scratch_shapes=[pltpu.VMEM((4, 8, 128), F32)],
        cost_estimate=HEAVY,
        compiler_params=params(4),
        name="spectral",
    )(slot, before, own, after)
    peak, held = lax.optimization_barrier((peak, (before, own, after)))
    peaks = lax.all_to_all(peak, "space", 0, 0, tiled=True)
    probe_turned, table = pl.pallas_call(
        prepare_kernel,
        out_shape=(
            jax.ShapeDtypeStruct((NEAR + 1, 128, 64), BF16),
            jax.ShapeDtypeStruct((NEAR, 128), F32),
        ),
        in_specs=[SMEM] + [WHOLE] * 3,
        out_specs=(WHOLE,) * 2,
        scratch_shapes=[pltpu.VMEM((128, 128), F32)],
        compiler_params=params(4),
        name="prepare",
    )(slot, *held)
    peaks, pair, across, probe_turned = lax.optimization_barrier(
        (peaks, pair, across, probe_turned)
    )
    quad = jnp.stack([pair, across])
    pieces = [quad] + [
        along_probe(quad, lambda i, distance=distance: (i + 2 * distance) % 8)
        for distance in range(1, 4)
    ]

    scaled, operand, one, half = pl.pallas_call(
        first_kernel,
        out_shape=(
            jax.ShapeDtypeStruct((8, 128, 2048), BF16),
            jax.ShapeDtypeStruct((8, 2048, 64), BF16),
            jax.ShapeDtypeStruct((8, 128, 64), F32),
            jax.ShapeDtypeStruct((4, 128, 128), BF16),
        ),
        in_specs=[SMEM] + [WHOLE] * 4,
        out_specs=(WHOLE,) * 4,
        scratch_shapes=[pltpu.VMEM((4, 8, 128), F32)],
        cost_estimate=LIGHT,
        compiler_params=params(16),
        name="first",
    )(slot, peaks, near, rows, probe_turned)
    half_before, half_after = both(half)

    send = pl.pallas_call(
        second_kernel,
        out_shape=jax.ShapeDtypeStruct((8, 88, 128), F32),
        in_specs=[SMEM] + [WHOLE] * 10,
        out_specs=WHOLE,
        cost_estimate=LIGHT,
        scratch_shapes=[
            pltpu.VMEM((NEAR + 1, 128, 64), BF16),
            pltpu.VMEM((2, 2048, 64), BF16),
            pltpu.VMEM((3, 32, 128), F32),
            pltpu.VMEM((3, 8, 128), F32),
            pltpu.VMEM((4, 8, 128), F32),
        ],
        compiler_params=params(16),
        name="second",
    )(slot, near, rows, scaled, operand, probe_turned, one, half_before, half, half_after, table)
    send, pieces = lax.optimization_barrier((send, pieces))
    swapped = [
        lax.ppermute(piece, "space", [(i, i ^ 1) for i in range(space_count)]) for piece in pieces
    ]
    received = lax.all_to_all(send, "probe", 0, 0, tiled=True)
    force = jnp.sum(received[:, 64:88], axis=0)
    from_after = around(force[0:8], space_count, -1)
    from_before = around(force[16:24], space_count, 1)

    density = pl.pallas_call(
        sample_kernel,
        out_shape=jax.ShapeDtypeStruct((16, 15, 8, 128), BF16),
        in_specs=[SMEM, SMEM] + [WHOLE] * 9,
        out_specs=WHOLE,
        scratch_shapes=[
            pltpu.VMEM((128, 512), BF16),
            pltpu.VMEM((NEAR + 1, 128, 128), F32),
            pltpu.VMEM((16 * 120, 128), F32),
        ],
        compiler_params=params(16),
        name="sample",
    )(
        slot, jnp.stack([lax.axis_index("probe"), core]), received, *pieces, *swapped
    )
    forces = force[8:16] + from_after + from_before
    forces = jnp.stack([forces[:, 32 * x : 32 * x + 32] for x in range(3)])
    return density.transpose(0, 2, 1, 3), forces.transpose(1, 0, 2)


def solution(mesh):
    in_specs = (P("space", None, None), P("space", "probe", None), P("space", None))
    out_specs = (P("probe", "space", None, None), P("space", None, None))
    return jax.shard_map(
        per_device, mesh=mesh, in_specs=in_specs, out_specs=out_specs, check_vma=False
    )
```

```python
import functools
import math

import jax
import jax.numpy as jnp
import numpy as np
from jax import lax
from jax.experimental import pallas as pl
from jax.experimental.pallas import tpu as pltpu
from jax.sharding import PartitionSpec as P

SS_SIGMA = -1.938
SP_SIGMA = 1.745
PP_SIGMA = 3.05
PP_PI = -1.075
BOND_LENGTH = 2.35
SOFT_SQUARE = 0.25
CELL_EDGE = 10.86
COEFF_ZERO = 0.6
COEFF_ONE = -0.7
COEFF_TWO = 0.45

PP_SUM = PP_SIGMA - PP_PI
BOND_SQUARE = BOND_LENGTH * BOND_LENGTH
NEAR = 24
DEAD = 24
FAR = 1000.0
SLOTS = 16
F32 = jnp.float32
BF16 = jnp.bfloat16
WHOLE = pl.BlockSpec()
SMEM = pl.BlockSpec(memory_space=pltpu.SMEM)
ANY = pl.BlockSpec(memory_space=pl.ANY)
HEAVY = pl.CostEstimate(flops=0, transcendentals=0, bytes_accessed=60_000_000)
LIGHT = pl.CostEstimate(flops=0, transcendentals=0, bytes_accessed=0)


def params(mebibytes):
    return pltpu.CompilerParams(vmem_limit_bytes=mebibytes * 1024 * 1024)


def slot_offsets():
    half = CELL_EDGE / 2.0
    table = [[0.0, 0.0, 0.0]]
    for sign_x in (-1.0, 1.0):
        for sign_y in (-1.0, 1.0):
            for sign_z in (-1.0, 1.0):
                table.append([sign_x * half, sign_y * half, sign_z * half])
    for axis_pick in range(3):
        for sign_a in (1.0, -1.0):
            entry = [0.0, 0.0, 0.0]
            entry[axis_pick] = sign_a * CELL_EDGE
            table.append(entry)
    table.append([0.0, 0.0, 0.0])
    return np.array(table, dtype=np.float32)


def fill_shifts(shift_ref):
    lane = lanes()
    table = slot_offsets()
    for g in range(4):
        for x in range(3):
            v = [float(table[4 * g + t, x]) for t in range(4)]
            shift_ref[g, x : x + 1, :] = jnp.where(
                lane < 32, v[0], jnp.where(lane < 64, v[1], jnp.where(lane < 96, v[2], v[3]))
            )


def lanes():
    return lax.broadcasted_iota(jnp.int32, (1, 128), 1)


def bond(columns, rows):
    d = [columns[x : x + 1, :] - rows[x] for x in range(3)]
    rho_square = d[0] * d[0] + d[1] * d[1] + d[2] * d[2] + SOFT_SQUARE
    inverse = lax.rsqrt(rho_square)
    radial = jnp.exp(1.0 - rho_square / BOND_SQUARE)
    return d, [v * inverse for v in d], radial, inverse


def four_slots(near_ref, slot_ref, shift_ref, c, g, lane):
    v = [near_ref[slot_ref[c, 4 * g + t]] for t in range(4)]
    joined = jnp.where(
        lane < 32, v[0], jnp.where(lane < 64, v[1], jnp.where(lane < 96, v[2], v[3]))
    )
    return joined + shift_ref[g]


def spectral_kernel(
    slot_ref, core_ref, before_ref, own_ref, after_ref, near_ref, row_ref, peak_ref, pair_ref,
    shift_ref, sem,
):
    kept = pltpu.make_async_copy(own_ref.at[0:512], pair_ref.at[1], sem.at[1])
    kept.start()

    @pl.when(core_ref[0] == 0)
    def _():
        pltpu.make_async_copy(before_ref.at[0:512], pair_ref.at[0], sem.at[0]).start()

    @pl.when(core_ref[0] != 0)
    def _():
        pltpu.make_async_copy(after_ref.at[0:512], pair_ref.at[0], sem.at[0]).start()

    fill_shifts(shift_ref)
    for part, ref in enumerate((before_ref, own_ref, after_ref)):
        for x in range(3):
            coords = ref[512 + 8 * x : 520 + 8 * x, 0:32].astype(F32)
            wide = jnp.concatenate([coords] * 4, axis=1)
            for n in range(8):
                near_ref[8 * part + n, x : x + 1, :] = wide[n : n + 1, :]
            if part == 1:
                upright = wide.T
                for c in range(8):
                    row_ref[c, x] = jnp.broadcast_to(upright[0:32, c : c + 1], (32, 128))
    near_ref[DEAD] = jnp.full((8, 128), FAR, F32)
    lane = lanes()

    def one_cluster(c, peak):
        rows = [row_ref[c, x] for x in range(3)]
        sums = [jnp.zeros((32, 128), F32) for _ in range(4)]
        for g in range(4):
            columns = four_slots(near_ref, slot_ref, shift_ref, c, g, lane)
            _, cosine, radial, _ = bond(columns, rows)
            size = [jnp.abs(v) for v in cosine]
            sums[0] += (-SS_SIGMA + SP_SIGMA * (size[0] + size[1] + size[2])) * radial
            cross = {}
            for a in range(3):
                for b in range(a, 3):
                    product = cosine[a] * cosine[b] * PP_SUM
                    cross[a, b] = cross[b, a] = jnp.abs(product + PP_PI if a == b else product)
            for a in range(3):
                sums[1 + a] += (
                    SP_SIGMA * size[a] + cross[a, 0] + cross[a, 1] + cross[a, 2]
                ) * radial
        for v in sums:
            peak = jnp.maximum(peak, jnp.sum(v, axis=1, keepdims=True))
        return peak

    peak = jnp.zeros((32, 1), F32)
    for c in range(8):
        peak = one_cluster(c, peak)
    peak_ref[...] = jnp.broadcast_to(jnp.max(peak), peak_ref.shape)
    kept.wait()
    pltpu.make_async_copy(before_ref.at[0:512], pair_ref.at[0], sem.at[0]).wait()


def gather_operand(slot_ref, source_ref, target_ref, c):
    for k in range(SLOTS):
        n = slot_ref[c, k]
        for b in range(4):
            low = 512 * (k // 4) + 128 * b + 32 * (k % 4)
            target_ref[low : low + 32, :] = source_ref[n, 32 * b : 32 * b + 32, :]


def prepare_kernel(
    slot_ref, before_ref, own_ref, after_ref, probe_ref, table_ref,
    hot_ref,
):
    lane = lanes()
    for t in range(4):
        for c in range(8):
            for g in range(4):
                row = 32 * t + 4 * c + g
                hot_ref[row : row + 1, :] = (lane == slot_ref[c, 4 * g + t]).astype(F32)
    table_ref[...] = hot_ref[...].T[0:NEAR, :]
    probe_ref[DEAD] = jnp.zeros((128, 64), BF16)
    for part, ref in enumerate((before_ref, own_ref, after_ref)):
        for c in range(8):
            turned = ref[64 * c : 64 * c + 64].astype(F32).T
            probe_ref[8 * part + c] = turned.astype(BF16)


def first_kernel(
    slot_ref, peak_ref, near_ref, row_ref, probe_ref,
    scaled_ref, operand_ref, one_ref, half_ref, shift_ref,
):
    fill_shifts(shift_ref)
    lane = lanes()
    inverse_peak = 1.0 / jnp.max(peak_ref[...])

    def one_pair(pair):
        for side in range(2):
            c = pair + 4 * side
            rows = [row_ref[c, x] for x in range(3)]
            gather_operand(slot_ref, probe_ref, operand_ref.at[c], c)
            for g in range(4):
                columns = four_slots(near_ref, slot_ref, shift_ref, c, g, lane)
                _, cosine, radial, _ = bond(columns, rows)
                radial = radial * inverse_peak
                place = functools.partial(block_at, scaled_ref, c, g)
                place(0, 0, SS_SIGMA * radial)
                sp = SP_SIGMA * radial
                pp = PP_SUM * radial
                pi = PP_PI * radial
                for a in range(3):
                    wave = cosine[a] * sp
                    place(0, a + 1, wave)
                    place(a + 1, 0, -wave)
                    leaning = cosine[a] * pp
                    for b in range(a, 3):
                        value = leaning * cosine[b]
                        if a == b:
                            place(a + 1, a + 1, value + pi)
                        else:
                            place(a + 1, b + 1, value)
                            place(b + 1, a + 1, value)
            one = jnp.dot(scaled_ref[c], operand_ref[c], preferred_element_type=F32)
            one_ref[c] = one
            half_ref[pair, :, 64 * side : 64 * side + 64] = one.astype(BF16)

    for pair in range(4):
        one_pair(pair)


def block_at(scaled_ref, c, g, a, b, value):
    low = 512 * g + 128 * b
    scaled_ref[c, 32 * a : 32 * a + 32, low : low + 128] = value.astype(BF16)


def second_kernel(
    slot_ref, near_ref, row_ref, scaled_ref, operand_ref, probe_ref, one_ref,
    before_ref, own_ref, after_ref, table_ref, send_ref,
    half_ref, gathered_ref, near_pull_ref, own_pull_ref, shift_ref,
):
    fill_shifts(shift_ref)
    lane = lanes()
    for part, ref in enumerate((before_ref, own_ref, after_ref)):
        for pair in range(4):
            half_ref[8 * part + pair] = ref[pair, :, 0:64]
            half_ref[8 * part + pair + 4] = ref[pair, :, 64:128]
    half_ref[DEAD] = jnp.zeros((128, 64), BF16)
    on_row = lax.broadcasted_iota(jnp.int32, (32, 128), 0) == lax.broadcasted_iota(
        jnp.int32, (32, 128), 1
    )

    def one_pair(pair):
        for side in range(2):
            c = pair + 4 * side
            gather_operand(slot_ref, half_ref, gathered_ref.at[side], c)
            two = jnp.dot(scaled_ref[c], gathered_ref[side], preferred_element_type=F32)
            probe = probe_ref[8 + c].astype(F32)
            term_two = 2.0 * two - probe
            mixture = COEFF_ZERO * probe + COEFF_ONE * one_ref[c] + COEFF_TWO * term_two
            mixture = mixture.astype(BF16)
            wide = mixture.astype(F32)
            for q in range(8):
                send_ref[
                    q, 16 * pair : 16 * pair + 16, 64 * side : 64 * side + 64
                ] = wide[16 * q : 16 * q + 16, :]
            rows = [row_ref[c, x] for x in range(3)]
            own = [jnp.zeros((32, 128), F32) for _ in range(3)]
            for g in range(4):
                sample = lax.dot_general(
                    mixture,
                    operand_ref[c, 512 * g : 512 * g + 512, :],
                    (((1,), (1,)), ((), ())),
                    preferred_element_type=F32,
                )
                columns = four_slots(near_ref, slot_ref, shift_ref, c, g, lane)
                pulls = pair_pulls(sample, columns, rows)
                for x in range(3):
                    own[x] = own[x] + pulls[x]
                    near_pull_ref[x, 4 * c + g : 4 * c + g + 1, :] = jnp.sum(
                        pulls[x], axis=0, keepdims=True
                    )
            for x in range(3):
                whole = jnp.broadcast_to(jnp.sum(own[x], axis=1, keepdims=True), (32, 128))
                own_pull_ref[x, c : c + 1, :] = jnp.sum(
                    jnp.where(on_row, whole, 0.0), axis=0, keepdims=True
                )

    for pair in range(4):
        one_pair(pair)

    stacked = jnp.concatenate(
        [
            jnp.concatenate(
                [jnp.where(lane // 32 == t, near_pull_ref[x], 0.0) for x in range(3)], axis=1
            )
            for t in range(4)
        ],
        axis=0,
    )
    gathered = jnp.dot(
        table_ref[...], stacked, precision=lax.Precision.HIGHEST, preferred_element_type=F32
    )
    total = [-gathered[:, 128 * x : 128 * x + 128] for x in range(3)]
    nothing = jnp.zeros((8, 128), F32)
    for x in range(3):
        v = total[x] + jnp.concatenate([nothing, own_pull_ref[x], nothing], axis=0)
        v = v + pltpu.roll(v, 64, 1)
        v = v + pltpu.roll(v, 32, 1)
        total[x] = v * (1.0 / 512.0)
    joined = jnp.where(lane < 32, total[0], jnp.where(lane < 64, total[1], total[2]))
    for q in range(8):
        send_ref[q, 64:88, :] = joined


def pair_pulls(sample, columns, rows):
    part = lambda a, b: sample[32 * a : 32 * a + 32, 128 * b : 128 * b + 128]
    d, cosine, radial, inverse = bond(columns, rows)
    mixed = [SP_SIGMA * (part(0, 1 + x) - part(1 + x, 0)) for x in range(3)]
    double = [2.0 * PP_SUM * part(1 + x, 1 + x) for x in range(3)]
    cross = {}
    for a, b in ((0, 1), (0, 2), (1, 2)):
        cross[a, b] = cross[b, a] = PP_SUM * (part(1 + a, 1 + b) + part(1 + b, 1 + a))
    bent = []
    for a in range(3):
        b, c = [x for x in range(3) if x != a]
        bent.append(double[a] * cosine[a] + cross[a, b] * cosine[b] + cross[a, c] * cosine[c])
    still = SS_SIGMA * part(0, 0) + PP_PI * (part(1, 1) + part(2, 2) + part(3, 3))
    straight = mixed[0] * cosine[0] + mixed[1] * cosine[1] + mixed[2] * cosine[2]
    curved = bent[0] * cosine[0] + bent[1] * cosine[1] + bent[2] * cosine[2]
    value = still + straight + 0.5 * curved
    across = radial * inverse
    inward = radial * value * (-2.0 / BOND_SQUARE) - across * inverse * (straight + curved)
    return [across * (mixed[x] + bent[x]) + inward * d[x] for x in range(3)]


def sample_kernel(
    slot_ref, rank_ref, core_ref, received_ref, *refs
):
    pieces, others = refs[0:4], refs[4:8]
    density_ref, left_ref, sample_ref, turn_ref, swapped_ref, sem = refs[8:]
    copies = [
        pltpu.make_async_copy(other.at[e, 1], swapped_ref.at[i, e, 1], sem.at[i, e])
        for i, other in enumerate(others)
        for e in range(2)
    ]
    for copy in copies:
        copy.start()
    rank, core = rank_ref[0], core_ref[0]
    for distance in range(4):
        source = (rank - 2 * distance + 8) % 8
        for e in range(2):
            q = source if e == 0 else source + 1 - 2 * (source % 2)
            low = 64 * (2 * distance + e)
            block = received_ref[q, 0:64, :].astype(BF16)
            left_ref[0:64, low : low + 64] = block[:, 0:64]
            left_ref[64:128, low : low + 64] = block[:, 64:128]
    left = left_ref[...]
    scale = 1.0 / math.sqrt(512.0)
    swapped = [swapped_ref.at[i] for i in range(4)]
    sides = ((pieces, 0, 16 * core), (pieces, 1, 8), (swapped, 1, 16 - 16 * core))
    for side, (source_refs, index, base) in enumerate(sides):
        if side == 2:
            for copy in copies:
                copy.wait()
        for pair in range(4):
            c = 2 * pair
            right = jnp.concatenate(
                [
                    jnp.concatenate(
                        [
                            ref[e, index, 64 * n : 64 * n + 64, :]
                            for ref in source_refs
                            for e in range(2)
                        ],
                        axis=0,
                    )
                    for n in (c, c + 1)
                ],
                axis=1,
            )
            product = jnp.dot(left, right, preferred_element_type=F32) * scale
            sample_ref[base + c] = product[:, 0:128]
            sample_ref[base + c + 1] = product[:, 128:256]
    sample_ref[DEAD] = jnp.zeros((128, 128), F32)
    for c in range(8):
        for k in range(15):
            turn_ref[pl.ds(8 * k + c, 16, stride=120), :] = sample_ref[
                slot_ref[c, k], 16 * c : 16 * c + 16, :
            ]
    for r in range(16):
        density_ref[r] = turn_ref[120 * r : 120 * r + 120].astype(BF16).reshape(15, 8, 128)


def around(block, size, distance):
    return lax.ppermute(block, "space", [((i - distance) % size, i) for i in range(size)])


def along_probe(block, target):
    return lax.ppermute(block, "probe", [(i, target(i)) for i in range(8)])


def per_device(positions, probes, neighbours):
    space_count = lax.axis_size("space")
    space_rank = lax.axis_index("space")
    both = lambda block: (around(block, space_count, 1), around(block, space_count, -1))

    coords = jnp.pad(positions.transpose(1, 0, 2), ((0, 0), (0, 0), (0, 96)))
    own = jnp.concatenate([probes.reshape(512, 128), coords.reshape(24, 128)])
    before, after = both(own)
    core = space_rank % 2
    present = neighbours >= 0
    slot = (neighbours // 8 - space_rank + 1) % space_count * 8 + neighbours % 8
    slot = jnp.pad(jnp.where(present, slot, DEAD), ((0, 0), (0, 1)), constant_values=DEAD)

    before, after, slot = lax.optimization_barrier((before, after, slot))
    near, rows, peak, pair = pl.pallas_call(
        spectral_kernel,
        out_shape=(
            jax.ShapeDtypeStruct((NEAR + 1, 8, 128), F32),
            jax.ShapeDtypeStruct((8, 3, 32, 128), F32),
            jax.ShapeDtypeStruct((space_count, 128), F32),
            jax.ShapeDtypeStruct((2, 512, 128), BF16),
        ),
        in_specs=[SMEM, SMEM] + [WHOLE] * 3,
        out_specs=(WHOLE,) * 4,
        scratch_shapes=[pltpu.VMEM((4, 8, 128), F32), pltpu.SemaphoreType.DMA((2,))],
        cost_estimate=HEAVY,
        compiler_params=params(4),
        name="spectral",
    )(slot, core.reshape(1), before, own, after)
    across = along_probe(pair, lambda i: i ^ 1)
    peak, held = lax.optimization_barrier((peak, (before, own, after)))
    peaks = lax.all_to_all(peak, "space", 0, 0, tiled=True)
    probe_turned, table = pl.pallas_call(
        prepare_kernel,
        out_shape=(
            jax.ShapeDtypeStruct((NEAR + 1, 128, 64), BF16),
            jax.ShapeDtypeStruct((NEAR, 128), F32),
        ),
        in_specs=[SMEM] + [WHOLE] * 3,
        out_specs=(WHOLE,) * 2,
        scratch_shapes=[pltpu.VMEM((128, 128), F32)],
        compiler_params=params(4),
        name="prepare",
    )(slot, *held)
    peaks, pair, across, probe_turned = lax.optimization_barrier(
        (peaks, pair, across, probe_turned)
    )
    quad = jnp.stack([pair, across])
    pieces = [quad] + [
        along_probe(quad, lambda i, distance=distance: (i + 2 * distance) % 8)
        for distance in range(1, 4)
    ]

    scaled, operand, one, half = pl.pallas_call(
        first_kernel,
        out_shape=(
            jax.ShapeDtypeStruct((8, 128, 2048), BF16),
            jax.ShapeDtypeStruct((8, 2048, 64), BF16),
            jax.ShapeDtypeStruct((8, 128, 64), F32),
            jax.ShapeDtypeStruct((4, 128, 128), BF16),
        ),
        in_specs=[SMEM] + [WHOLE] * 4,
        out_specs=(WHOLE,) * 4,
        scratch_shapes=[pltpu.VMEM((4, 8, 128), F32)],
        cost_estimate=LIGHT,
        compiler_params=params(16),
        name="first",
    )(slot, peaks, near, rows, probe_turned)
    half_before, half_after = both(half)

    send = pl.pallas_call(
        second_kernel,
        out_shape=jax.ShapeDtypeStruct((8, 88, 128), F32),
        in_specs=[SMEM] + [WHOLE] * 10,
        out_specs=WHOLE,
        cost_estimate=LIGHT,
        scratch_shapes=[
            pltpu.VMEM((NEAR + 1, 128, 64), BF16),
            pltpu.VMEM((2, 2048, 64), BF16),
            pltpu.VMEM((3, 32, 128), F32),
            pltpu.VMEM((3, 8, 128), F32),
            pltpu.VMEM((4, 8, 128), F32),
        ],
        compiler_params=params(16),
        name="second",
    )(slot, near, rows, scaled, operand, probe_turned, one, half_before, half, half_after, table)
    send, pieces = lax.optimization_barrier((send, pieces))
    swapped = [
        lax.ppermute(piece, "space", [(i, i ^ 1) for i in range(space_count)]) for piece in pieces
    ]
    received = lax.all_to_all(send, "probe", 0, 0, tiled=True)
    force = jnp.sum(received[:, 64:88], axis=0)
    from_after = around(force[0:8], space_count, -1)
    from_before = around(force[16:24], space_count, 1)

    density = pl.pallas_call(
        sample_kernel,
        out_shape=jax.ShapeDtypeStruct((16, 15, 8, 128), BF16),
        in_specs=[SMEM] * 3 + [WHOLE] * 5 + [ANY] * 4,
        out_specs=WHOLE,
        scratch_shapes=[
            pltpu.VMEM((128, 512), BF16),
            pltpu.VMEM((NEAR + 1, 128, 128), F32),
            pltpu.VMEM((16 * 120, 128), F32),
            pltpu.VMEM((4, 2, 2, 512, 128), BF16),
            pltpu.SemaphoreType.DMA((4, 2)),
        ],
        compiler_params=params(16),
        name="sample",
    )(
        slot, lax.axis_index("probe").reshape(1), core.reshape(1), received, *pieces, *swapped
    )
    forces = force[8:16] + from_after + from_before
    forces = jnp.stack([forces[:, 32 * x : 32 * x + 32] for x in range(3)])
    return density.transpose(0, 2, 1, 3), forces.transpose(1, 0, 2)


def solution(mesh):
    in_specs = (P("space", None, None), P("space", "probe", None), P("space", None))
    out_specs = (P("probe", "space", None, None), P("space", None, None))
    return jax.shard_map(
        per_device, mesh=mesh, in_specs=in_specs, out_specs=out_specs, check_vma=False
    )
```

```python
import functools
import math

import jax
import jax.numpy as jnp
import numpy as np
from jax import lax
from jax.experimental import pallas as pl
from jax.experimental.pallas import tpu as pltpu
from jax.sharding import PartitionSpec as P

SS_SIGMA = -1.938
SP_SIGMA = 1.745
PP_SIGMA = 3.05
PP_PI = -1.075
BOND_LENGTH = 2.35
SOFT_SQUARE = 0.25
CELL_EDGE = 10.86
COEFF_ZERO = 0.6
COEFF_ONE = -0.7
COEFF_TWO = 0.45

PP_SUM = PP_SIGMA - PP_PI
BOND_SQUARE = BOND_LENGTH * BOND_LENGTH
NEAR = 24
DEAD = 24
FAR = 1000.0
SLOTS = 16
F32 = jnp.float32
BF16 = jnp.bfloat16
WHOLE = pl.BlockSpec()
SMEM = pl.BlockSpec(memory_space=pltpu.SMEM)
HEAVY = pl.CostEstimate(flops=0, transcendentals=0, bytes_accessed=60_000_000)
LIGHT = pl.CostEstimate(flops=0, transcendentals=0, bytes_accessed=0)


def params(mebibytes):
    return pltpu.CompilerParams(vmem_limit_bytes=mebibytes * 1024 * 1024)


def slot_offsets():
    half = CELL_EDGE / 2.0
    table = [[0.0, 0.0, 0.0]]
    for sign_x in (-1.0, 1.0):
        for sign_y in (-1.0, 1.0):
            for sign_z in (-1.0, 1.0):
                table.append([sign_x * half, sign_y * half, sign_z * half])
    for axis_pick in range(3):
        for sign_a in (1.0, -1.0):
            entry = [0.0, 0.0, 0.0]
            entry[axis_pick] = sign_a * CELL_EDGE
            table.append(entry)
    table.append([0.0, 0.0, 0.0])
    return np.array(table, dtype=np.float32)


def fill_shifts(shift_ref):
    lane = lanes()
    table = slot_offsets()
    for g in range(4):
        for x in range(3):
            v = [float(table[4 * g + t, x]) for t in range(4)]
            shift_ref[g, x : x + 1, :] = jnp.where(
                lane < 32, v[0], jnp.where(lane < 64, v[1], jnp.where(lane < 96, v[2], v[3]))
            )


def lanes():
    return lax.broadcasted_iota(jnp.int32, (1, 128), 1)


def bond(columns, rows):
    d = [columns[x : x + 1, :] - rows[x] for x in range(3)]
    rho_square = d[0] * d[0] + d[1] * d[1] + d[2] * d[2] + SOFT_SQUARE
    inverse = lax.rsqrt(rho_square)
    radial = jnp.exp(1.0 - rho_square / BOND_SQUARE)
    return d, [v * inverse for v in d], radial, inverse


def four_slots(near_ref, slot_ref, shift_ref, c, g, lane):
    v = [near_ref[slot_ref[c, 4 * g + t]] for t in range(4)]
    joined = jnp.where(
        lane < 32, v[0], jnp.where(lane < 64, v[1], jnp.where(lane < 96, v[2], v[3]))
    )
    return joined + shift_ref[g]


def spectral_kernel(
    slot_ref, core_ref, before_ref, own_ref, after_ref, near_ref, row_ref, peak_ref, pair_ref,
    shift_ref, sem,
):
    kept = pltpu.make_async_copy(own_ref.at[0:512], pair_ref.at[1], sem.at[1])
    kept.start()

    @pl.when(core_ref[0] == 0)
    def _():
        pltpu.make_async_copy(before_ref.at[0:512], pair_ref.at[0], sem.at[0]).start()

    @pl.when(core_ref[0] != 0)
    def _():
        pltpu.make_async_copy(after_ref.at[0:512], pair_ref.at[0], sem.at[0]).start()

    fill_shifts(shift_ref)
    for part, ref in enumerate((before_ref, own_ref, after_ref)):
        for x in range(3):
            coords = ref[512 + 8 * x : 520 + 8 * x, 0:32].astype(F32)
            wide = jnp.concatenate([coords] * 4, axis=1)
            for n in range(8):
                near_ref[8 * part + n, x : x + 1, :] = wide[n : n + 1, :]
            if part == 1:
                upright = wide.T
                for c in range(8):
                    row_ref[c, x] = jnp.broadcast_to(upright[0:32, c : c + 1], (32, 128))
    near_ref[DEAD] = jnp.full((8, 128), FAR, F32)
    lane = lanes()

    def one_cluster(c, peak):
        rows = [row_ref[c, x] for x in range(3)]
        sums = [jnp.zeros((32, 128), F32) for _ in range(4)]
        for g in range(4):
            columns = four_slots(near_ref, slot_ref, shift_ref, c, g, lane)
            _, cosine, radial, _ = bond(columns, rows)
            size = [jnp.abs(v) for v in cosine]
            sums[0] += (-SS_SIGMA + SP_SIGMA * (size[0] + size[1] + size[2])) * radial
            cross = {}
            for a in range(3):
                for b in range(a, 3):
                    product = cosine[a] * cosine[b] * PP_SUM
                    cross[a, b] = cross[b, a] = jnp.abs(product + PP_PI if a == b else product)
            for a in range(3):
                sums[1 + a] += (
                    SP_SIGMA * size[a] + cross[a, 0] + cross[a, 1] + cross[a, 2]
                ) * radial
        for v in sums:
            peak = jnp.maximum(peak, jnp.sum(v, axis=1, keepdims=True))
        return peak

    peak = jnp.zeros((32, 1), F32)
    for c in range(8):
        peak = one_cluster(c, peak)
    peak_ref[...] = jnp.broadcast_to(jnp.max(peak), peak_ref.shape)
    kept.wait()
    pltpu.make_async_copy(before_ref.at[0:512], pair_ref.at[0], sem.at[0]).wait()


def gather_operand(slot_ref, source_ref, target_ref, c):
    for k in range(SLOTS):
        n = slot_ref[c, k]
        for b in range(4):
            low = 512 * (k // 4) + 128 * b + 32 * (k % 4)
            target_ref[low : low + 32, :] = source_ref[n, 32 * b : 32 * b + 32, :]


def prepare_kernel(
    slot_ref, before_ref, own_ref, after_ref, probe_ref, table_ref,
    hot_ref,
):
    lane = lanes()
    for t in range(4):
        for c in range(8):
            for g in range(4):
                row = 32 * t + 4 * c + g
                hot_ref[row : row + 1, :] = (lane == slot_ref[c, 4 * g + t]).astype(F32)
    table_ref[...] = hot_ref[...].T[0:NEAR, :]
    probe_ref[DEAD] = jnp.zeros((128, 64), BF16)
    for part, ref in enumerate((before_ref, own_ref, after_ref)):
        for c in range(8):
            turned = ref[64 * c : 64 * c + 64].astype(F32).T
            probe_ref[8 * part + c] = turned.astype(BF16)


def first_kernel(
    slot_ref, peak_ref, near_ref, row_ref, probe_ref,
    scaled_ref, operand_ref, one_ref, half_ref, shift_ref,
):
    fill_shifts(shift_ref)
    lane = lanes()
    inverse_peak = 1.0 / jnp.max(peak_ref[...])

    def one_pair(pair):
        for side in range(2):
            c = pair + 4 * side
            rows = [row_ref[c, x] for x in range(3)]
            gather_operand(slot_ref, probe_ref, operand_ref.at[c], c)
            for g in range(4):
                columns = four_slots(near_ref, slot_ref, shift_ref, c, g, lane)
                _, cosine, radial, _ = bond(columns, rows)
                radial = radial * inverse_peak
                place = functools.partial(block_at, scaled_ref, c, g)
                place(0, 0, SS_SIGMA * radial)
                sp = SP_SIGMA * radial
                pp = PP_SUM * radial
                pi = PP_PI * radial
                for a in range(3):
                    wave = cosine[a] * sp
                    place(0, a + 1, wave)
                    place(a + 1, 0, -wave)
                    leaning = cosine[a] * pp
                    for b in range(a, 3):
                        value = leaning * cosine[b]
                        if a == b:
                            place(a + 1, a + 1, value + pi)
                        else:
                            place(a + 1, b + 1, value)
                            place(b + 1, a + 1, value)
            one = jnp.dot(scaled_ref[c], operand_ref[c], preferred_element_type=F32)
            one_ref[c] = one
            half_ref[pair, :, 64 * side : 64 * side + 64] = one.astype(BF16)

    for pair in range(4):
        one_pair(pair)


def block_at(scaled_ref, c, g, a, b, value):
    low = 512 * g + 128 * b
    scaled_ref[c, 32 * a : 32 * a + 32, low : low + 128] = value.astype(BF16)


def second_kernel(
    slot_ref, near_ref, row_ref, scaled_ref, operand_ref, probe_ref, one_ref,
    before_ref, own_ref, after_ref, table_ref, send_ref,
    half_ref, gathered_ref, near_pull_ref, own_pull_ref, shift_ref,
):
    fill_shifts(shift_ref)
    lane = lanes()
    for part, ref in enumerate((before_ref, own_ref, after_ref)):
        for pair in range(4):
            half_ref[8 * part + pair] = ref[pair, :, 0:64]
            half_ref[8 * part + pair + 4] = ref[pair, :, 64:128]
    half_ref[DEAD] = jnp.zeros((128, 64), BF16)
    on_row = lax.broadcasted_iota(jnp.int32, (32, 128), 0) == lax.broadcasted_iota(
        jnp.int32, (32, 128), 1
    )

    def one_pair(pair):
        for side in range(2):
            c = pair + 4 * side
            gather_operand(slot_ref, half_ref, gathered_ref.at[side], c)
            two = jnp.dot(scaled_ref[c], gathered_ref[side], preferred_element_type=F32)
            probe = probe_ref[8 + c].astype(F32)
            term_two = 2.0 * two - probe
            mixture = COEFF_ZERO * probe + COEFF_ONE * one_ref[c] + COEFF_TWO * term_two
            mixture = mixture.astype(BF16)
            wide = mixture.astype(F32)
            for q in range(8):
                send_ref[
                    q, 16 * pair : 16 * pair + 16, 64 * side : 64 * side + 64
                ] = wide[16 * q : 16 * q + 16, :]
            rows = [row_ref[c, x] for x in range(3)]
            own = [jnp.zeros((32, 128), F32) for _ in range(3)]
            for g in range(4):
                sample = lax.dot_general(
                    mixture,
                    operand_ref[c, 512 * g : 512 * g + 512, :],
                    (((1,), (1,)), ((), ())),
                    preferred_element_type=F32,
                )
                columns = four_slots(near_ref, slot_ref, shift_ref, c, g, lane)
                pulls = pair_pulls(sample, columns, rows)
                for x in range(3):
                    own[x] = own[x] + pulls[x]
                    near_pull_ref[x, 4 * c + g : 4 * c + g + 1, :] = jnp.sum(
                        pulls[x], axis=0, keepdims=True
                    )
            for x in range(3):
                whole = jnp.broadcast_to(jnp.sum(own[x], axis=1, keepdims=True), (32, 128))
                own_pull_ref[x, c : c + 1, :] = jnp.sum(
                    jnp.where(on_row, whole, 0.0), axis=0, keepdims=True
                )

    for pair in range(4):
        one_pair(pair)

    stacked = jnp.concatenate(
        [
            jnp.concatenate(
                [jnp.where(lane // 32 == t, near_pull_ref[x], 0.0) for x in range(3)], axis=1
            )
            for t in range(4)
        ],
        axis=0,
    )
    gathered = jnp.dot(
        table_ref[...], stacked, precision=lax.Precision.HIGHEST, preferred_element_type=F32
    )
    total = [-gathered[:, 128 * x : 128 * x + 128] for x in range(3)]
    nothing = jnp.zeros((8, 128), F32)
    for x in range(3):
        v = total[x] + jnp.concatenate([nothing, own_pull_ref[x], nothing], axis=0)
        v = v + pltpu.roll(v, 64, 1)
        v = v + pltpu.roll(v, 32, 1)
        total[x] = v * (1.0 / 512.0)
    joined = jnp.where(lane < 32, total[0], jnp.where(lane < 64, total[1], total[2]))
    for q in range(8):
        send_ref[q, 64:88, :] = joined


def pair_pulls(sample, columns, rows):
    part = lambda a, b: sample[32 * a : 32 * a + 32, 128 * b : 128 * b + 128]
    d, cosine, radial, inverse = bond(columns, rows)
    mixed = [SP_SIGMA * (part(0, 1 + x) - part(1 + x, 0)) for x in range(3)]
    double = [2.0 * PP_SUM * part(1 + x, 1 + x) for x in range(3)]
    cross = {}
    for a, b in ((0, 1), (0, 2), (1, 2)):
        cross[a, b] = cross[b, a] = PP_SUM * (part(1 + a, 1 + b) + part(1 + b, 1 + a))
    bent = []
    for a in range(3):
        b, c = [x for x in range(3) if x != a]
        bent.append(double[a] * cosine[a] + cross[a, b] * cosine[b] + cross[a, c] * cosine[c])
    still = SS_SIGMA * part(0, 0) + PP_PI * (part(1, 1) + part(2, 2) + part(3, 3))
    straight = mixed[0] * cosine[0] + mixed[1] * cosine[1] + mixed[2] * cosine[2]
    curved = bent[0] * cosine[0] + bent[1] * cosine[1] + bent[2] * cosine[2]
    value = still + straight + 0.5 * curved
    across = radial * inverse
    inward = radial * value * (-2.0 / BOND_SQUARE) - across * inverse * (straight + curved)
    return [across * (mixed[x] + bent[x]) + inward * d[x] for x in range(3)]


def sample_kernel(
    slot_ref, rank_ref, core_ref, received_ref, *refs
):
    pieces, swapped = refs[0:4], refs[4:8]
    density_ref, left_ref, sample_ref, turn_ref = refs[8:]
    rank, core = rank_ref[0], core_ref[0]
    for distance in range(4):
        source = (rank - 2 * distance + 8) % 8
        for e in range(2):
            q = source if e == 0 else source + 1 - 2 * (source % 2)
            low = 64 * (2 * distance + e)
            block = received_ref[q, 0:64, :].astype(BF16)
            left_ref[0:64, low : low + 64] = block[:, 0:64]
            left_ref[64:128, low : low + 64] = block[:, 64:128]
    left = left_ref[...]
    scale = 1.0 / math.sqrt(512.0)
    sides = ((pieces, 0, 16 * core), (pieces, 1, 8), (swapped, 1, 16 - 16 * core))
    for source_refs, index, base in sides:
        for pair in range(4):
            c = 2 * pair
            right = jnp.concatenate(
                [
                    jnp.concatenate(
                        [
                            ref[e, index, 64 * n : 64 * n + 64, :]
                            for ref in source_refs
                            for e in range(2)
                        ],
                        axis=0,
                    )
                    for n in (c, c + 1)
                ],
                axis=1,
            )
            product = jnp.dot(left, right, preferred_element_type=F32) * scale
            sample_ref[base + c] = product[:, 0:128]
            sample_ref[base + c + 1] = product[:, 128:256]
    sample_ref[DEAD] = jnp.zeros((128, 128), F32)
    for c in range(8):
        for k in range(15):
            turn_ref[pl.ds(8 * k + c, 16, stride=120), :] = sample_ref[
                slot_ref[c, k], 16 * c : 16 * c + 16, :
            ]
    for r in range(16):
        density_ref[r] = turn_ref[120 * r : 120 * r + 120].astype(BF16).reshape(15, 8, 128)


def around(block, size, distance):
    return lax.ppermute(block, "space", [((i - distance) % size, i) for i in range(size)])


def along_probe(block, target):
    return lax.ppermute(block, "probe", [(i, target(i)) for i in range(8)])


def per_device(positions, probes, neighbours):
    space_count = lax.axis_size("space")
    space_rank = lax.axis_index("space")
    both = lambda block: (around(block, space_count, 1), around(block, space_count, -1))

    coords = jnp.pad(positions.transpose(1, 0, 2), ((0, 0), (0, 0), (0, 96)))
    own = jnp.concatenate([probes.reshape(64, 8, 128), coords]).reshape(536, 128)
    before, after = both(own)
    core = space_rank % 2
    present = neighbours >= 0
    slot = (neighbours // 8 - space_rank + 1) % space_count * 8 + neighbours % 8
    slot = jnp.pad(jnp.where(present, slot, DEAD), ((0, 0), (0, 1)), constant_values=DEAD)

    before, after, slot = lax.optimization_barrier((before, after, slot))
    near, rows, peak, pair = pl.pallas_call(
        spectral_kernel,
        out_shape=(
            jax.ShapeDtypeStruct((NEAR + 1, 8, 128), F32),
            jax.ShapeDtypeStruct((8, 3, 32, 128), F32),
            jax.ShapeDtypeStruct((space_count, 128), F32),
            jax.ShapeDtypeStruct((2, 512, 128), BF16),
        ),
        in_specs=[SMEM, SMEM] + [WHOLE] * 3,
        out_specs=(WHOLE,) * 4,
        scratch_shapes=[pltpu.VMEM((4, 8, 128), F32), pltpu.SemaphoreType.DMA((2,))],
        cost_estimate=HEAVY,
        compiler_params=params(4),
        name="spectral",
    )(slot, core.reshape(1), before, own, after)
    across = along_probe(pair, lambda i: i ^ 1)
    peak, held = lax.optimization_barrier((peak, (before, own, after)))
    peaks = lax.all_to_all(peak, "space", 0, 0, tiled=True)
    probe_turned, table = pl.pallas_call(
        prepare_kernel,
        out_shape=(
            jax.ShapeDtypeStruct((NEAR + 1, 128, 64), BF16),
            jax.ShapeDtypeStruct((NEAR, 128), F32),
        ),
        in_specs=[SMEM] + [WHOLE] * 3,
        out_specs=(WHOLE,) * 2,
        scratch_shapes=[pltpu.VMEM((128, 128), F32)],
        compiler_params=params(4),
        name="prepare",
    )(slot, *held)
    peaks, pair, across, probe_turned = lax.optimization_barrier(
        (peaks, pair, across, probe_turned)
    )
    quad = jnp.stack([pair, across])
    pieces = [quad] + [
        along_probe(quad, lambda i, distance=distance: (i + 2 * distance) % 8)
        for distance in range(1, 4)
    ]

    scaled, operand, one, half = pl.pallas_call(
        first_kernel,
        out_shape=(
            jax.ShapeDtypeStruct((8, 128, 2048), BF16),
            jax.ShapeDtypeStruct((8, 2048, 64), BF16),
            jax.ShapeDtypeStruct((8, 128, 64), F32),
            jax.ShapeDtypeStruct((4, 128, 128), BF16),
        ),
        in_specs=[SMEM] + [WHOLE] * 4,
        out_specs=(WHOLE,) * 4,
        scratch_shapes=[pltpu.VMEM((4, 8, 128), F32)],
        cost_estimate=LIGHT,
        compiler_params=params(16),
        name="first",
    )(slot, peaks, near, rows, probe_turned)
    half_before, half_after = both(half)

    send = pl.pallas_call(
        second_kernel,
        out_shape=jax.ShapeDtypeStruct((8, 88, 128), F32),
        in_specs=[SMEM] + [WHOLE] * 10,
        out_specs=WHOLE,
        cost_estimate=LIGHT,
        scratch_shapes=[
            pltpu.VMEM((NEAR + 1, 128, 64), BF16),
            pltpu.VMEM((2, 2048, 64), BF16),
            pltpu.VMEM((3, 32, 128), F32),
            pltpu.VMEM((3, 8, 128), F32),
            pltpu.VMEM((4, 8, 128), F32),
        ],
        compiler_params=params(16),
        name="second",
    )(slot, near, rows, scaled, operand, probe_turned, one, half_before, half, half_after, table)
    send, pieces = lax.optimization_barrier((send, pieces))
    swapped = [
        lax.ppermute(piece, "space", [(i, i ^ 1) for i in range(space_count)]) for piece in pieces
    ]
    received = lax.all_to_all(send, "probe", 0, 0, tiled=True)
    force = jnp.sum(received[:, 64:88], axis=0)
    from_after = around(force[0:8], space_count, -1)
    from_before = around(force[16:24], space_count, 1)

    density = pl.pallas_call(
        sample_kernel,
        out_shape=jax.ShapeDtypeStruct((16, 15, 8, 128), BF16),
        in_specs=[SMEM] * 3 + [WHOLE] * 9,
        out_specs=WHOLE,
        scratch_shapes=[
            pltpu.VMEM((128, 512), BF16),
            pltpu.VMEM((NEAR + 1, 128, 128), F32),
            pltpu.VMEM((16 * 120, 128), F32),
        ],
        compiler_params=params(16),
        name="sample",
    )(
        slot, lax.axis_index("probe").reshape(1), core.reshape(1), received, *pieces, *swapped
    )
    forces = force[8:16] + from_after + from_before
    forces = jnp.stack([forces[:, 32 * x : 32 * x + 32] for x in range(3)])
    return density.transpose(0, 2, 1, 3), forces.transpose(1, 0, 2)


def solution(mesh):
    in_specs = (P("space", None, None), P("space", "probe", None), P("space", None))
    out_specs = (P("probe", "space", None, None), P("space", None, None))
    return jax.shard_map(
        per_device, mesh=mesh, in_specs=in_specs, out_specs=out_specs, check_vma=False
    )
```

```python
import functools
import math

import jax
import jax.numpy as jnp
import numpy as np
from jax import lax
from jax.experimental import pallas as pl
from jax.experimental.pallas import tpu as pltpu
from jax.sharding import PartitionSpec as P

SS_SIGMA = -1.938
SP_SIGMA = 1.745
PP_SIGMA = 3.05
PP_PI = -1.075
BOND_LENGTH = 2.35
SOFT_SQUARE = 0.25
CELL_EDGE = 10.86
COEFF_ZERO = 0.6
COEFF_ONE = -0.7
COEFF_TWO = 0.45

PP_SUM = PP_SIGMA - PP_PI
BOND_SQUARE = BOND_LENGTH * BOND_LENGTH
NEAR = 24
DEAD = 24
FAR = 1000.0
SLOTS = 16
F32 = jnp.float32
BF16 = jnp.bfloat16
WHOLE = pl.BlockSpec()
SMEM = pl.BlockSpec(memory_space=pltpu.SMEM)
HEAVY = pl.CostEstimate(flops=0, transcendentals=0, bytes_accessed=60_000_000)
LIGHT = pl.CostEstimate(flops=0, transcendentals=0, bytes_accessed=0)


def params(mebibytes):
    return pltpu.CompilerParams(vmem_limit_bytes=mebibytes * 1024 * 1024)


def slot_offsets():
    half = CELL_EDGE / 2.0
    table = [[0.0, 0.0, 0.0]]
    for sign_x in (-1.0, 1.0):
        for sign_y in (-1.0, 1.0):
            for sign_z in (-1.0, 1.0):
                table.append([sign_x * half, sign_y * half, sign_z * half])
    for axis_pick in range(3):
        for sign_a in (1.0, -1.0):
            entry = [0.0, 0.0, 0.0]
            entry[axis_pick] = sign_a * CELL_EDGE
            table.append(entry)
    table.append([0.0, 0.0, 0.0])
    return np.array(table, dtype=np.float32)


def fill_shifts(shift_ref):
    lane = lanes()
    table = slot_offsets()
    for g in range(4):
        for x in range(3):
            v = [float(table[4 * g + t, x]) for t in range(4)]
            shift_ref[g, x : x + 1, :] = jnp.where(
                lane < 32, v[0], jnp.where(lane < 64, v[1], jnp.where(lane < 96, v[2], v[3]))
            )


def lanes():
    return lax.broadcasted_iota(jnp.int32, (1, 128), 1)


def bond(columns, rows):
    d = [columns[x : x + 1, :] - rows[x] for x in range(3)]
    rho_square = d[0] * d[0] + d[1] * d[1] + d[2] * d[2] + SOFT_SQUARE
    inverse = lax.rsqrt(rho_square)
    radial = jnp.exp(1.0 - rho_square / BOND_SQUARE)
    return d, [v * inverse for v in d], radial, inverse


def four_slots(near_ref, slot_ref, shift_ref, c, g, lane):
    v = [near_ref[slot_ref[c, 4 * g + t]] for t in range(4)]
    joined = jnp.where(
        lane < 32, v[0], jnp.where(lane < 64, v[1], jnp.where(lane < 96, v[2], v[3]))
    )
    return joined + shift_ref[g]


def spectral_kernel(
    slot_ref, core_ref, before_ref, own_ref, after_ref, near_ref, row_ref, peak_ref, pair_ref,
    shift_ref, sem,
):
    kept = pltpu.make_async_copy(own_ref.at[0:512], pair_ref.at[1], sem.at[1])
    kept.start()

    @pl.when(core_ref[0] == 0)
    def _():
        pltpu.make_async_copy(before_ref.at[0:512], pair_ref.at[0], sem.at[0]).start()

    @pl.when(core_ref[0] != 0)
    def _():
        pltpu.make_async_copy(after_ref.at[0:512], pair_ref.at[0], sem.at[0]).start()

    fill_shifts(shift_ref)
    for part, ref in enumerate((before_ref, own_ref, after_ref)):
        for x in range(3):
            coords = ref[512 + 8 * x : 520 + 8 * x, 0:32].astype(F32)
            wide = jnp.concatenate([coords] * 4, axis=1)
            for n in range(8):
                near_ref[8 * part + n, x : x + 1, :] = wide[n : n + 1, :]
            if part == 1:
                upright = wide.T
                for c in range(8):
                    row_ref[c, x] = jnp.broadcast_to(upright[0:32, c : c + 1], (32, 128))
    near_ref[DEAD] = jnp.full((8, 128), FAR, F32)
    lane = lanes()

    def one_cluster(c, peak):
        rows = [row_ref[c, x] for x in range(3)]
        sums = [jnp.zeros((32, 128), F32) for _ in range(4)]
        for g in range(4):
            columns = four_slots(near_ref, slot_ref, shift_ref, c, g, lane)
            _, cosine, radial, _ = bond(columns, rows)
            size = [jnp.abs(v) for v in cosine]
            sums[0] += (-SS_SIGMA + SP_SIGMA * (size[0] + size[1] + size[2])) * radial
            cross = {}
            for a in range(3):
                for b in range(a, 3):
                    product = cosine[a] * cosine[b] * PP_SUM
                    cross[a, b] = cross[b, a] = jnp.abs(product + PP_PI if a == b else product)
            for a in range(3):
                sums[1 + a] += (
                    SP_SIGMA * size[a] + cross[a, 0] + cross[a, 1] + cross[a, 2]
                ) * radial
        for v in sums:
            peak = jnp.maximum(peak, jnp.sum(v, axis=1, keepdims=True))
        return peak

    peak = jnp.zeros((32, 1), F32)
    for c in range(8):
        peak = one_cluster(c, peak)
    peak_ref[...] = jnp.broadcast_to(jnp.max(peak), peak_ref.shape)
    kept.wait()
    pltpu.make_async_copy(before_ref.at[0:512], pair_ref.at[0], sem.at[0]).wait()


def gather_operand(slot_ref, source_ref, target_ref, c):
    for k in range(SLOTS):
        n = slot_ref[c, k]
        for b in range(4):
            low = 512 * (k // 4) + 128 * b + 32 * (k % 4)
            target_ref[low : low + 32, :] = source_ref[n, 32 * b : 32 * b + 32, :]


def prepare_kernel(
    slot_ref, before_ref, own_ref, after_ref, probe_ref, table_ref,
    hot_ref,
):
    lane = lanes()
    for t in range(4):
        for c in range(8):
            for g in range(4):
                row = 32 * t + 4 * c + g
                hot_ref[row : row + 1, :] = (lane == slot_ref[c, 4 * g + t]).astype(F32)
    table_ref[...] = hot_ref[...].T[0:NEAR, :]
    probe_ref[DEAD] = jnp.zeros((128, 64), BF16)
    for part, ref in enumerate((before_ref, own_ref, after_ref)):
        for c in range(8):
            turned = ref[64 * c : 64 * c + 64].astype(F32).T
            probe_ref[8 * part + c] = turned.astype(BF16)


def first_kernel(
    slot_ref, peak_ref, near_ref, row_ref, probe_ref,
    scaled_ref, operand_ref, one_ref, half_ref, shift_ref,
):
    fill_shifts(shift_ref)
    lane = lanes()
    inverse_peak = 1.0 / jnp.max(peak_ref[...])

    def one_pair(pair):
        for side in range(2):
            c = pair + 4 * side
            rows = [row_ref[c, x] for x in range(3)]
            gather_operand(slot_ref, probe_ref, operand_ref.at[c], c)
            for g in range(4):
                columns = four_slots(near_ref, slot_ref, shift_ref, c, g, lane)
                _, cosine, radial, _ = bond(columns, rows)
                radial = radial * inverse_peak
                place = functools.partial(block_at, scaled_ref, c, g)
                place(0, 0, SS_SIGMA * radial)
                sp = SP_SIGMA * radial
                pp = PP_SUM * radial
                pi = PP_PI * radial
                for a in range(3):
                    wave = cosine[a] * sp
                    place(0, a + 1, wave)
                    place(a + 1, 0, -wave)
                    leaning = cosine[a] * pp
                    for b in range(a, 3):
                        value = leaning * cosine[b]
                        if a == b:
                            place(a + 1, a + 1, value + pi)
                        else:
                            place(a + 1, b + 1, value)
                            place(b + 1, a + 1, value)
            one = jnp.dot(scaled_ref[c], operand_ref[c], preferred_element_type=F32)
            one_ref[c] = one
            half_ref[pair, :, 64 * side : 64 * side + 64] = one.astype(BF16)

    for pair in range(4):
        one_pair(pair)


def block_at(scaled_ref, c, g, a, b, value):
    low = 512 * g + 128 * b
    scaled_ref[c, 32 * a : 32 * a + 32, low : low + 128] = value.astype(BF16)


def second_kernel(
    slot_ref, near_ref, row_ref, scaled_ref, operand_ref, probe_ref, one_ref,
    before_ref, own_ref, after_ref, table_ref, send_ref,
    half_ref, gathered_ref, near_pull_ref, own_pull_ref, shift_ref,
):
    fill_shifts(shift_ref)
    lane = lanes()
    for part, ref in enumerate((before_ref, own_ref, after_ref)):
        for pair in range(4):
            half_ref[8 * part + pair] = ref[pair, :, 0:64]
            half_ref[8 * part + pair + 4] = ref[pair, :, 64:128]
    half_ref[DEAD] = jnp.zeros((128, 64), BF16)
    on_row = lax.broadcasted_iota(jnp.int32, (32, 128), 0) == lax.broadcasted_iota(
        jnp.int32, (32, 128), 1
    )

    def one_pair(pair):
        for side in range(2):
            c = pair + 4 * side
            gather_operand(slot_ref, half_ref, gathered_ref.at[side], c)
            two = jnp.dot(scaled_ref[c], gathered_ref[side], preferred_element_type=F32)
            probe = probe_ref[8 + c].astype(F32)
            term_two = 2.0 * two - probe
            mixture = COEFF_ZERO * probe + COEFF_ONE * one_ref[c] + COEFF_TWO * term_two
            mixture = mixture.astype(BF16)
            wide = mixture.astype(F32)
            for q in range(8):
                send_ref[
                    q, 16 * pair : 16 * pair + 16, 64 * side : 64 * side + 64
                ] = wide[16 * q : 16 * q + 16, :]
            rows = [row_ref[c, x] for x in range(3)]
            own = [jnp.zeros((32, 128), F32) for _ in range(3)]
            for g in range(4):
                sample = lax.dot_general(
                    mixture,
                    operand_ref[c, 512 * g : 512 * g + 512, :],
                    (((1,), (1,)), ((), ())),
                    preferred_element_type=F32,
                )
                columns = four_slots(near_ref, slot_ref, shift_ref, c, g, lane)
                pulls = pair_pulls(sample, columns, rows)
                for x in range(3):
                    own[x] = own[x] + pulls[x]
                    near_pull_ref[x, 4 * c + g : 4 * c + g + 1, :] = jnp.sum(
                        pulls[x], axis=0, keepdims=True
                    )
            for x in range(3):
                whole = jnp.broadcast_to(jnp.sum(own[x], axis=1, keepdims=True), (32, 128))
                own_pull_ref[x, c : c + 1, :] = jnp.sum(
                    jnp.where(on_row, whole, 0.0), axis=0, keepdims=True
                )

    for pair in range(4):
        one_pair(pair)

    stacked = jnp.concatenate(
        [
            jnp.concatenate(
                [jnp.where(lane // 32 == t, near_pull_ref[x], 0.0) for x in range(3)], axis=1
            )
            for t in range(4)
        ],
        axis=0,
    )
    gathered = jnp.dot(
        table_ref[...], stacked, precision=lax.Precision.HIGHEST, preferred_element_type=F32
    )
    total = [-gathered[:, 128 * x : 128 * x + 128] for x in range(3)]
    nothing = jnp.zeros((8, 128), F32)
    for x in range(3):
        v = total[x] + jnp.concatenate([nothing, own_pull_ref[x], nothing], axis=0)
        v = v + pltpu.roll(v, 64, 1)
        v = v + pltpu.roll(v, 32, 1)
        total[x] = v * (1.0 / 512.0)
    joined = jnp.where(lane < 32, total[0], jnp.where(lane < 64, total[1], total[2]))
    for q in range(8):
        send_ref[q, 64:88, :] = joined


def pair_pulls(sample, columns, rows):
    part = lambda a, b: sample[32 * a : 32 * a + 32, 128 * b : 128 * b + 128]
    d, cosine, radial, inverse = bond(columns, rows)
    mixed = [SP_SIGMA * (part(0, 1 + x) - part(1 + x, 0)) for x in range(3)]
    double = [2.0 * PP_SUM * part(1 + x, 1 + x) for x in range(3)]
    cross = {}
    for a, b in ((0, 1), (0, 2), (1, 2)):
        cross[a, b] = cross[b, a] = PP_SUM * (part(1 + a, 1 + b) + part(1 + b, 1 + a))
    bent = []
    for a in range(3):
        b, c = [x for x in range(3) if x != a]
        bent.append(double[a] * cosine[a] + cross[a, b] * cosine[b] + cross[a, c] * cosine[c])
    still = SS_SIGMA * part(0, 0) + PP_PI * (part(1, 1) + part(2, 2) + part(3, 3))
    straight = mixed[0] * cosine[0] + mixed[1] * cosine[1] + mixed[2] * cosine[2]
    curved = bent[0] * cosine[0] + bent[1] * cosine[1] + bent[2] * cosine[2]
    value = still + straight + 0.5 * curved
    across = radial * inverse
    inward = radial * value * (-2.0 / BOND_SQUARE) - across * inverse * (straight + curved)
    return [across * (mixed[x] + bent[x]) + inward * d[x] for x in range(3)]


def sample_kernel(
    slot_ref, rank_ref, core_ref, received_ref, *refs
):
    pieces, swapped = refs[0:4], refs[4:8]
    density_ref, left_ref, sample_ref, turn_ref = refs[8:]
    rank, core = rank_ref[0], core_ref[0]
    for distance in range(4):
        source = (rank - 2 * distance + 8) % 8
        for e in range(2):
            q = source if e == 0 else source + 1 - 2 * (source % 2)
            low = 64 * (2 * distance + e)
            block = received_ref[q, 0:64, :].astype(BF16)
            left_ref[0:64, low : low + 64] = block[:, 0:64]
            left_ref[64:128, low : low + 64] = block[:, 64:128]
    left = left_ref[...]
    scale = 1.0 / math.sqrt(512.0)
    sides = ((pieces, 0, 16 * core), (pieces, 1, 8), (swapped, 1, 16 - 16 * core))
    for source_refs, index, base in sides:
        for pair in range(4):
            c = 2 * pair
            right = jnp.concatenate(
                [
                    jnp.concatenate(
                        [
                            ref[e, index, 64 * n : 64 * n + 64, :]
                            for ref in source_refs
                            for e in range(2)
                        ],
                        axis=0,
                    )
                    for n in (c, c + 1)
                ],
                axis=1,
            )
            product = jnp.dot(left, right, preferred_element_type=F32) * scale
            sample_ref[base + c] = product[:, 0:128]
            sample_ref[base + c + 1] = product[:, 128:256]
    sample_ref[DEAD] = jnp.zeros((128, 128), F32)
    for c in range(8):
        for k in range(15):
            turn_ref[pl.ds(8 * k + c, 16, stride=120), :] = sample_ref[
                slot_ref[c, k], 16 * c : 16 * c + 16, :
            ]
    for r in range(16):
        density_ref[r] = turn_ref[120 * r : 120 * r + 120].astype(BF16).reshape(15, 8, 128)


def around(block, size, distance):
    return lax.ppermute(block, "space", [((i - distance) % size, i) for i in range(size)])


def along_probe(block, target):
    return lax.ppermute(block, "probe", [(i, target(i)) for i in range(8)])


def per_device(positions, probes, neighbours):
    space_count = lax.axis_size("space")
    space_rank = lax.axis_index("space")
    both = lambda block: (around(block, space_count, 1), around(block, space_count, -1))

    coords = jnp.pad(positions.transpose(1, 0, 2), ((0, 0), (0, 0), (0, 96)))
    own = jnp.concatenate([probes.reshape(64, 8, 128), coords]).reshape(536, 128)
    before, after = both(own)
    core = space_rank % 2
    present = neighbours >= 0
    slot = (neighbours // 8 - space_rank + 1) % space_count * 8 + neighbours % 8
    slot = jnp.pad(jnp.where(present, slot, DEAD), ((0, 0), (0, 1)), constant_values=DEAD)

    before, after, slot = lax.optimization_barrier((before, after, slot))
    near, rows, peak, pair = pl.pallas_call(
        spectral_kernel,
        out_shape=(
            jax.ShapeDtypeStruct((NEAR + 1, 8, 128), F32),
            jax.ShapeDtypeStruct((8, 3, 32, 128), F32),
            jax.ShapeDtypeStruct((space_count, 128), F32),
            jax.ShapeDtypeStruct((2, 512, 128), BF16),
        ),
        in_specs=[SMEM, SMEM] + [WHOLE] * 3,
        out_specs=(WHOLE,) * 4,
        scratch_shapes=[pltpu.VMEM((4, 8, 128), F32), pltpu.SemaphoreType.DMA((2,))],
        cost_estimate=HEAVY,
        compiler_params=params(4),
        name="spectral",
    )(slot, core.reshape(1), before, own, after)
    across = along_probe(pair, lambda i: i ^ 1)
    peak, held = lax.optimization_barrier((peak, (before, own, after)))
    peaks = lax.all_to_all(peak, "space", 0, 0, tiled=True)
    probe_turned, table = pl.pallas_call(
        prepare_kernel,
        out_shape=(
            jax.ShapeDtypeStruct((NEAR + 1, 128, 64), BF16),
            jax.ShapeDtypeStruct((NEAR, 128), F32),
        ),
        in_specs=[SMEM] + [WHOLE] * 3,
        out_specs=(WHOLE,) * 2,
        scratch_shapes=[pltpu.VMEM((128, 128), F32)],
        compiler_params=params(4),
        name="prepare",
    )(slot, *held)
    peaks, quad, probe_turned = lax.optimization_barrier(
        (peaks, jnp.stack([pair, across]), probe_turned)
    )
    pieces = [quad] + [
        along_probe(quad, lambda i, distance=distance: (i + 2 * distance) % 8)
        for distance in range(1, 4)
    ]

    scaled, operand, one, half = pl.pallas_call(
        first_kernel,
        out_shape=(
            jax.ShapeDtypeStruct((8, 128, 2048), BF16),
            jax.ShapeDtypeStruct((8, 2048, 64), BF16),
            jax.ShapeDtypeStruct((8, 128, 64), F32),
            jax.ShapeDtypeStruct((4, 128, 128), BF16),
        ),
        in_specs=[SMEM] + [WHOLE] * 4,
        out_specs=(WHOLE,) * 4,
        scratch_shapes=[pltpu.VMEM((4, 8, 128), F32)],
        cost_estimate=LIGHT,
        compiler_params=params(16),
        name="first",
    )(slot, peaks, near, rows, probe_turned)
    half_before, half_after = both(half)

    send = pl.pallas_call(
        second_kernel,
        out_shape=jax.ShapeDtypeStruct((8, 88, 128), F32),
        in_specs=[SMEM] + [WHOLE] * 10,
        out_specs=WHOLE,
        cost_estimate=LIGHT,
        scratch_shapes=[
            pltpu.VMEM((NEAR + 1, 128, 64), BF16),
            pltpu.VMEM((2, 2048, 64), BF16),
            pltpu.VMEM((3, 32, 128), F32),
            pltpu.VMEM((3, 8, 128), F32),
            pltpu.VMEM((4, 8, 128), F32),
        ],
        compiler_params=params(16),
        name="second",
    )(slot, near, rows, scaled, operand, probe_turned, one, half_before, half, half_after, table)
    send, pieces = lax.optimization_barrier((send, pieces))
    swapped = [
        lax.ppermute(piece, "space", [(i, i ^ 1) for i in range(space_count)]) for piece in pieces
    ]
    received = lax.all_to_all(send, "probe", 0, 0, tiled=True)
    force = jnp.sum(received[:, 64:88], axis=0)
    from_after = around(force[0:8], space_count, -1)
    from_before = around(force[16:24], space_count, 1)

    density = pl.pallas_call(
        sample_kernel,
        out_shape=jax.ShapeDtypeStruct((16, 15, 8, 128), BF16),
        in_specs=[SMEM] * 3 + [WHOLE] * 9,
        out_specs=WHOLE,
        scratch_shapes=[
            pltpu.VMEM((128, 512), BF16),
            pltpu.VMEM((NEAR + 1, 128, 128), F32),
            pltpu.VMEM((16 * 120, 128), F32),
        ],
        compiler_params=params(16),
        name="sample",
    )(
        slot, lax.axis_index("probe").reshape(1), core.reshape(1), received, *pieces, *swapped
    )
    forces = force[8:16] + from_after + from_before
    forces = jnp.stack([forces[:, 32 * x : 32 * x + 32] for x in range(3)])
    return density.transpose(0, 2, 1, 3), forces.transpose(1, 0, 2)


def solution(mesh):
    in_specs = (P("space", None, None), P("space", "probe", None), P("space", None))
    out_specs = (P("probe", "space", None, None), P("space", None, None))
    return jax.shard_map(
        per_device, mesh=mesh, in_specs=in_specs, out_specs=out_specs, check_vma=False
    )
```

```python
import functools
import math

import jax
import jax.numpy as jnp
import numpy as np
from jax import lax
from jax.experimental import pallas as pl
from jax.experimental.pallas import tpu as pltpu
from jax.sharding import PartitionSpec as P

SS_SIGMA = -1.938
SP_SIGMA = 1.745
PP_SIGMA = 3.05
PP_PI = -1.075
BOND_LENGTH = 2.35
SOFT_SQUARE = 0.25
CELL_EDGE = 10.86
COEFF_ZERO = 0.6
COEFF_ONE = -0.7
COEFF_TWO = 0.45

PP_SUM = PP_SIGMA - PP_PI
BOND_SQUARE = BOND_LENGTH * BOND_LENGTH
NEAR = 24
DEAD = 24
FAR = 1000.0
SLOTS = 16
F32 = jnp.float32
BF16 = jnp.bfloat16
WHOLE = pl.BlockSpec()
SMEM = pl.BlockSpec(memory_space=pltpu.SMEM)
HEAVY = pl.CostEstimate(flops=0, transcendentals=0, bytes_accessed=60_000_000)
LIGHT = pl.CostEstimate(flops=0, transcendentals=0, bytes_accessed=0)


def params(mebibytes):
    return pltpu.CompilerParams(vmem_limit_bytes=mebibytes * 1024 * 1024)


def slot_offsets():
    half = CELL_EDGE / 2.0
    table = [[0.0, 0.0, 0.0]]
    for sign_x in (-1.0, 1.0):
        for sign_y in (-1.0, 1.0):
            for sign_z in (-1.0, 1.0):
                table.append([sign_x * half, sign_y * half, sign_z * half])
    for axis_pick in range(3):
        for sign_a in (1.0, -1.0):
            entry = [0.0, 0.0, 0.0]
            entry[axis_pick] = sign_a * CELL_EDGE
            table.append(entry)
    table.append([0.0, 0.0, 0.0])
    return np.array(table, dtype=np.float32)


def fill_shifts(shift_ref):
    lane = lanes()
    table = slot_offsets()
    for g in range(4):
        for x in range(3):
            v = [float(table[4 * g + t, x]) for t in range(4)]
            shift_ref[g, x : x + 1, :] = jnp.where(
                lane < 32, v[0], jnp.where(lane < 64, v[1], jnp.where(lane < 96, v[2], v[3]))
            )


def lanes():
    return lax.broadcasted_iota(jnp.int32, (1, 128), 1)


def bond(columns, rows):
    d = [columns[x : x + 1, :] - rows[x] for x in range(3)]
    rho_square = d[0] * d[0] + d[1] * d[1] + d[2] * d[2] + SOFT_SQUARE
    inverse = lax.rsqrt(rho_square)
    radial = jnp.exp(1.0 - rho_square / BOND_SQUARE)
    return d, [v * inverse for v in d], radial, inverse


def four_slots(near_ref, slot_ref, shift_ref, c, g, lane):
    v = [near_ref[slot_ref[c, 4 * g + t]] for t in range(4)]
    joined = jnp.where(
        lane < 32, v[0], jnp.where(lane < 64, v[1], jnp.where(lane < 96, v[2], v[3]))
    )
    return joined + shift_ref[g]


def spectral_kernel(
    slot_ref, core_ref, before_ref, own_ref, after_ref, near_ref, row_ref, peak_ref, pair_ref,
    shift_ref, sem,
):
    kept = pltpu.make_async_copy(own_ref.at[0:512], pair_ref.at[1], sem.at[1])
    kept.start()

    @pl.when(core_ref[0] == 0)
    def _():
        pltpu.make_async_copy(before_ref.at[0:512], pair_ref.at[0], sem.at[0]).start()

    @pl.when(core_ref[0] != 0)
    def _():
        pltpu.make_async_copy(after_ref.at[0:512], pair_ref.at[0], sem.at[0]).start()

    fill_shifts(shift_ref)
    for part, ref in enumerate((before_ref, own_ref, after_ref)):
        for x in range(3):
            coords = ref[512 + 8 * x : 520 + 8 * x, 0:32].astype(F32)
            wide = jnp.concatenate([coords] * 4, axis=1)
            for n in range(8):
                near_ref[8 * part + n, x : x + 1, :] = wide[n : n + 1, :]
            if part == 1:
                upright = wide.T
                for c in range(8):
                    row_ref[c, x] = jnp.broadcast_to(upright[0:32, c : c + 1], (32, 128))
    near_ref[DEAD] = jnp.full((8, 128), FAR, F32)
    lane = lanes()

    def one_cluster(c, peak):
        rows = [row_ref[c, x] for x in range(3)]
        sums = [jnp.zeros((32, 128), F32) for _ in range(4)]
        for g in range(4):
            columns = four_slots(near_ref, slot_ref, shift_ref, c, g, lane)
            _, cosine, radial, _ = bond(columns, rows)
            size = [jnp.abs(v) for v in cosine]
            sums[0] += (-SS_SIGMA + SP_SIGMA * (size[0] + size[1] + size[2])) * radial
            cross = {}
            for a in range(3):
                for b in range(a, 3):
                    product = cosine[a] * cosine[b] * PP_SUM
                    cross[a, b] = cross[b, a] = jnp.abs(product + PP_PI if a == b else product)
            for a in range(3):
                sums[1 + a] += (
                    SP_SIGMA * size[a] + cross[a, 0] + cross[a, 1] + cross[a, 2]
                ) * radial
        for v in sums:
            peak = jnp.maximum(peak, jnp.sum(v, axis=1, keepdims=True))
        return peak

    peak = jnp.zeros((32, 1), F32)
    for c in range(8):
        peak = one_cluster(c, peak)
    peak_ref[...] = jnp.broadcast_to(jnp.max(peak), peak_ref.shape)
    kept.wait()
    pltpu.make_async_copy(before_ref.at[0:512], pair_ref.at[0], sem.at[0]).wait()


def gather_operand(slot_ref, source_ref, target_ref, c):
    for k in range(SLOTS):
        n = slot_ref[c, k]
        for b in range(4):
            low = 512 * (k // 4) + 128 * b + 32 * (k % 4)
            target_ref[low : low + 32, :] = source_ref[n, 32 * b : 32 * b + 32, :]


def prepare_kernel(
    slot_ref, before_ref, own_ref, after_ref, probe_ref, table_ref,
    hot_ref,
):
    lane = lanes()
    for t in range(4):
        for c in range(8):
            for g in range(4):
                row = 32 * t + 4 * c + g
                hot_ref[row : row + 1, :] = (lane == slot_ref[c, 4 * g + t]).astype(F32)
    table_ref[...] = hot_ref[...].T[0:NEAR, :]
    probe_ref[DEAD] = jnp.zeros((128, 64), BF16)
    for part, ref in enumerate((before_ref, own_ref, after_ref)):
        for c in range(8):
            turned = ref[64 * c : 64 * c + 64].astype(F32).T
            probe_ref[8 * part + c] = turned.astype(BF16)


def first_kernel(
    slot_ref, peak_ref, near_ref, row_ref, probe_ref,
    scaled_ref, operand_ref, one_ref, half_ref, shift_ref,
):
    fill_shifts(shift_ref)
    lane = lanes()
    inverse_peak = 1.0 / jnp.max(peak_ref[...])

    def one_pair(pair):
        for side in range(2):
            c = pair + 4 * side
            rows = [row_ref[c, x] for x in range(3)]
            gather_operand(slot_ref, probe_ref, operand_ref.at[c], c)
            for g in range(4):
                columns = four_slots(near_ref, slot_ref, shift_ref, c, g, lane)
                _, cosine, radial, _ = bond(columns, rows)
                radial = radial * inverse_peak
                place = functools.partial(block_at, scaled_ref, c, g)
                place(0, 0, SS_SIGMA * radial)
                sp = SP_SIGMA * radial
                pp = PP_SUM * radial
                pi = PP_PI * radial
                for a in range(3):
                    wave = cosine[a] * sp
                    place(0, a + 1, wave)
                    place(a + 1, 0, -wave)
                    leaning = cosine[a] * pp
                    for b in range(a, 3):
                        value = leaning * cosine[b]
                        if a == b:
                            place(a + 1, a + 1, value + pi)
                        else:
                            place(a + 1, b + 1, value)
                            place(b + 1, a + 1, value)
            one = jnp.dot(scaled_ref[c], operand_ref[c], preferred_element_type=F32)
            one_ref[c] = one
            half_ref[pair, :, 64 * side : 64 * side + 64] = one.astype(BF16)

    for pair in range(4):
        one_pair(pair)


def block_at(scaled_ref, c, g, a, b, value):
    low = 512 * g + 128 * b
    scaled_ref[c, 32 * a : 32 * a + 32, low : low + 128] = value.astype(BF16)


def second_kernel(
    slot_ref, near_ref, row_ref, scaled_ref, operand_ref, probe_ref, one_ref,
    before_ref, own_ref, after_ref, table_ref, send_ref,
    half_ref, gathered_ref, near_pull_ref, own_pull_ref, shift_ref,
):
    fill_shifts(shift_ref)
    lane = lanes()
    for part, ref in enumerate((before_ref, own_ref, after_ref)):
        for pair in range(4):
            half_ref[8 * part + pair] = ref[pair, :, 0:64]
            half_ref[8 * part + pair + 4] = ref[pair, :, 64:128]
    half_ref[DEAD] = jnp.zeros((128, 64), BF16)
    on_row = lax.broadcasted_iota(jnp.int32, (32, 128), 0) == lax.broadcasted_iota(
        jnp.int32, (32, 128), 1
    )

    def one_pair(pair):
        for side in range(2):
            c = pair + 4 * side
            gather_operand(slot_ref, half_ref, gathered_ref.at[side], c)
            two = jnp.dot(scaled_ref[c], gathered_ref[side], preferred_element_type=F32)
            probe = probe_ref[8 + c].astype(F32)
            term_two = 2.0 * two - probe
            mixture = COEFF_ZERO * probe + COEFF_ONE * one_ref[c] + COEFF_TWO * term_two
            mixture = mixture.astype(BF16)
            wide = mixture.astype(F32)
            for q in range(8):
                send_ref[
                    q, 16 * pair : 16 * pair + 16, 64 * side : 64 * side + 64
                ] = wide[16 * q : 16 * q + 16, :]
            rows = [row_ref[c, x] for x in range(3)]
            own = [jnp.zeros((32, 128), F32) for _ in range(3)]
            for g in range(4):
                sample = lax.dot_general(
                    mixture,
                    operand_ref[c, 512 * g : 512 * g + 512, :],
                    (((1,), (1,)), ((), ())),
                    preferred_element_type=F32,
                )
                columns = four_slots(near_ref, slot_ref, shift_ref, c, g, lane)
                pulls = pair_pulls(sample, columns, rows)
                for x in range(3):
                    own[x] = own[x] + pulls[x]
                    near_pull_ref[x, 4 * c + g : 4 * c + g + 1, :] = jnp.sum(
                        pulls[x], axis=0, keepdims=True
                    )
            for x in range(3):
                whole = jnp.broadcast_to(jnp.sum(own[x], axis=1, keepdims=True), (32, 128))
                own_pull_ref[x, c : c + 1, :] = jnp.sum(
                    jnp.where(on_row, whole, 0.0), axis=0, keepdims=True
                )

    for pair in range(4):
        one_pair(pair)

    stacked = jnp.concatenate(
        [
            jnp.concatenate(
                [jnp.where(lane // 32 == t, near_pull_ref[x], 0.0) for x in range(3)], axis=1
            )
            for t in range(4)
        ],
        axis=0,
    )
    gathered = jnp.dot(
        table_ref[...], stacked, precision=lax.Precision.HIGHEST, preferred_element_type=F32
    )
    total = [-gathered[:, 128 * x : 128 * x + 128] for x in range(3)]
    nothing = jnp.zeros((8, 128), F32)
    for x in range(3):
        v = total[x] + jnp.concatenate([nothing, own_pull_ref[x], nothing], axis=0)
        v = v + pltpu.roll(v, 64, 1)
        v = v + pltpu.roll(v, 32, 1)
        total[x] = v * (1.0 / 512.0)
    joined = jnp.where(lane < 32, total[0], jnp.where(lane < 64, total[1], total[2]))
    for q in range(8):
        send_ref[q, 64:88, :] = joined


def pair_pulls(sample, columns, rows):
    part = lambda a, b: sample[32 * a : 32 * a + 32, 128 * b : 128 * b + 128]
    d, cosine, radial, inverse = bond(columns, rows)
    mixed = [SP_SIGMA * (part(0, 1 + x) - part(1 + x, 0)) for x in range(3)]
    double = [2.0 * PP_SUM * part(1 + x, 1 + x) for x in range(3)]
    cross = {}
    for a, b in ((0, 1), (0, 2), (1, 2)):
        cross[a, b] = cross[b, a] = PP_SUM * (part(1 + a, 1 + b) + part(1 + b, 1 + a))
    bent = []
    for a in range(3):
        b, c = [x for x in range(3) if x != a]
        bent.append(double[a] * cosine[a] + cross[a, b] * cosine[b] + cross[a, c] * cosine[c])
    still = SS_SIGMA * part(0, 0) + PP_PI * (part(1, 1) + part(2, 2) + part(3, 3))
    straight = mixed[0] * cosine[0] + mixed[1] * cosine[1] + mixed[2] * cosine[2]
    curved = bent[0] * cosine[0] + bent[1] * cosine[1] + bent[2] * cosine[2]
    value = still + straight + 0.5 * curved
    across = radial * inverse
    inward = radial * value * (-2.0 / BOND_SQUARE) - across * inverse * (straight + curved)
    return [across * (mixed[x] + bent[x]) + inward * d[x] for x in range(3)]


def both_halves(refs):
    own, first, second, third, last = refs
    return [own.at[0], own.at[1], first.at[0], first.at[1], second, third, last.at[0], last.at[1]]


def sample_kernel(
    slot_ref, rank_ref, core_ref, received_ref, *refs
):
    pieces, swapped = both_halves(refs[0:5]), both_halves(refs[5:10])
    density_ref, left_ref, sample_ref, turn_ref = refs[10:]
    rank, core = rank_ref[0], core_ref[0]
    for distance in range(4):
        source = (rank - 2 * distance + 8) % 8
        for e in range(2):
            q = source if e == 0 else source + 1 - 2 * (source % 2)
            low = 64 * (2 * distance + e)
            block = received_ref[q, 0:64, :].astype(BF16)
            left_ref[0:64, low : low + 64] = block[:, 0:64]
            left_ref[64:128, low : low + 64] = block[:, 64:128]
    left = left_ref[...]
    scale = 1.0 / math.sqrt(512.0)
    sides = ((pieces, 0, 16 * core), (pieces, 1, 8), (swapped, 1, 16 - 16 * core))
    for source_refs, index, base in sides:
        for pair in range(4):
            c = 2 * pair
            right = jnp.concatenate(
                [
                    jnp.concatenate(
                        [
                            ref[index, 64 * n : 64 * n + 64, :] for ref in source_refs
                        ],
                        axis=0,
                    )
                    for n in (c, c + 1)
                ],
                axis=1,
            )
            product = jnp.dot(left, right, preferred_element_type=F32) * scale
            sample_ref[base + c] = product[:, 0:128]
            sample_ref[base + c + 1] = product[:, 128:256]
    sample_ref[DEAD] = jnp.zeros((128, 128), F32)
    for c in range(8):
        for k in range(15):
            turn_ref[pl.ds(8 * k + c, 16, stride=120), :] = sample_ref[
                slot_ref[c, k], 16 * c : 16 * c + 16, :
            ]
    for r in range(16):
        density_ref[r] = turn_ref[120 * r : 120 * r + 120].astype(BF16).reshape(15, 8, 128)


def around(block, size, distance):
    return lax.ppermute(block, "space", [((i - distance) % size, i) for i in range(size)])


def along_probe(block, target):
    return lax.ppermute(block, "probe", [(i, target(i)) for i in range(8)])


def per_device(positions, probes, neighbours):
    space_count = lax.axis_size("space")
    space_rank = lax.axis_index("space")
    both = lambda block: (around(block, space_count, 1), around(block, space_count, -1))

    coords = jnp.pad(positions.transpose(1, 0, 2), ((0, 0), (0, 0), (0, 96)))
    own = jnp.concatenate([probes.reshape(64, 8, 128), coords]).reshape(536, 128)
    before, after = both(own)
    core = space_rank % 2
    present = neighbours >= 0
    slot = (neighbours // 8 - space_rank + 1) % space_count * 8 + neighbours % 8
    slot = jnp.pad(jnp.where(present, slot, DEAD), ((0, 0), (0, 1)), constant_values=DEAD)

    before, after, slot = lax.optimization_barrier((before, after, slot))
    near, rows, peak, pair = pl.pallas_call(
        spectral_kernel,
        out_shape=(
            jax.ShapeDtypeStruct((NEAR + 1, 8, 128), F32),
            jax.ShapeDtypeStruct((8, 3, 32, 128), F32),
            jax.ShapeDtypeStruct((space_count, 128), F32),
            jax.ShapeDtypeStruct((2, 512, 128), BF16),
        ),
        in_specs=[SMEM, SMEM] + [WHOLE] * 3,
        out_specs=(WHOLE,) * 4,
        scratch_shapes=[pltpu.VMEM((4, 8, 128), F32), pltpu.SemaphoreType.DMA((2,))],
        cost_estimate=HEAVY,
        compiler_params=params(4),
        name="spectral",
    )(slot, core.reshape(1), before, own, after)
    across = along_probe(pair, lambda i: i ^ 1)
    peak, held = lax.optimization_barrier((peak, (before, own, after)))
    peaks = lax.all_to_all(peak, "space", 0, 0, tiled=True)
    probe_turned, table = pl.pallas_call(
        prepare_kernel,
        out_shape=(
            jax.ShapeDtypeStruct((NEAR + 1, 128, 64), BF16),
            jax.ShapeDtypeStruct((NEAR, 128), F32),
        ),
        in_specs=[SMEM] + [WHOLE] * 3,
        out_specs=(WHOLE,) * 2,
        scratch_shapes=[pltpu.VMEM((128, 128), F32)],
        compiler_params=params(4),
        name="prepare",
    )(slot, *held)
    peaks, quad, probe_turned = lax.optimization_barrier(
        (peaks, jnp.stack([pair, across]), probe_turned)
    )
    ahead, behind = lambda i: (i + 2) % 8, lambda i: (i + 6) % 8
    one_back, one_on = along_probe(quad, ahead), along_probe(quad, behind)

    scaled, operand, one, half = pl.pallas_call(
        first_kernel,
        out_shape=(
            jax.ShapeDtypeStruct((8, 128, 2048), BF16),
            jax.ShapeDtypeStruct((8, 2048, 64), BF16),
            jax.ShapeDtypeStruct((8, 128, 64), F32),
            jax.ShapeDtypeStruct((4, 128, 128), BF16),
        ),
        in_specs=[SMEM] + [WHOLE] * 4,
        out_specs=(WHOLE,) * 4,
        scratch_shapes=[pltpu.VMEM((4, 8, 128), F32)],
        cost_estimate=LIGHT,
        compiler_params=params(16),
        name="first",
    )(slot, peaks, near, rows, probe_turned)
    half_before, half_after = both(half)
    half_before, half_after, one_back, one_on = lax.optimization_barrier(
        (half_before, half_after, one_back, one_on)
    )
    pieces = [
        quad,
        one_back,
        along_probe(one_back[0], ahead),
        along_probe(one_on[1], behind),
        one_on,
    ]

    send = pl.pallas_call(
        second_kernel,
        out_shape=jax.ShapeDtypeStruct((8, 88, 128), F32),
        in_specs=[SMEM] + [WHOLE] * 10,
        out_specs=WHOLE,
        cost_estimate=LIGHT,
        scratch_shapes=[
            pltpu.VMEM((NEAR + 1, 128, 64), BF16),
            pltpu.VMEM((2, 2048, 64), BF16),
            pltpu.VMEM((3, 32, 128), F32),
            pltpu.VMEM((3, 8, 128), F32),
            pltpu.VMEM((4, 8, 128), F32),
        ],
        compiler_params=params(16),
        name="second",
    )(slot, near, rows, scaled, operand, probe_turned, one, half_before, half, half_after, table)
    send, pieces = lax.optimization_barrier((send, pieces))
    swapped = [
        lax.ppermute(piece, "space", [(i, i ^ 1) for i in range(space_count)]) for piece in pieces
    ]
    received = lax.all_to_all(send, "probe", 0, 0, tiled=True)
    force = jnp.sum(received[:, 64:88], axis=0)
    from_after = around(force[0:8], space_count, -1)
    from_before = around(force[16:24], space_count, 1)

    density = pl.pallas_call(
        sample_kernel,
        out_shape=jax.ShapeDtypeStruct((16, 15, 8, 128), BF16),
        in_specs=[SMEM] * 3 + [WHOLE] * 11,
        out_specs=WHOLE,
        scratch_shapes=[
            pltpu.VMEM((128, 512), BF16),
            pltpu.VMEM((NEAR + 1, 128, 128), F32),
            pltpu.VMEM((16 * 120, 128), F32),
        ],
        compiler_params=params(16),
        name="sample",
    )(
        slot, lax.axis_index("probe").reshape(1), core.reshape(1), received, *pieces, *swapped
    )
    forces = force[8:16] + from_after + from_before
    forces = jnp.stack([forces[:, 32 * x : 32 * x + 32] for x in range(3)])
    return density.transpose(0, 2, 1, 3), forces.transpose(1, 0, 2)


def solution(mesh):
    in_specs = (P("space", None, None), P("space", "probe", None), P("space", None))
    out_specs = (P("probe", "space", None, None), P("space", None, None))
    return jax.shard_map(
        per_device, mesh=mesh, in_specs=in_specs, out_specs=out_specs, check_vma=False
    )
```
